32 devices in a mesh: rep: 8 (over y, x, core), tp: 4 (over z).
Axes of the slice: x: 2, y: 2, z: 4, core: 2. Of those that a mesh axis runs over, the one named last changes fastest.
Arguments:
- tokens_in: bfloat16 [16384, 8192], P('rep', 'tp'), may hold values from -6 to 6
- cotangent: bfloat16 [16384, 1024], P('rep', 'tp'), may hold values from -0.046875 to 0.046875
- master: float32 [4, 2048, 1024], P('tp', 'rep'), may hold values from -0.0625 to 0.0625
- moment_one: float32 [4, 2048, 1024], P('tp', 'rep'), may hold values from -4 to 4
- moment_two: float32 [4, 2048, 1024], P('tp', 'rep'), may hold values from 0.01 to 1
- inputs_one: bfloat16 [512, 8192], P('rep', 'tp'), may hold values from -6 to 6
- inputs_two: bfloat16 [512, 8192], P('rep', 'tp'), may hold values from -6 to 6
- queries_one: bfloat16 [512, 4096], P(('rep', 'tp')), may hold values from -128 to 128
- queries_two: bfloat16 [512, 4096], P(('rep', 'tp')), may hold values from -128 to 128
- cache_keys: bfloat16 [512, 128, 512], P(('rep', 'tp')), may hold values from -4 to 4
- cache_values: bfloat16 [512, 128, 512], P(('rep', 'tp')), may hold values from -6 to 6
- lengths: int32 [512], P(('rep', 'tp')), may hold values from 16 to 128
Outputs:
- master_new: float32 [4, 2048, 1024], P('tp', 'rep')
- moment_one_new: float32 [4, 2048, 1024], P('tp', 'rep')
- moment_two_new: float32 [4, 2048, 1024], P('tp', 'rep')
- projected_one: float32 [512, 1024], P(('rep', 'tp'))
- projected_two: float32 [512, 1024], P(('rep', 'tp'))
- attended_one: float32 [512, 4096], P(('rep', 'tp'))
- attended_two: float32 [512, 4096], P(('rep', 'tp'))
The draws below stay inside these ranges and needn't reach their ends.
Inputs may be any that keep to these rules, and one draw needn't show every extreme that they name: The new key of step one takes position lengths and that of step two lengths + 1.
All inputs are finite; a program needn't handle non-finite values.
Results may differ from the reference program's by a relative error of at most 0.0029.
Values may be sent and summed in bfloat16 or wider, within the bound.
A program may use at most 64 MiB of HBM per device.

```python
import math
import jax
import jax.numpy as jnp
from jax import lax

D = 8192
KVH = 4
QH = 32
HD = 128
DEC = 64
CTX = 128
KVW = 1024
TOKENS = 16384
ROWS = 512
N_REP = 8
N_TP = 4


def shared_keys(key):
    base_key = jax.random.fold_in(key, 7)
    cache_rows = jnp.clip(jax.random.normal(base_key, (ROWS, CTX, KVH * HD), jnp.float32), -4.0, 4.0)
    return cache_rows


def drawn_queries(key, offset_salt):
    random_part = jnp.clip(jax.random.normal(jax.random.fold_in(key, offset_salt), (ROWS, QH * HD), jnp.float32), -4.0, 4.0)
    return random_part


def draw_cache_keys(key, part):
    return shared_keys(key).astype(jnp.bfloat16)


def draw_queries_one(key, part):
    return drawn_queries(key, 101).astype(jnp.bfloat16)


def draw_queries_two(key, part):
    return drawn_queries(key, 203).astype(jnp.bfloat16)


def set_ends(values, own_key, smallest, high):
    longest = values.shape.index(max(values.shape))
    spots = []
    for shift in (0, 1):
        where = [jax.random.randint(jax.random.fold_in(own_key, axis), (), 0, length) for axis, length in enumerate(values.shape)]
        where[longest] = (where[longest] + shift) % values.shape[longest]
        spots.append(tuple(where))
    return values.at[spots[0]].set(smallest).at[spots[1]].set(high)


def with_spikes(array, own_key, source, target, parts, factor):
    def block_of(axis_at):
        return (jnp.arange(array.shape[axis_at]) // (array.shape[axis_at] // parts)).reshape((-1,) + (1,) * (array.ndim - 1 - axis_at))

    one_side = jax.random.permutation(own_key, parts)[block_of(target)]
    second = (block_of(target) + parts // 2) % parts
    return jnp.where((block_of(source) == one_side) | (block_of(source) == second), factor * array, array)


def levels(stream_key, dims, cuts, low, high):
    def one(position, blocks):
        heights = jax.random.uniform(jax.random.fold_in(jax.random.fold_in(stream_key, 6), position), (blocks,), jnp.float32, low / len(cuts), high / len(cuts))
        return jnp.repeat(jnp.exp(heights), dims[position] // blocks).reshape((-1,) + (1,) * (len(dims) - position - 1))

    factor_of = one(*cuts[0])
    for cut in cuts[1:]:
        factor_of = factor_of * one(*cut)
    return factor_of


def bell_draw(rng, shape, width, most, cuts=(), kind=jnp.bfloat16):
    entries = jax.random.normal(rng, shape, jnp.float32) * width
    if len(cuts) > 0:
        entries = levels(rng, shape, cuts, -0.22, 0.18) * entries
    return jnp.clip(entries, min=-most, max=most).astype(kind)


def gaussian_with(own_key, extent, spread, reach, split, heavy, kind=jnp.bfloat16):
    drawn = spread * jax.random.normal(own_key, extent, jnp.float32)
    if split:
        drawn = drawn * levels(own_key, extent, split, -0.22, 0.18)
    return jnp.clip(with_spikes(drawn, jax.random.fold_in(own_key, 3), *heavy), -reach, reach).astype(kind)


def setup_inputs(seed: int = 0) -> dict:
    key_list = jax.random.split(jax.random.key(seed), 13)
    tokens_in = gaussian_with(key_list[0], (TOKENS, D), 1.0, 6.0, ((0, 8), (1, 4)), (0, 1, 8, 2.0))
    cotangent = bell_draw(key_list[1], (TOKENS, KVW), TOKENS ** -0.5, 0.046875, ((0, 8), (1, 4)))
    master = bell_draw(key_list[2], (N_TP, D // N_TP, KVW), D ** -0.5, 0.0625, ((0, 4), (1, 8)), jnp.float32)
    moment_one = bell_draw(key_list[3], (N_TP, D // N_TP, KVW), 0.3, 4.0, ((0, 4), (1, 8)), jnp.float32)
    moment_two = jnp.clip(jnp.exp(math.log(1.0) - 4.6051702 * jax.random.uniform(key_list[4], (N_TP, D // N_TP, KVW), jnp.float32) ** levels(key_list[4], (N_TP, D // N_TP, KVW), ((0, 4), (1, 8)), -0.2, 0.2)), 0.01, 1.0)
    inputs_one = bell_draw(key_list[5], (ROWS, D), 1.0, 6.0, ((0, 8), (1, 4)))
    inputs_two = bell_draw(key_list[6], (ROWS, D), 1.0, 6.0, ((0, 8), (1, 4)))
    queries_one = draw_queries_one(jax.random.fold_in(key_list[12], 71), 0)
    queries_two = draw_queries_two(jax.random.fold_in(key_list[12], 71), 0)
    cache_keys = draw_cache_keys(jax.random.fold_in(key_list[12], 71), 0)
    cache_values = bell_draw(key_list[10], (ROWS, CTX, KVH * HD), 1.0, 6.0, ((0, 32),))
    lengths = set_ends(jax.random.randint(key_list[11], (ROWS,), CTX // 8, CTX + 1), jax.random.fold_in(key_list[11], 1), CTX // 8, CTX).astype(jnp.int32)
    return dict(tokens_in=tokens_in, cotangent=cotangent, master=master, moment_one=moment_one, moment_two=moment_two, inputs_one=inputs_one, inputs_two=inputs_two, queries_one=queries_one, queries_two=queries_two, cache_keys=cache_keys, cache_values=cache_values, lengths=lengths)


learning_rate = 0.001
beta_one = 0.9
beta_two = 0.99
epsilon = 1e-08
weight_decay = 0.1
step_count = 10.0
rope_base = 500000.0

def rotate(vectors, positions):
    row_count = vectors.shape[0]
    half_size = HD // 2
    inverse = rope_base ** (-2.0 * jnp.arange(half_size).astype(jnp.float32) / HD)
    angles = positions.astype(jnp.float32)[:, None, None] * inverse[None, None, :]
    shaped = vectors.reshape(row_count, -1, HD)
    first_half = shaped[..., :half_size]
    second_half = shaped[..., half_size:]
    cosine = jnp.cos(angles)
    sine = jnp.sin(angles)
    turned = jnp.concatenate([first_half * cosine - second_half * sine, second_half * cosine + first_half * sine], axis=-1)
    return turned.reshape(row_count, -1)

def partial_scores(queries, all_keys, all_values, allowed):
    row_count = all_keys.shape[0]
    places = all_keys.shape[1]
    group_size = QH // KVH
    shaped_queries = queries.astype(jnp.float32).reshape(row_count, KVH, group_size, HD)
    shaped_keys = all_keys.astype(jnp.float32).reshape(row_count, places, KVH, HD)
    shaped_values = all_values.astype(jnp.float32).reshape(row_count, places, KVH, HD)
    scores = jnp.einsum('rkgd,rpkd->rkgp', shaped_queries, shaped_keys) / HD ** 0.5
    scores = jnp.where(allowed[:, None, None, :], scores, -1e+30)
    highest = lax.optimization_barrier(jnp.max(scores, axis=-1))
    weights = lax.optimization_barrier(jnp.exp(scores - highest[..., None]).astype(jnp.bfloat16)).astype(jnp.float32)
    return (highest, lax.optimization_barrier(jnp.sum(weights, axis=-1)), jnp.einsum('rkgp,rpkd->rkgd', weights, shaped_values))

def finish(highest, denominator, numerator):
    row_count = numerator.shape[0]
    return (numerator / denominator[..., None]).reshape(row_count, -1)

def block_attend(items):
    return finish(*partial_scores(items[0], items[1], items[2], items[3]))

def attend_blocks(queries, all_keys, all_values, allowed):
    items = (queries.reshape((N_REP, DEC) + queries.shape[1:]), all_keys.reshape((N_REP, DEC) + all_keys.shape[1:]), all_values.reshape((N_REP, DEC) + all_values.shape[1:]), allowed.reshape((N_REP, DEC) + allowed.shape[1:]))
    result = lax.map(block_attend, items)
    return result.reshape(ROWS, QH * HD)

def reference(tokens_in, cotangent, master, moment_one, moment_two, inputs_one, inputs_two, queries_one, queries_two, cache_keys, cache_values, lengths):
    gradient = lax.dot_general(tokens_in, cotangent, (((0,), (0,)), ((), ())), preferred_element_type=jnp.float32)
    gradient = gradient.reshape(master.shape)
    moment_one_new = beta_one * moment_one + (1.0 - beta_one) * gradient
    moment_two_new = beta_two * moment_two + (1.0 - beta_two) * gradient * gradient
    corrected_one = moment_one_new / (1.0 - beta_one ** step_count)
    corrected_two = moment_two_new / (1.0 - beta_two ** step_count)
    master_new = master - learning_rate * (corrected_one / (jnp.sqrt(corrected_two) + epsilon) + weight_decay * master)
    rollout_weights = master_new.reshape(D, KVW).astype(jnp.bfloat16)
    key_width = KVH * HD
    projected_one = jnp.dot(inputs_one, rollout_weights, preferred_element_type=jnp.float32)
    projected_two = jnp.dot(inputs_two, rollout_weights, preferred_element_type=jnp.float32)
    keys_one = rotate(projected_one[:, :key_width], lengths).astype(jnp.bfloat16)
    values_one = projected_one[:, key_width:].astype(jnp.bfloat16)
    keys_two = rotate(projected_two[:, :key_width], lengths + 1).astype(jnp.bfloat16)
    values_two = projected_two[:, key_width:].astype(jnp.bfloat16)
    places = jnp.arange(CTX, dtype=jnp.int32)
    cache_allowed = places[None, :] < lengths[:, None]
    fresh = jnp.zeros((ROWS, 1), jnp.int32) == 0
    keys_first = jnp.concatenate([cache_keys, keys_one[:, None]], axis=1)
    values_first = jnp.concatenate([cache_values, values_one[:, None]], axis=1)
    allowed_first = jnp.concatenate([cache_allowed, fresh], axis=1)
    attended_one = attend_blocks(queries_one, keys_first, values_first, allowed_first)
    keys_second = jnp.concatenate([keys_first, keys_two[:, None]], axis=1)
    values_second = jnp.concatenate([values_first, values_two[:, None]], axis=1)
    allowed_second = jnp.concatenate([allowed_first, fresh], axis=1)
    attended_two = attend_blocks(queries_two, keys_second, values_second, allowed_second)
    return (master_new, moment_one_new, moment_two_new, projected_one, projected_two, attended_one, attended_two)
```

```python
import functools

import jax
import jax.numpy as jnp
from jax import lax
from jax.experimental import pallas as pl
from jax.experimental.pallas import tpu as pltpu
from jax.sharding import PartitionSpec as P

KVH = 4
QH = 32
HD = 128


learning_rate = 0.001
beta_one = 0.9
beta_two = 0.99
epsilon = 1e-08
weight_decay = 0.1
step_count = 10.0
rope_base = 500000.0


def rotate(vectors, positions):
    row_count = vectors.shape[0]
    half_size = HD // 2
    inverse = rope_base ** (-2.0 * jnp.arange(half_size).astype(jnp.float32) / HD)
    angles = positions.astype(jnp.float32)[:, None, None] * inverse[None, None, :]
    shaped = vectors.reshape(row_count, -1, HD)
    first_half = shaped[..., :half_size]
    second_half = shaped[..., half_size:]
    cosine = jnp.cos(angles)
    sine = jnp.sin(angles)
    turned = jnp.concatenate(
        [first_half * cosine - second_half * sine, second_half * cosine + first_half * sine],
        axis=-1,
    )
    return turned.reshape(row_count, -1)


def partial_scores(queries, all_keys, all_values, allowed):
    row_count = all_keys.shape[0]
    places = all_keys.shape[1]
    group_size = QH // KVH
    shaped_queries = queries.astype(jnp.float32).reshape(row_count, KVH, group_size, HD)
    shaped_keys = all_keys.astype(jnp.float32).reshape(row_count, places, KVH, HD)
    shaped_values = all_values.astype(jnp.float32).reshape(row_count, places, KVH, HD)
    scores = jnp.einsum("rkgd,rpkd->rkgp", shaped_queries, shaped_keys) / HD**0.5
    scores = jnp.where(allowed[:, None, None, :], scores, -1e30)
    highest = jnp.max(scores, axis=-1)
    weights = lax.optimization_barrier(
        jnp.exp(scores - highest[..., None]).astype(jnp.bfloat16)
    ).astype(jnp.float32)
    return (
        highest,
        jnp.sum(weights, axis=-1),
        jnp.einsum("rkgp,rpkd->rkgd", weights, shaped_values),
    )


def finish(highest, denominator, numerator):
    row_count = numerator.shape[0]
    return (numerator / denominator[..., None]).reshape(row_count, -1)


def combine(earlier, later):
    highest = jnp.maximum(earlier[0], later[0])
    scale_early = jnp.exp(earlier[0] - highest)
    scale_late = jnp.exp(later[0] - highest)
    denominator = earlier[1] * scale_early + later[1] * scale_late
    numerator = earlier[2] * scale_early[..., None] + later[2] * scale_late[..., None]
    return (highest, denominator, numerator)


MESH = pl.DeviceIdType.MESH
SUB = 128


def arrival_orders(n_tp, sub):
    orders = []
    for t in range(n_tp):
        near = 0 if 2 * t < n_tp else n_tp - 1
        inner = t not in (0, n_tp - 1)
        pieces = []
        for b in range(n_tp):
            away = abs(b - t)
            rank = away
            if inner and away:
                rank = 2 * away + (0 if (b > t) == (near == 0) else 1) - 1
            pieces += [(rank, u, b) for u in range(sub)]
        pieces.sort()
        orders.append([b * sub + u for _, u, b in pieces])
    return orders


def piece_at(orders, t, s):
    found = 0
    for place, order in enumerate(orders):
        for step, piece in enumerate(order):
            found = found + jnp.where(jnp.logical_and(t == place, s == step), piece, 0)
    return found


def sync_kernel(
    n_rep,
    n_tp,
    sub,
    tok_hbm,
    cot_hbm,
    master_hbm,
    m1_hbm,
    m2_hbm,
    keys_hbm,
    values_hbm,
    in1_hbm,
    in2_hbm,
    q1_hbm,
    q2_hbm,
    lengths_hbm,
    master_out,
    m1_out,
    m2_out,
    p1_out,
    p2_out,
    early_max,
    early_sum,
    early_mix,
    table_ref,
    queries,
    state,
    keys,
    values,
    inputs,
    lengths_ref,
    mask,
    q_ref,
    state_sem,
    cache_sem,
    row_sem,
    tok,
    cot,
    cot_t,
    a_send,
    a_keep,
    a_recv,
    b_send,
    b_recv,
    w_buf,
    part,
    part_recv,
    tok_sem,
    cot_sem,
    z_send_sem,
    z_recv_sem,
    a_sems,
    b_ss,
    b_rs,
    w_ss,
    w_rs,
    v_ss,
    v_rs,
    p_ss,
    p_rs,
):
    nc = n_rep // 2
    steps = n_tp * sub
    cw = SUB
    r = lax.axis_index("rep")
    t = lax.axis_index("tp")
    k = r // 2
    c = r % 2
    sibling = (2 * k + 1 - c, t)
    own_rows = master_hbm.shape[0]
    att_rows, groups, stacked, _ = q_ref.shape
    master_ref, m1_ref, m2_ref = state.at[0], state.at[1], state.at[2]
    load_state = [
        pltpu.make_async_copy(source, state.at[i], state_sem.at[i])
        for i, source in enumerate((master_hbm, m1_hbm, m2_hbm))
    ]
    load_cache = [
        pltpu.make_async_copy(keys_hbm, keys, cache_sem.at[0]),
        pltpu.make_async_copy(values_hbm, values, cache_sem.at[1]),
    ]
    load_rows = [
        pltpu.make_async_copy(q1_hbm, queries.at[0], row_sem.at[0]),
        pltpu.make_async_copy(q2_hbm, queries.at[1], row_sem.at[1]),
        pltpu.make_async_copy(lengths_hbm, lengths_ref, row_sem.at[2]),
    ]
    load_inputs = [
        pltpu.make_async_copy(in1_hbm, inputs.at[0], row_sem.at[3]),
        pltpu.make_async_copy(in2_hbm, inputs.at[1], row_sem.at[4]),
    ]
    orders = arrival_orders(n_tp, sub)

    def chip(j):
        return (k + j) % nc

    def source_chip(j):
        return (k + nc - j) % nc

    load_tok = pltpu.make_async_copy(tok_hbm, tok, tok_sem)
    load_cots = [
        pltpu.make_async_copy(
            cot_hbm.at[:, u * cw : (u + 1) * cw], cot.at[t * sub + u], cot_sem.at[u]
        )
        for u in range(sub)
    ]
    for load in load_cots:
        load.start()
    load_tok.start()
    for load in load_rows + load_cache + load_state + load_inputs:
        load.start()

    barrier = pltpu.get_barrier_semaphore()
    pl.semaphore_signal(barrier, inc=1, device_id=sibling, device_id_type=MESH)
    for j in range(1, nc):
        pl.semaphore_signal(barrier, inc=1, device_id=(2 * chip(j) + c, t), device_id_type=MESH)
    for j in range(1, n_tp):
        pl.semaphore_signal(barrier, inc=1, device_id=(r, (t + j) % n_tp), device_id_type=MESH)
    pl.semaphore_wait(barrier, 1 + (nc - 1) + (n_tp - 1))

    half_tokens = tok_hbm.shape[0] // 2

    def z_copy(g, side, half):
        rows = pl.ds(half * half_tokens, half_tokens)
        target = jnp.minimum(t + 1, n_tp - 1) if side == 0 else jnp.maximum(t - 1, 0)
        return pltpu.make_async_remote_copy(
            cot.at[g, rows], cot.at[g, rows], z_send_sem.at[side, half, g], z_recv_sem.at[half, g],
            device_id=(r, target), device_id_type=MESH,
        )

    def z_goes(g, side):
        b = g // sub
        if side == 0:
            return jnp.logical_and(b <= t, t < n_tp - 1)
        return jnp.logical_and(b >= t, t > 0)

    def z_forward(g, half):
        for side in (0, 1):
            @pl.when(z_goes(g, side))
            def _():
                z_copy(g, side, half).start()

    for u, load in enumerate(load_cots):
        load.wait()
        for half in (0, 1):
            z_forward(t * sub + u, half)
    for load in load_rows:
        load.wait()
    row_ids = lax.broadcasted_iota(jnp.int32, (att_rows, HD), 0)
    length = jnp.zeros((att_rows, HD), jnp.int32)
    for row in range(att_rows):
        length = jnp.where(row_ids == row, lengths_ref[row], length)
    table_ref[...] = decode_table(length[:, 0:1])
    for i in range(2):
        for h in range(groups):
            for place in range(stacked // 2):
                at = (h * (stacked // 2) + place) * HD
                q_ref[:, h, i * (stacked // 2) + place, :] = queries[i, :, at : at + HD].astype(
                    jnp.float32
                )
    mask[...] = table_ref[:, 0:HD]
    load_tok.wait()
    for load in load_cache + load_state + load_inputs:
        load.wait()

    def a_copy(s):
        return pltpu.make_async_remote_copy(
            a_send.at[s], a_recv.at[s], a_sems.at[0, s], a_sems.at[1, s],
            device_id=sibling, device_id_type=MESH,
        )

    def b_copy(s, j):
        return pltpu.make_async_remote_copy(
            b_send.at[s, j - 1], b_recv.at[s, j - 1], b_ss.at[s, j - 1], b_rs.at[s, j - 1],
            device_id=(2 * chip(j) + c, t), device_id_type=MESH,
        )

    def w_copy(s, j):
        return pltpu.make_async_remote_copy(
            w_buf.at[s, r], w_buf.at[s, r], w_ss.at[s, j - 1], w_rs.at[s, j - 1],
            device_id=(2 * chip(j) + c, t), device_id_type=MESH,
        )

    def v_copy(s, j):
        row = 2 * source_chip(j) + c
        return pltpu.make_async_remote_copy(
            w_buf.at[s, row], w_buf.at[s, row], v_ss.at[s, j], v_rs.at[s, j],
            device_id=sibling, device_id_type=MESH,
        )

    def gradient_stage(s):
        g = piece_at(orders, t, s)

        def arrive(half):
            @pl.when(g // sub != t)
            def _():
                z_copy(g, 0, half).wait_recv()
                z_forward(g, half)

            rows = slice(half * half_tokens, (half + 1) * half_tokens)
            cot_t[...] = cot[g, rows].T

        def term(owner, half):
            at = pl.multiple_of(owner * own_rows, own_rows)
            rows = slice(half * half_tokens, (half + 1) * half_tokens)
            return jnp.dot(
                cot_t[...], tok[rows, pl.ds(at, own_rows)], preferred_element_type=jnp.float32
            )

        arrive(0)
        for q in range(nc):
            a_send[s, q] = term(2 * q + 1 - c, 0)
        for q in range(nc):
            a_keep[s, q] = term(2 * q + c, 0)
        arrive(1)
        for q in range(nc):
            a_send[s, q] = a_send[s, q] + term(2 * q + 1 - c, 1)
        a_copy(s).start()
        for q in range(nc):
            a_keep[s, q] = a_keep[s, q] + term(2 * q + c, 1)

    def chip_sum_stage(s):
        a_copy(s).wait_recv()
        for j in range(1, nc):
            q = chip(j)
            b_send[s, j - 1] = (a_keep[s, q] + a_recv[s, q]).astype(jnp.bfloat16)
            b_copy(s, j).start()

    def update_stage(s):
        total = a_keep[s, k] + a_recv[s, k]
        for j in range(1, nc):
            b_copy(s, j).wait_recv()
            total = total + b_recv[s, j - 1].astype(jnp.float32)
        gradient = total.T
        cols = pl.ds(pl.multiple_of(piece_at(orders, t, s) * cw, cw), cw)
        master = master_ref[:, cols]
        moment_one_new = beta_one * m1_ref[:, cols] + (1.0 - beta_one) * gradient
        moment_two_new = beta_two * m2_ref[:, cols] + (1.0 - beta_two) * gradient * gradient
        corrected_one = moment_one_new / (1.0 - beta_one**step_count)
        corrected_two = moment_two_new / (1.0 - beta_two**step_count)
        master_new = master - learning_rate * (
            corrected_one / (jnp.sqrt(corrected_two) + epsilon) + weight_decay * master
        )
        w_buf[s, r] = master_new.astype(jnp.bfloat16)
        for j in range(1, nc):
            w_copy(s, j).start()
        v_copy(s, 0).start()
        master_out[:, cols] = master_new
        m1_out[:, cols] = moment_one_new
        m2_out[:, cols] = moment_two_new

    def share_stage(s):
        for j in range(1, nc):
            w_copy(s, j).wait_recv()
            v_copy(s, j).start()

    at_end = jnp.logical_or(t == 0, t == n_tp - 1)

    def to_end(j):
        to = (t + j) % n_tp
        return jnp.logical_or(to == 0, to == n_tp - 1)

    def p_copy(g, j):
        to = (t + j) % n_tp
        return pltpu.make_async_remote_copy(
            part.at[g, to], part_recv.at[j - 1, g], p_ss.at[j - 1, g], p_rs.at[j - 1, g],
            device_id=(r, to), device_id_type=MESH,
        )

    def decode_stage(s):
        for j in range(nc):
            v_copy(s, j).wait_recv()
        g = piece_at(orders, t, s)
        block = w_buf[s].reshape(n_rep * own_rows, cw)
        for i in range(2):
            product = jnp.dot(inputs[i], block, preferred_element_type=jnp.float32)
            part[g, :, i] = product.reshape(n_tp, product.shape[0] // n_tp, cw)

        last = jnp.logical_and(at_end, s >= steps - 4)
        for j in range(1, n_tp):
            @pl.when(jnp.logical_or(last, jnp.logical_not(to_end(j))))
            def _():
                p_copy(g, j).start()

    def late_stage(s):
        g = piece_at(orders, t, s)
        for j in range(1, n_tp):
            @pl.when(to_end(j))
            def _():
                p_copy(g, j).start()

    def cache_stage(s):
        per_step = att_rows // steps
        for i in range(per_step):
            row = s * per_step + i
            allowed = mask[pl.ds(row, 1), :] > 0.0
            for h in range(groups):
                head = slice(h * HD, (h + 1) * HD)
                scores = lax.dot_general(
                    q_ref[row, h].astype(jnp.bfloat16),
                    keys[row, :, head],
                    (((1,), (1,)), ((), ())),
                    preferred_element_type=jnp.float32,
                )
                scores = jnp.where(allowed, scores / HD**0.5, -1e30)
                highest = jnp.max(scores, axis=-1, keepdims=True)
                weights = jnp.exp(scores - highest).astype(jnp.bfloat16)
                total = jnp.sum(weights.astype(jnp.float32), axis=-1, keepdims=True)
                mix = jnp.dot(weights, values[row, :, head], preferred_element_type=jnp.float32)
                for ref, value in ((early_max, highest), (early_sum, total), (early_mix, mix)):
                    value = jnp.broadcast_to(value, (stacked, HD))
                    ref[h, :, pl.ds(row, 1), :] = value.reshape(stacked, 1, HD)

    stages = (
        (chip_sum_stage, 1),
        (update_stage, 2),
        (share_stage, 3),
        (decode_stage, 4),
        (cache_stage, 0),
        (gradient_stage, 0),
    )

    @pl.loop(0, steps + 4)
    def _(it):
        @pl.when(jnp.logical_and(at_end, it == steps))
        def _():
            @pl.loop(0, steps - 4)
            def _(s):
                late_stage(s)

        for stage, lag in stages:
            @pl.when(jnp.logical_and(it >= lag, it < steps + lag))
            def _():
                stage(it - lag)

    @pl.loop(0, steps)
    def _(s):
        for side in (0, 1):
            @pl.when(z_goes(s, side))
            def _():
                z_copy(s, side, 0).wait_send()
                z_copy(s, side, 1).wait_send()

    @pl.when(jnp.logical_not(at_end))
    def _():
        @pl.loop(0, steps)
        def _(s):
            late_stage(s)

    @pl.loop(0, steps)
    def _(s):
        a_copy(s).wait_send()
        for j in range(1, nc):
            b_copy(s, j).wait_send()
            w_copy(s, j).wait_send()
        for j in range(nc):
            v_copy(s, j).wait_send()

    for g in range(steps):
        for j in range(1, n_tp):
            p_copy(g, j).wait_recv()
        for i, out in enumerate((p1_out, p2_out)):
            total = part[g, t, i]
            for j in range(1, n_tp):
                total = total + part_recv[j - 1, g, i]
            out[:, g * cw : (g + 1) * cw] = total
    @pl.loop(0, steps)
    def _(g):
        for j in range(1, n_tp):
            p_copy(g, j).wait_send()


def finish_kernel(
    master,
    m1,
    m2,
    p1,
    p2,
    early_max,
    early_sum,
    early_mix,
    table,
    queries,
    master_out,
    m1_out,
    m2_out,
    p1_out,
    p2_out,
    att1_out,
    att2_out,
    att,
    sems,
    att_sems,
):
    stores = [
        pltpu.make_async_copy(source, target, sems.at[i])
        for i, (source, target) in enumerate(
            ((master, master_out), (m1, m1_out), (m2, m2_out), (p1, p1_out), (p2, p2_out))
        )
    ]
    for store in stores:
        store.start()
    groups, stacked = early_max.shape[:2]
    half = stacked // 2
    keys, values = [], []
    for i, ref in enumerate((p1, p2)):
        total = ref[...]
        cosine = table[:, (1 + 2 * i) * HD : (2 + 2 * i) * HD]
        sine = table[:, (2 + 2 * i) * HD : (3 + 2 * i) * HD]
        for h in range(groups):
            head = total[:, h * HD : (h + 1) * HD]
            turned = head * cosine + pltpu.roll(head, HD // 2, 1) * sine
            value = total[:, (groups + h) * HD : (groups + h + 1) * HD]
            keys.append(turned.astype(jnp.bfloat16).astype(jnp.float32))
            values.append(value.astype(jnp.bfloat16).astype(jnp.float32))
    for i, out in enumerate((att1_out, att2_out)):
        for h in range(groups):
            for place in range(half):
                at = slice((h * half + place) * HD, (h * half + place + 1) * HD)
                query = queries[i, :, at].astype(jnp.float32)
                scores = [
                    jnp.sum(query * keys[n * groups + h], axis=-1, keepdims=True) / HD**0.5
                    for n in range(i + 1)
                ]
                before = early_max[h, i * half + place]
                highest = before
                for score in scores:
                    highest = jnp.maximum(highest, score)
                scale = jnp.exp(before - highest)
                below = early_sum[h, i * half + place] * scale
                above = early_mix[h, i * half + place] * scale
                for n, score in enumerate(scores):
                    weight = jnp.exp(score - highest).astype(jnp.bfloat16).astype(jnp.float32)
                    below = below + weight
                    above = above + weight * values[n * groups + h]
                att[i, :, at] = above / below
        store = pltpu.make_async_copy(att.at[i], out, att_sems.at[i])
        store.start()
        stores.append(store)
    for store in stores:
        store.wait()


def synchronise(
    n_rep,
    n_tp,
    tokens_in,
    cotangent,
    master,
    m1,
    m2,
    cache_keys,
    cache_values,
    inputs_one,
    inputs_two,
    queries_one,
    queries_two,
    lengths,
):
    tokens, width = tokens_in.shape
    sub = cotangent.shape[1] // SUB
    steps = n_tp * sub
    nc = n_rep // 2
    rows, cols = master.shape
    decode = inputs_one.shape[0]
    share = decode // n_tp
    f32, bf16 = jnp.float32, jnp.bfloat16
    count = queries_one.shape[0]
    stacked = (count, KVH, 2 * QH // KVH, HD)
    early = (KVH, 2 * QH // KVH, count, HD)
    vmem = pl.BlockSpec(memory_space=pltpu.VMEM)
    hbm = pl.BlockSpec(memory_space=pl.ANY)
    dma = pltpu.SemaphoreType.DMA
    held = pl.pallas_call(
        functools.partial(sync_kernel, n_rep, n_tp, sub),
        out_shape=[pltpu.VMEM((rows, cols), f32)] * 3
        + [pltpu.VMEM((share, cols), f32)] * 2
        + [pltpu.VMEM(early, f32)] * 3
        + [pltpu.VMEM((count, 5 * HD), f32), pltpu.VMEM((2, *queries_one.shape), bf16)],
        in_specs=[hbm] * 12,
        out_specs=[vmem] * 10,
        scratch_shapes=[
            pltpu.VMEM((3, rows, cols), f32),
            pltpu.VMEM(cache_keys.shape, bf16),
            pltpu.VMEM(cache_values.shape, bf16),
            pltpu.VMEM((2, *inputs_one.shape), bf16),
            pltpu.SMEM(lengths.shape, jnp.int32),
            pltpu.VMEM((count, HD), f32),
            pltpu.VMEM(stacked, f32),
            dma((3,)),
            dma((2,)),
            dma((5,)),
            pltpu.VMEM((tokens, width), bf16),
            pltpu.VMEM((steps, tokens, SUB), bf16),
            pltpu.VMEM((SUB, tokens // 2), bf16),
            pltpu.VMEM((steps, nc, SUB, rows), f32),
            pltpu.VMEM((steps, nc, SUB, rows), f32),
            pltpu.VMEM((steps, nc, SUB, rows), f32),
            pltpu.VMEM((steps, nc - 1, SUB, rows), bf16),
            pltpu.VMEM((steps, nc - 1, SUB, rows), bf16),
            pltpu.VMEM((steps, n_rep, rows, SUB), bf16),
            pltpu.VMEM((steps, n_tp, 2, share, SUB), f32),
            pltpu.VMEM((n_tp - 1, steps, 2, share, SUB), f32),
            dma(()),
            dma((sub,)),
            dma((2, 2, steps)),
            dma((2, steps)),
            dma((2, steps)),
            dma((steps, nc - 1)),
            dma((steps, nc - 1)),
            dma((steps, nc - 1)),
            dma((steps, nc - 1)),
            dma((steps, nc)),
            dma((steps, nc)),
            dma((n_tp - 1, steps)),
            dma((n_tp - 1, steps)),
        ],
        compiler_params=pltpu.CompilerParams(
            collective_id=0, has_side_effects=True, vmem_limit_bytes=52 * 2**20
        ),
        name="synchronise",
    )(
        tokens_in,
        cotangent,
        master,
        m1,
        m2,
        cache_keys,
        cache_values,
        inputs_one,
        inputs_two,
        queries_one,
        queries_two,
        lengths,
    )
    wide = queries_one.shape
    return pl.pallas_call(
        finish_kernel,
        out_shape=[jax.ShapeDtypeStruct((rows, cols), f32)] * 3
        + [jax.ShapeDtypeStruct((share, cols), f32)] * 2
        + [jax.ShapeDtypeStruct(wide, f32)] * 2,
        in_specs=[vmem] * 10,
        out_specs=[hbm] * 7,
        scratch_shapes=[pltpu.VMEM((2, *wide), f32), dma((5,)), dma((2,))],
        compiler_params=pltpu.CompilerParams(vmem_limit_bytes=4 * 2**20),
        name="finish",
    )(*held)


def decode_table(lengths):
    shape = (lengths.shape[0], 5 * HD)
    column = lax.broadcasted_iota(jnp.int32, shape, 1)
    kind = column // HD
    lane = column % HD
    half_size = HD // 2
    inverse = rope_base ** (-2.0 * (lane % half_size).astype(jnp.float32) / HD)
    position = lengths + jnp.where(kind >= 3, 1, 0)
    angles = position.astype(jnp.float32) * inverse
    sine = jnp.where(lane < half_size, -jnp.sin(angles), jnp.sin(angles))
    allowed = jnp.where(lane < lengths, 1.0, 0.0)
    return jnp.where(kind == 0, allowed, jnp.where(kind % 2 == 1, jnp.cos(angles), sine))


def fits_kernel(n_rep, n_tp, cotangent, master, inputs_one, cache_keys):
    steps = n_tp * (cotangent.shape[1] // SUB)
    return (
        cache_keys.shape[1] == HD
        and steps > 0
        and cache_keys.shape[0] % max(steps, 1) == 0
        and n_rep % 2 == 0
        and n_rep >= 4
        and n_tp >= 2
        and cotangent.shape[1] % SUB == 0
        and cotangent.shape[0] % 256 == 0
        and master.shape[1] % 128 == 0
        and inputs_one.shape[0] % (8 * n_tp) == 0
    )


def shards(
    n_rep,
    n_tp,
    tokens_in,
    cotangent,
    master,
    moment_one,
    moment_two,
    inputs_one,
    inputs_two,
    queries_one,
    queries_two,
    cache_keys,
    cache_values,
    lengths,
):
    row_count = cache_keys.shape[0]
    if fits_kernel(n_rep, n_tp, cotangent, master[0], inputs_one, cache_keys):
        *updated, both_one, both_two, attended_one, attended_two = synchronise(
            n_rep,
            n_tp,
            tokens_in,
            cotangent,
            master[0],
            moment_one[0],
            moment_two[0],
            cache_keys,
            cache_values,
            inputs_one,
            inputs_two,
            queries_one,
            queries_two,
            lengths,
        )
        return (
            *(array[None] for array in updated),
            both_one,
            both_two,
            attended_one,
            attended_two,
        )
    places = jnp.arange(cache_keys.shape[1], dtype=jnp.int32)
    cache_allowed = places[None, :] < lengths[:, None]
    fresh = jnp.zeros((row_count, 1), jnp.int32) == 0
    early_one = partial_scores(queries_one, cache_keys, cache_values, cache_allowed)
    early_two = partial_scores(queries_two, cache_keys, cache_values, cache_allowed)
    columns = lax.all_gather(cotangent, "tp", axis=1, tiled=True)
    gradient = lax.psum_scatter(
        lax.dot_general(
            tokens_in, columns, (((0,), (0,)), ((), ())), preferred_element_type=jnp.float32
        ),
        "rep",
        scatter_dimension=0,
        tiled=True,
    ).reshape(master.shape)
    moment_one_new = beta_one * moment_one + (1.0 - beta_one) * gradient
    moment_two_new = beta_two * moment_two + (1.0 - beta_two) * gradient * gradient
    corrected_one = moment_one_new / (1.0 - beta_one**step_count)
    corrected_two = moment_two_new / (1.0 - beta_two**step_count)
    master_new = master - learning_rate * (
        corrected_one / (jnp.sqrt(corrected_two) + epsilon) + weight_decay * master
    )
    weights = master_new[0].astype(jnp.bfloat16)
    shard_rows = lax.all_gather(weights, "rep", axis=0, tiled=True)
    partial_one = jnp.dot(inputs_one, shard_rows, preferred_element_type=jnp.float32)
    partial_two = jnp.dot(inputs_two, shard_rows, preferred_element_type=jnp.float32)
    both_one, both_two = (
        lax.psum_scatter(partial_one, "tp", scatter_dimension=0, tiled=True),
        lax.psum_scatter(partial_two, "tp", scatter_dimension=0, tiled=True),
    )
    key_width = both_one.shape[1] // 2
    keys_one = rotate(both_one[:, :key_width], lengths).astype(jnp.bfloat16)
    values_one = both_one[:, key_width:].astype(jnp.bfloat16)
    keys_two = rotate(both_two[:, :key_width], lengths + 1).astype(jnp.bfloat16)
    values_two = both_two[:, key_width:].astype(jnp.bfloat16)
    late_one = partial_scores(queries_one, keys_one[:, None], values_one[:, None], fresh)
    attended_one = finish(*combine(early_one, late_one))
    fresh_pair = jnp.concatenate([fresh, fresh], axis=1)
    late_two = partial_scores(
        queries_two,
        jnp.stack([keys_one, keys_two], axis=1),
        jnp.stack([values_one, values_two], axis=1),
        fresh_pair,
    )
    attended_two = finish(*combine(early_two, late_two))
    return (
        master_new,
        moment_one_new,
        moment_two_new,
        both_one,
        both_two,
        attended_one,
        attended_two,
    )


def solution(mesh):
    return jax.shard_map(
        functools.partial(shards, mesh.shape["rep"], mesh.shape["tp"]),
        mesh=mesh,
        in_specs=(
            P("rep", "tp"),
            P("rep", "tp"),
            P("tp", "rep", None),
            P("tp", "rep", None),
            P("tp", "rep", None),
            P("rep", "tp"),
            P("rep", "tp"),
            P(("rep", "tp"), None),
            P(("rep", "tp"), None),
            P(("rep", "tp"), None, None),
            P(("rep", "tp"), None, None),
            P(("rep", "tp")),
        ),
        out_specs=(
            P("tp", "rep", None),
            P("tp", "rep", None),
            P("tp", "rep", None),
            P(("rep", "tp"), None),
            P(("rep", "tp"), None),
            P(("rep", "tp"), None),
            P(("rep", "tp"), None),
        ),
        check_vma=False,
    )
```

```python
import functools

import jax
import jax.numpy as jnp
from jax import lax
from jax.experimental import pallas as pl
from jax.experimental.pallas import tpu as pltpu
from jax.sharding import PartitionSpec as P

KVH = 4
QH = 32
HD = 128


learning_rate = 0.001
beta_one = 0.9
beta_two = 0.99
epsilon = 1e-08
weight_decay = 0.1
step_count = 10.0
rope_base = 500000.0


def rotate(vectors, positions):
    row_count = vectors.shape[0]
    half_size = HD // 2
    inverse = rope_base ** (-2.0 * jnp.arange(half_size).astype(jnp.float32) / HD)
    angles = positions.astype(jnp.float32)[:, None, None] * inverse[None, None, :]
    shaped = vectors.reshape(row_count, -1, HD)
    first_half = shaped[..., :half_size]
    second_half = shaped[..., half_size:]
    cosine = jnp.cos(angles)
    sine = jnp.sin(angles)
    turned = jnp.concatenate(
        [first_half * cosine - second_half * sine, second_half * cosine + first_half * sine],
        axis=-1,
    )
    return turned.reshape(row_count, -1)


def partial_scores(queries, all_keys, all_values, allowed):
    row_count = all_keys.shape[0]
    places = all_keys.shape[1]
    group_size = QH // KVH
    shaped_queries = queries.astype(jnp.float32).reshape(row_count, KVH, group_size, HD)
    shaped_keys = all_keys.astype(jnp.float32).reshape(row_count, places, KVH, HD)
    shaped_values = all_values.astype(jnp.float32).reshape(row_count, places, KVH, HD)
    scores = jnp.einsum("rkgd,rpkd->rkgp", shaped_queries, shaped_keys) / HD**0.5
    scores = jnp.where(allowed[:, None, None, :], scores, -1e30)
    highest = jnp.max(scores, axis=-1)
    weights = lax.optimization_barrier(
        jnp.exp(scores - highest[..., None]).astype(jnp.bfloat16)
    ).astype(jnp.float32)
    return (
        highest,
        jnp.sum(weights, axis=-1),
        jnp.einsum("rkgp,rpkd->rkgd", weights, shaped_values),
    )


def finish(highest, denominator, numerator):
    row_count = numerator.shape[0]
    return (numerator / denominator[..., None]).reshape(row_count, -1)


def combine(earlier, later):
    highest = jnp.maximum(earlier[0], later[0])
    scale_early = jnp.exp(earlier[0] - highest)
    scale_late = jnp.exp(later[0] - highest)
    denominator = earlier[1] * scale_early + later[1] * scale_late
    numerator = earlier[2] * scale_early[..., None] + later[2] * scale_late[..., None]
    return (highest, denominator, numerator)


MESH = pl.DeviceIdType.MESH
SUB = 128
CHUNKS = (32, 32, 32, 32)


def arrival_orders(n_tp, sub):
    orders = []
    for t in range(n_tp):
        near = 0 if 2 * t < n_tp else n_tp - 1
        inner = t not in (0, n_tp - 1)
        pieces = []
        for b in range(n_tp):
            away = abs(b - t)
            rank = away
            if inner and away:
                rank = 2 * away + (0 if (b > t) == (near == 0) else 1) - 1
            pieces += [(rank, u, b) for u in range(sub)]
        pieces.sort()
        orders.append([b * sub + u for _, u, b in pieces])
    return orders


def piece_at(orders, t, s):
    found = 0
    for place, order in enumerate(orders):
        for step, piece in enumerate(order):
            if isinstance(s, int):
                if s == step:
                    found = found + jnp.where(t == place, piece, 0)
            else:
                found = found + jnp.where(jnp.logical_and(t == place, s == step), piece, 0)
    return found


def sync_kernel(
    n_rep,
    n_tp,
    sub,
    tok_hbm,
    cot_hbm,
    master_hbm,
    m1_hbm,
    m2_hbm,
    keys_hbm,
    values_hbm,
    in1_hbm,
    in2_hbm,
    q1_hbm,
    q2_hbm,
    lengths_hbm,
    master_out,
    m1_out,
    m2_out,
    p1_out,
    p2_out,
    early_max,
    early_sum,
    early_mix,
    table_ref,
    queries,
    state,
    state_t,
    new_t,
    keys,
    values,
    inputs,
    lengths_ref,
    mask,
    q_ref,
    tok,
    cot_raw,
    cot,
    a_send,
    a_keep,
    a_recv,
    b_send,
    b_recv,
    w_buf,
    w_fine,
    part,
    part_recv,
    load_sem,
    z_ss,
    z_rs,
    z_fs,
    send_sem,
    a_rs,
    b_rs,
    w_rs,
    v_rs,
    p_rs,
):
    nc = n_rep // 2
    steps = n_tp * sub
    coarse = steps - 1
    cw = SUB
    chunks = []
    for width in CHUNKS:
        chunks.append(slice(sum(CHUNKS[: len(chunks)]), sum(CHUNKS[: len(chunks)]) + width))
    whole = slice(0, cw)
    r = lax.axis_index("rep")
    t = lax.axis_index("tp")
    k = r // 2
    c = r % 2
    sibling = (2 * k + 1 - c, t)
    own_rows = master_hbm.shape[0]
    att_rows, groups, stacked, _ = q_ref.shape
    orders = arrival_orders(n_tp, sub)
    last = piece_at(orders, t, coarse)
    last_cols = pl.ds(pl.multiple_of(last * cw, cw), cw)

    def chip(j):
        return (k + j) % nc

    def source_chip(j):
        return (k + nc - j) % nc

    def send(source, target, send_sem_ref, recv_sem_ref, device):
        return pltpu.make_async_remote_copy(
            source, target, send_sem_ref, recv_sem_ref, device_id=device, device_id_type=MESH
        )

    load_cot = pltpu.make_async_copy(cot_hbm, cot_raw, load_sem.at[0])
    load_tok = pltpu.make_async_copy(tok_hbm, tok, load_sem.at[1])
    load_lengths = pltpu.make_async_copy(lengths_hbm, lengths_ref, load_sem.at[2])
    load_keys = pltpu.make_async_copy(keys_hbm, keys, load_sem.at[3])
    load_values = pltpu.make_async_copy(values_hbm, values, load_sem.at[4])
    load_queries = [
        pltpu.make_async_copy(source, queries.at[i], load_sem.at[5 + i])
        for i, source in enumerate((q1_hbm, q2_hbm))
    ]
    load_inputs = [
        pltpu.make_async_copy(source, inputs.at[i], load_sem.at[7 + i])
        for i, source in enumerate((in1_hbm, in2_hbm))
    ]
    load_state = [
        pltpu.make_async_copy(source, state.at[i], load_sem.at[9 + i])
        for i, source in enumerate((master_hbm, m1_hbm, m2_hbm))
    ]
    load_cot.start()
    load_tok.start()
    late_loads = [*load_queries, load_keys, load_values, *load_state, *load_inputs]
    for load in [load_lengths, *late_loads]:
        load.start()

    barrier = pltpu.get_barrier_semaphore()
    pl.semaphore_signal(barrier, inc=1, device_id=sibling, device_id_type=MESH)
    for j in range(1, nc):
        pl.semaphore_signal(barrier, inc=1, device_id=(2 * chip(j) + c, t), device_id_type=MESH)
    for j in range(1, n_tp):
        pl.semaphore_signal(barrier, inc=1, device_id=(r, (t + j) % n_tp), device_id_type=MESH)
    load_cot.wait()
    for u in range(sub):
        cot[t * sub + u] = cot_raw[:, u * cw : (u + 1) * cw].T
    pl.semaphore_wait(barrier, 1 + (nc - 1) + (n_tp - 1))

    def neighbour(side):
        return jnp.minimum(t + 1, n_tp - 1) if side == 0 else jnp.maximum(t - 1, 0)

    def z_copy(g, side):
        return send(cot.at[g], cot.at[g], z_ss.at[side], z_rs.at[g], (r, neighbour(side)))

    def z_chunk(g, side, f):
        view = cot.at[g, chunks[f]]
        return send(view, view, z_ss.at[side], z_fs.at[f], (r, neighbour(side)))

    def z_goes(g, side):
        b = g // sub
        if side == 0:
            return jnp.logical_and(b <= t, t < n_tp - 1)
        return jnp.logical_and(b >= t, t > 0)

    def in_chunks(g, side):
        return g == piece_at(orders, neighbour(side), coarse)

    def z_forward(g):
        for side in (0, 1):
            @pl.when(jnp.logical_and(z_goes(g, side), jnp.logical_not(in_chunks(g, side))))
            def _():
                z_copy(g, side).start()

            @pl.when(jnp.logical_and(z_goes(g, side), in_chunks(g, side)))
            def _():
                for f in range(len(chunks)):
                    z_chunk(g, side, f).start()

    def z_forward_chunk(f):
        for side in (0, 1):
            @pl.when(jnp.logical_and(z_goes(last, side), in_chunks(last, side)))
            def _():
                z_chunk(last, side, f).start()

            if f == len(chunks) - 1:
                @pl.when(
                    jnp.logical_and(z_goes(last, side), jnp.logical_not(in_chunks(last, side)))
                )
                def _():
                    z_copy(last, side).start()

    for u in range(sub):
        z_forward(t * sub + u)
    load_lengths.wait()
    row_ids = lax.broadcasted_iota(jnp.int32, (att_rows, HD), 0)
    length = jnp.zeros((att_rows, HD), jnp.int32)
    for row in range(att_rows):
        length = jnp.where(row_ids == row, lengths_ref[row], length)
    table_ref[...] = decode_table(length[:, 0:1])
    mask[...] = table_ref[:, 0:HD]
    for load in load_queries:
        load.wait()
    for i in range(2):
        for h in range(groups):
            for place in range(stacked // 2):
                at = (h * (stacked // 2) + place) * HD
                q_ref[:, h, i * (stacked // 2) + place, :] = queries[i, :, at : at + HD].astype(
                    jnp.float32
                )
    load_tok.wait()
    for load in late_loads[2:]:
        load.wait()

    def a_copy(s, cols, slot):
        return send(
            a_send.at[s, :, cols], a_recv.at[s, :, cols], send_sem.at[0], a_rs.at[slot], sibling
        )

    def b_copy(s, cols, slot, j):
        return send(
            b_send.at[s, j - 1, cols], b_recv.at[s, j - 1, cols], send_sem.at[1], b_rs.at[slot],
            (2 * chip(j) + c, t),
        )

    def w_at(s, cols, slot, row):
        if isinstance(slot, int) and slot >= coarse:
            return w_fine.at[row, cols]
        return w_buf.at[s, row]

    def w_send(slot):
        return 2 if isinstance(slot, int) and slot >= coarse else 1

    def w_copy(s, cols, slot, j):
        view = w_at(s, cols, slot, r)
        return send(
            view, view, send_sem.at[1 + w_send(slot)], w_rs.at[slot], (2 * chip(j) + c, t)
        )

    def v_copy(s, cols, slot, j):
        view = w_at(s, cols, slot, 2 * source_chip(j) + c)
        slot = coarse if w_send(slot) == 2 else slot
        return send(view, view, send_sem.at[3 + w_send(slot)], v_rs.at[slot], sibling)

    def wait_recv(ref, sem):
        send(ref, ref, send_sem.at[0], sem, sibling).wait_recv()

    def wait_send(ref, sem):
        send(ref, ref, sem, a_rs.at[0], sibling).wait_send()

    def terms(g, s, cols, slot):
        def term(owner):
            at = pl.multiple_of(owner * own_rows, own_rows)
            return jnp.dot(
                cot[g, cols], tok[:, pl.ds(at, own_rows)], preferred_element_type=jnp.float32
            )

        for q in range(nc):
            a_send[s, q, cols] = term(2 * q + 1 - c)
        a_copy(s, cols, slot).start()
        for q in range(nc):
            a_keep[s, q, cols] = term(2 * q + c)

    def gradient_stage(s):
        g = piece_at(orders, t, s)

        @pl.when(g // sub != t)
        def _():
            z_copy(g, 0).wait_recv()
            z_forward(g)

        terms(g, s, whole, s)

    def gradient_chunk(f):
        z_chunk(last, 0, f).wait_recv()
        z_forward_chunk(f)
        terms(last, coarse, chunks[f], coarse + f)

    def chip_sum_stage(s, cols, slot):
        a_copy(s, cols, slot).wait_recv()
        for j in range(1, nc):
            q = chip(j)
            b_send[s, j - 1, cols] = (a_keep[s, q, cols] + a_recv[s, q, cols]).astype(
                jnp.bfloat16
            )
            b_copy(s, cols, slot, j).start()

    def summed(s, cols, slot):
        total = a_keep[s, k, cols] + a_recv[s, k, cols]
        wait_recv(b_recv.at[s, :, cols], b_rs.at[slot])
        for j in range(1, nc):
            total = total + b_recv[s, j - 1, cols].astype(jnp.float32)
        return total

    def adam(master, m1, m2, gradient):
        moment_one_new = beta_one * m1 + (1.0 - beta_one) * gradient
        moment_two_new = beta_two * m2 + (1.0 - beta_two) * gradient * gradient
        corrected_one = moment_one_new / (1.0 - beta_one**step_count)
        corrected_two = moment_two_new / (1.0 - beta_two**step_count)
        master_new = master - learning_rate * (
            corrected_one / (jnp.sqrt(corrected_two) + epsilon) + weight_decay * master
        )
        return master_new, moment_one_new, moment_two_new

    outs = (master_out, m1_out, m2_out)

    def spread(s, cols, slot):
        for j in range(1, nc):
            w_copy(s, cols, slot, j).start()
        v_copy(s, cols, slot, 0).start()

    def update_stage(s):
        cols = pl.ds(pl.multiple_of(piece_at(orders, t, s) * cw, cw), cw)
        updated = adam(*(state[i, :, cols] for i in range(3)), summed(s, whole, s).T)
        w_buf[s, r] = updated[0].astype(jnp.bfloat16)
        spread(s, whole, s)
        for out, value in zip(outs, updated):
            out[:, cols] = value

    def update_chunk(f):
        cols = chunks[f]
        updated = adam(*(state_t[i, cols] for i in range(3)), summed(coarse, cols, coarse + f))
        w_fine[r, cols] = updated[0].astype(jnp.bfloat16)
        spread(coarse, cols, coarse + f)
        for i, value in enumerate(updated):
            new_t[i, cols] = value

    def share_stage(s, cols, slot):
        if isinstance(slot, int) and slot >= coarse:
            view = w_fine.at[0 : nc - 1, cols]
        else:
            view = w_buf.at[s, 0 : nc - 1]
        wait_recv(view, w_rs.at[slot])
        for j in range(1, nc):
            v_copy(s, cols, slot, j).start()

    at_end = jnp.logical_or(t == 0, t == n_tp - 1)

    def to_end(j):
        to = (t + j) % n_tp
        return jnp.logical_or(to == 0, to == n_tp - 1)

    def p_copy(g, j):
        to = (t + j) % n_tp
        return send(part.at[g, to], part_recv.at[j - 1, g], send_sem.at[6], p_rs, (r, to))

    def decoded(g, product):
        rows = product.shape[0] // 2
        for i in range(2):
            part[g, :, i] = product[i * rows : (i + 1) * rows].reshape(n_tp, rows // n_tp, cw)

    both = inputs.shape[0] * inputs.shape[1]

    def decode_stage(s):
        wait_recv(w_buf.at[s, 0:nc], v_rs.at[s])
        g = piece_at(orders, t, s)
        block = w_buf[s].reshape(n_rep * own_rows, cw)
        decoded(
            g,
            jnp.dot(
                inputs[...].reshape(both, -1), block, preferred_element_type=jnp.float32
            ),
        )
        for j in range(1, n_tp):
            @pl.when(jnp.logical_not(to_end(j)))
            def _():
                p_copy(g, j).start()

    def decode_last():
        wait_recv(w_fine.at[0:nc], v_rs.at[coarse])
        product = 0.0
        for owner in range(n_rep):
            rows = inputs[:, :, owner * own_rows : (owner + 1) * own_rows]
            product = product + lax.dot_general(
                rows.reshape(both, own_rows),
                w_fine[owner],
                (((1,), (1,)), ((), ())),
                preferred_element_type=jnp.float32,
            )
        decoded(last, product)

        @pl.when(at_end)
        def _():
            for j in range(1, n_tp):
                p_copy(last, j).start()

        @pl.when(jnp.logical_not(at_end))
        def _():
            for j in range(1, n_tp):
                @pl.when(jnp.logical_not(to_end(j)))
                def _():
                    p_copy(last, j).start()

    def late_stage(s):
        g = piece_at(orders, t, s)
        for j in range(1, n_tp):
            @pl.when(to_end(j))
            def _():
                p_copy(g, j).start()

    cache_steps = min(4, coarse)

    def cache_stage(s):
        per_step = att_rows // cache_steps

        @pl.loop(0, per_step)
        def _(i):
            row = s * per_step + i
            allowed = mask[pl.ds(row, 1), :] > 0.0
            for h in range(groups):
                head = slice(h * HD, (h + 1) * HD)
                scores = lax.dot_general(
                    q_ref[row, h].astype(jnp.bfloat16),
                    keys[row, :, head],
                    (((1,), (1,)), ((), ())),
                    preferred_element_type=jnp.float32,
                )
                scores = jnp.where(allowed, scores / HD**0.5, -1e30)
                highest = jnp.max(scores, axis=-1, keepdims=True)
                weights = jnp.exp(scores - highest).astype(jnp.bfloat16)
                total = jnp.sum(weights.astype(jnp.float32), axis=-1, keepdims=True)
                mix = jnp.dot(weights, values[row, :, head], preferred_element_type=jnp.float32)
                for ref, value in ((early_max, highest), (early_sum, total), (early_mix, mix)):
                    value = jnp.broadcast_to(value, (stacked, HD))
                    ref[h, :, pl.ds(row, 1), :] = value.reshape(stacked, 1, HD)

    def turn_state():
        for i in range(3):
            state_t[i] = state[i, :, last_cols].T

    stages = (
        (gradient_stage, 0, coarse),
        (update_stage, 1, coarse),
        (cache_stage, 0, cache_steps),
        (lambda s: chip_sum_stage(s, whole, s), 0, coarse),
        (lambda s: share_stage(s, whole, s), 2, coarse),
        (decode_stage, 3, coarse),
    )

    @pl.loop(0, coarse)
    def _(it):
        for stage, lag, end in stages:
            @pl.when(jnp.logical_and(it >= lag, it < end + lag))
            def _():
                stage(it - lag)

        @pl.when(it == cache_steps - 1)
        def _():
            turn_state()

    def update_any(n):
        if n < coarse:
            update_stage(n)
        else:
            update_chunk(n - coarse)

    def share_any(n):
        if n < coarse:
            share_stage(n, whole, n)
        else:
            share_stage(coarse, chunks[n - coarse], n)

    units = coarse + len(chunks)
    for f, cols in enumerate(chunks):
        n = coarse + f
        gradient_chunk(f)
        update_any(n - 1)
        chip_sum_stage(coarse, cols, n)
        share_any(n - 2)
        if n - 3 < coarse:
            decode_stage(n - 3)
    for n in range(units - 3, coarse):
        decode_stage(n)

    @pl.when(at_end)
    def _():
        @pl.loop(0, coarse)
        def _(s):
            late_stage(s)

    update_any(units - 1)
    share_any(units - 2)
    for out, value in zip(outs, (new_t.at[0], new_t.at[1], new_t.at[2])):
        out[:, last_cols] = value[...].T
    share_any(units - 1)
    decode_last()

    for place in range(n_tp):
        @pl.when(t == place)
        def _():
            if place < n_tp - 1:
                wait_send(cot.at[0 : (place + 1) * sub], z_ss.at[0])
            if place > 0:
                wait_send(cot.at[0 : (n_tp - place) * sub], z_ss.at[1])

    @pl.when(jnp.logical_not(at_end))
    def _():
        @pl.loop(0, steps)
        def _(s):
            late_stage(s)

    wait_send(a_send, send_sem.at[0])
    wait_send(b_send, send_sem.at[1])
    wait_send(w_buf.at[:, 0 : nc - 1], send_sem.at[2])
    wait_send(w_fine.at[0 : nc - 1], send_sem.at[3])
    wait_send(w_buf.at[:, 0:nc], send_sem.at[4])
    wait_send(w_fine.at[0:nc], send_sem.at[5])
    wait_recv(part_recv, p_rs)
    for g in range(steps):
        for i, out in enumerate((p1_out, p2_out)):
            total = part[g, t, i]
            for j in range(1, n_tp):
                total = total + part_recv[j - 1, g, i]
            out[:, g * cw : (g + 1) * cw] = total
    wait_send(part.at[:, 0 : n_tp - 1], send_sem.at[6])


def finish_kernel(
    master,
    m1,
    m2,
    p1,
    p2,
    early_max,
    early_sum,
    early_mix,
    table,
    queries,
    master_out,
    m1_out,
    m2_out,
    p1_out,
    p2_out,
    att1_out,
    att2_out,
    att,
    sems,
    att_sems,
):
    stores = [
        pltpu.make_async_copy(source, target, sems.at[i])
        for i, (source, target) in enumerate(
            ((master, master_out), (m1, m1_out), (m2, m2_out), (p1, p1_out), (p2, p2_out))
        )
    ]
    for store in stores:
        store.start()
    groups, stacked = early_max.shape[:2]
    half = stacked // 2
    keys, values = [], []
    for i, ref in enumerate((p1, p2)):
        total = ref[...]
        cosine = table[:, (1 + 2 * i) * HD : (2 + 2 * i) * HD]
        sine = table[:, (2 + 2 * i) * HD : (3 + 2 * i) * HD]
        for h in range(groups):
            head = total[:, h * HD : (h + 1) * HD]
            turned = head * cosine + pltpu.roll(head, HD // 2, 1) * sine
            value = total[:, (groups + h) * HD : (groups + h + 1) * HD]
            keys.append(turned.astype(jnp.bfloat16).astype(jnp.float32))
            values.append(value.astype(jnp.bfloat16).astype(jnp.float32))
    for i, out in enumerate((att1_out, att2_out)):
        for h in range(groups):
            for place in range(half):
                at = slice((h * half + place) * HD, (h * half + place + 1) * HD)
                query = queries[i, :, at].astype(jnp.float32)
                scores = [
                    jnp.sum(query * keys[n * groups + h], axis=-1, keepdims=True) / HD**0.5
                    for n in range(i + 1)
                ]
                before = early_max[h, i * half + place]
                highest = before
                for score in scores:
                    highest = jnp.maximum(highest, score)
                scale = jnp.exp(before - highest)
                below = early_sum[h, i * half + place] * scale
                above = early_mix[h, i * half + place] * scale
                for n, score in enumerate(scores):
                    weight = jnp.exp(score - highest).astype(jnp.bfloat16).astype(jnp.float32)
                    below = below + weight
                    above = above + weight * values[n * groups + h]
                att[i, :, at] = above / below
        store = pltpu.make_async_copy(att.at[i], out, att_sems.at[i])
        store.start()
        stores.append(store)
    for store in stores:
        store.wait()


def synchronise(
    n_rep,
    n_tp,
    tokens_in,
    cotangent,
    master,
    m1,
    m2,
    cache_keys,
    cache_values,
    inputs_one,
    inputs_two,
    queries_one,
    queries_two,
    lengths,
):
    tokens, width = tokens_in.shape
    sub = cotangent.shape[1] // SUB
    steps = n_tp * sub
    units = steps - 1 + len(CHUNKS)
    nc = n_rep // 2
    rows, cols = master.shape
    decode = inputs_one.shape[0]
    share = decode // n_tp
    f32, bf16 = jnp.float32, jnp.bfloat16
    count = queries_one.shape[0]
    stacked = (count, KVH, 2 * QH // KVH, HD)
    early = (KVH, 2 * QH // KVH, count, HD)
    vmem = pl.BlockSpec(memory_space=pltpu.VMEM)
    hbm = pl.BlockSpec(memory_space=pl.ANY)
    dma = pltpu.SemaphoreType.DMA
    held = pl.pallas_call(
        functools.partial(sync_kernel, n_rep, n_tp, sub),
        out_shape=[pltpu.VMEM((rows, cols), f32)] * 3
        + [pltpu.VMEM((share, cols), f32)] * 2
        + [pltpu.VMEM(early, f32)] * 3
        + [pltpu.VMEM((count, 5 * HD), f32), pltpu.VMEM((2, *queries_one.shape), bf16)],
        in_specs=[hbm] * 12,
        out_specs=[vmem] * 10,
        scratch_shapes=[
            pltpu.VMEM((3, rows, cols), f32),
            pltpu.VMEM((3, SUB, rows), f32),
            pltpu.VMEM((3, SUB, rows), f32),
            pltpu.VMEM(cache_keys.shape, bf16),
            pltpu.VMEM(cache_values.shape, bf16),
            pltpu.VMEM((2, *inputs_one.shape), bf16),
            pltpu.SMEM(lengths.shape, jnp.int32),
            pltpu.VMEM((count, HD), f32),
            pltpu.VMEM(stacked, f32),
            pltpu.VMEM((tokens, width), bf16),
            pltpu.VMEM((tokens, sub * SUB), bf16),
            pltpu.VMEM((steps, SUB, tokens), bf16),
            pltpu.VMEM((steps, nc, SUB, rows), f32),
            pltpu.VMEM((steps, nc, SUB, rows), f32),
            pltpu.VMEM((steps, nc, SUB, rows), f32),
            pltpu.VMEM((steps, nc - 1, SUB, rows), bf16),
            pltpu.VMEM((steps, nc - 1, SUB, rows), bf16),
            pltpu.VMEM((steps - 1, n_rep, rows, SUB), bf16),
            pltpu.VMEM((n_rep, SUB, rows), bf16),
            pltpu.VMEM((steps, n_tp, 2, share, SUB), f32),
            pltpu.VMEM((n_tp - 1, steps, 2, share, SUB), f32),
            dma((12,)),
            dma((2,)),
            dma((steps,)),
            dma((len(CHUNKS),)),
            dma((7,)),
            dma((units,)),
            dma((units,)),
            dma((units,)),
            dma((steps,)),
            dma(()),
        ],
        compiler_params=pltpu.CompilerParams(
            collective_id=0, has_side_effects=True, vmem_limit_bytes=52 * 2**20
        ),
        name="synchronise",
    )(
        tokens_in,
        cotangent,
        master,
        m1,
        m2,
        cache_keys,
        cache_values,
        inputs_one,
        inputs_two,
        queries_one,
        queries_two,
        lengths,
    )
    wide = queries_one.shape
    return pl.pallas_call(
        finish_kernel,
        out_shape=[jax.ShapeDtypeStruct((rows, cols), f32)] * 3
        + [jax.ShapeDtypeStruct((share, cols), f32)] * 2
        + [jax.ShapeDtypeStruct(wide, f32)] * 2,
        in_specs=[vmem] * 10,
        out_specs=[hbm] * 7,
        scratch_shapes=[pltpu.VMEM((2, *wide), f32), dma((5,)), dma((2,))],
        compiler_params=pltpu.CompilerParams(vmem_limit_bytes=4 * 2**20),
        name="finish",
    )(*held)


def decode_table(lengths):
    shape = (lengths.shape[0], 5 * HD)
    column = lax.broadcasted_iota(jnp.int32, shape, 1)
    kind = column // HD
    lane = column % HD
    half_size = HD // 2
    inverse = rope_base ** (-2.0 * (lane % half_size).astype(jnp.float32) / HD)
    position = lengths + jnp.where(kind >= 3, 1, 0)
    angles = position.astype(jnp.float32) * inverse
    sine = jnp.where(lane < half_size, -jnp.sin(angles), jnp.sin(angles))
    allowed = jnp.where(lane < lengths, 1.0, 0.0)
    return jnp.where(kind == 0, allowed, jnp.where(kind % 2 == 1, jnp.cos(angles), sine))


def fits_kernel(n_rep, n_tp, cotangent, master, inputs_one, cache_keys):
    steps = n_tp * (cotangent.shape[1] // SUB)
    return (
        cache_keys.shape[1] == HD
        and steps > 4
        and cache_keys.shape[0] % 4 == 0
        and n_rep % 2 == 0
        and n_rep >= 4
        and n_tp >= 2
        and cotangent.shape[1] % SUB == 0
        and cotangent.shape[0] % 256 == 0
        and master.shape[1] % 128 == 0
        and inputs_one.shape[0] % (8 * n_tp) == 0
    )


def shards(
    n_rep,
    n_tp,
    tokens_in,
    cotangent,
    master,
    moment_one,
    moment_two,
    inputs_one,
    inputs_two,
    queries_one,
    queries_two,
    cache_keys,
    cache_values,
    lengths,
):
    row_count = cache_keys.shape[0]
    if fits_kernel(n_rep, n_tp, cotangent, master[0], inputs_one, cache_keys):
        *updated, both_one, both_two, attended_one, attended_two = synchronise(
            n_rep,
            n_tp,
            tokens_in,
            cotangent,
            master[0],
            moment_one[0],
            moment_two[0],
            cache_keys,
            cache_values,
            inputs_one,
            inputs_two,
            queries_one,
            queries_two,
            lengths,
        )
        return (
            *(array[None] for array in updated),
            both_one,
            both_two,
            attended_one,
            attended_two,
        )
    places = jnp.arange(cache_keys.shape[1], dtype=jnp.int32)
    cache_allowed = places[None, :] < lengths[:, None]
    fresh = jnp.zeros((row_count, 1), jnp.int32) == 0
    early_one = partial_scores(queries_one, cache_keys, cache_values, cache_allowed)
    early_two = partial_scores(queries_two, cache_keys, cache_values, cache_allowed)
    columns = lax.all_gather(cotangent, "tp", axis=1, tiled=True)
    gradient = lax.psum_scatter(
        lax.dot_general(
            tokens_in, columns, (((0,), (0,)), ((), ())), preferred_element_type=jnp.float32
        ),
        "rep",
        scatter_dimension=0,
        tiled=True,
    ).reshape(master.shape)
    moment_one_new = beta_one * moment_one + (1.0 - beta_one) * gradient
    moment_two_new = beta_two * moment_two + (1.0 - beta_two) * gradient * gradient
    corrected_one = moment_one_new / (1.0 - beta_one**step_count)
    corrected_two = moment_two_new / (1.0 - beta_two**step_count)
    master_new = master - learning_rate * (
        corrected_one / (jnp.sqrt(corrected_two) + epsilon) + weight_decay * master
    )
    weights = master_new[0].astype(jnp.bfloat16)
    shard_rows = lax.all_gather(weights, "rep", axis=0, tiled=True)
    partial_one = jnp.dot(inputs_one, shard_rows, preferred_element_type=jnp.float32)
    partial_two = jnp.dot(inputs_two, shard_rows, preferred_element_type=jnp.float32)
    both_one, both_two = (
        lax.psum_scatter(partial_one, "tp", scatter_dimension=0, tiled=True),
        lax.psum_scatter(partial_two, "tp", scatter_dimension=0, tiled=True),
    )
    key_width = both_one.shape[1] // 2
    keys_one = rotate(both_one[:, :key_width], lengths).astype(jnp.bfloat16)
    values_one = both_one[:, key_width:].astype(jnp.bfloat16)
    keys_two = rotate(both_two[:, :key_width], lengths + 1).astype(jnp.bfloat16)
    values_two = both_two[:, key_width:].astype(jnp.bfloat16)
    late_one = partial_scores(queries_one, keys_one[:, None], values_one[:, None], fresh)
    attended_one = finish(*combine(early_one, late_one))
    fresh_pair = jnp.concatenate([fresh, fresh], axis=1)
    late_two = partial_scores(
        queries_two,
        jnp.stack([keys_one, keys_two], axis=1),
        jnp.stack([values_one, values_two], axis=1),
        fresh_pair,
    )
    attended_two = finish(*combine(early_two, late_two))
    return (
        master_new,
        moment_one_new,
        moment_two_new,
        both_one,
        both_two,
        attended_one,
        attended_two,
    )


def solution(mesh):
    return jax.shard_map(
        functools.partial(shards, mesh.shape["rep"], mesh.shape["tp"]),
        mesh=mesh,
        in_specs=(
            P("rep", "tp"),
            P("rep", "tp"),
            P("tp", "rep", None),
            P("tp", "rep", None),
            P("tp", "rep", None),
            P("rep", "tp"),
            P("rep", "tp"),
            P(("rep", "tp"), None),
            P(("rep", "tp"), None),
            P(("rep", "tp"), None, None),
            P(("rep", "tp"), None, None),
            P(("rep", "tp")),
        ),
        out_specs=(
            P("tp", "rep", None),
            P("tp", "rep", None),
            P("tp", "rep", None),
            P(("rep", "tp"), None),
            P(("rep", "tp"), None),
            P(("rep", "tp"), None),
            P(("rep", "tp"), None),
        ),
        check_vma=False,
    )
```

```python
import functools

import jax
import jax.numpy as jnp
from jax import lax
from jax.experimental import pallas as pl
from jax.experimental.pallas import tpu as pltpu
from jax.sharding import PartitionSpec as P

KVH = 4
QH = 32
HD = 128


learning_rate = 0.001
beta_one = 0.9
beta_two = 0.99
epsilon = 1e-08
weight_decay = 0.1
step_count = 10.0
rope_base = 500000.0


def rotate(vectors, positions):
    row_count = vectors.shape[0]
    half_size = HD // 2
    inverse = rope_base ** (-2.0 * jnp.arange(half_size).astype(jnp.float32) / HD)
    angles = positions.astype(jnp.float32)[:, None, None] * inverse[None, None, :]
    shaped = vectors.reshape(row_count, -1, HD)
    first_half = shaped[..., :half_size]
    second_half = shaped[..., half_size:]
    cosine = jnp.cos(angles)
    sine = jnp.sin(angles)
    turned = jnp.concatenate(
        [first_half * cosine - second_half * sine, second_half * cosine + first_half * sine],
        axis=-1,
    )
    return turned.reshape(row_count, -1)


def partial_scores(queries, all_keys, all_values, allowed):
    row_count = all_keys.shape[0]
    places = all_keys.shape[1]
    group_size = QH // KVH
    shaped_queries = queries.astype(jnp.float32).reshape(row_count, KVH, group_size, HD)
    shaped_keys = all_keys.astype(jnp.float32).reshape(row_count, places, KVH, HD)
    shaped_values = all_values.astype(jnp.float32).reshape(row_count, places, KVH, HD)
    scores = jnp.einsum("rkgd,rpkd->rkgp", shaped_queries, shaped_keys) / HD**0.5
    scores = jnp.where(allowed[:, None, None, :], scores, -1e30)
    highest = jnp.max(scores, axis=-1)
    weights = lax.optimization_barrier(
        jnp.exp(scores - highest[..., None]).astype(jnp.bfloat16)
    ).astype(jnp.float32)
    return (
        highest,
        jnp.sum(weights, axis=-1),
        jnp.einsum("rkgp,rpkd->rkgd", weights, shaped_values),
    )


def finish(highest, denominator, numerator):
    row_count = numerator.shape[0]
    return (numerator / denominator[..., None]).reshape(row_count, -1)


def combine(earlier, later):
    highest = jnp.maximum(earlier[0], later[0])
    scale_early = jnp.exp(earlier[0] - highest)
    scale_late = jnp.exp(later[0] - highest)
    denominator = earlier[1] * scale_early + later[1] * scale_late
    numerator = earlier[2] * scale_early[..., None] + later[2] * scale_late[..., None]
    return (highest, denominator, numerator)


MESH = pl.DeviceIdType.MESH
SUB = 128
CHUNKS = (48, 32, 32, 16)


def arrival_orders(n_tp, sub):
    orders = []
    for t in range(n_tp):
        near = 0 if 2 * t < n_tp else n_tp - 1
        inner = t not in (0, n_tp - 1)
        pieces = []
        for b in range(n_tp):
            away = abs(b - t)
            rank = away
            if inner and away:
                rank = 2 * away + (0 if (b > t) == (near == 0) else 1) - 1
            pieces += [(rank, u, b) for u in range(sub)]
        pieces.sort()
        orders.append([b * sub + u for _, u, b in pieces])
    return orders


def piece_at(orders, t, s):
    found = 0
    for place, order in enumerate(orders):
        for step, piece in enumerate(order):
            if isinstance(s, int):
                if s == step:
                    found = found + jnp.where(t == place, piece, 0)
            else:
                found = found + jnp.where(jnp.logical_and(t == place, s == step), piece, 0)
    return found


def sync_kernel(
    n_rep,
    n_tp,
    sub,
    tok_hbm,
    cot_hbm,
    master_hbm,
    m1_hbm,
    m2_hbm,
    keys_hbm,
    values_hbm,
    in1_hbm,
    in2_hbm,
    q1_hbm,
    q2_hbm,
    lengths_hbm,
    master_out,
    m1_out,
    m2_out,
    p1_out,
    p2_out,
    early_max,
    early_sum,
    early_mix,
    table_ref,
    queries,
    state,
    state_t,
    new_t,
    keys,
    values,
    inputs,
    lengths_ref,
    mask,
    q_ref,
    tok,
    cot_raw,
    cot,
    a_send,
    a_keep,
    a_recv,
    b_send,
    b_recv,
    w_buf,
    w_fine,
    part,
    part_recv,
    load_sem,
    z_ss,
    z_rs,
    z_fs,
    send_sem,
    a_rs,
    b_rs,
    w_rs,
    v_rs,
    p_rs,
):
    nc = n_rep // 2
    steps = n_tp * sub
    coarse = steps - 1
    cw = SUB
    chunks = []
    for width in CHUNKS:
        chunks.append(slice(sum(CHUNKS[: len(chunks)]), sum(CHUNKS[: len(chunks)]) + width))
    whole = slice(0, cw)
    r = lax.axis_index("rep")
    t = lax.axis_index("tp")
    k = r // 2
    c = r % 2
    sibling = (2 * k + 1 - c, t)
    own_rows = master_hbm.shape[0]
    att_rows, groups, stacked, _ = q_ref.shape
    orders = arrival_orders(n_tp, sub)
    last = piece_at(orders, t, coarse)
    last_cols = pl.ds(pl.multiple_of(last * cw, cw), cw)

    def chip(j):
        return (k + j) % nc

    def source_chip(j):
        return (k + nc - j) % nc

    def send(source, target, send_sem_ref, recv_sem_ref, device):
        return pltpu.make_async_remote_copy(
            source, target, send_sem_ref, recv_sem_ref, device_id=device, device_id_type=MESH
        )

    load_cot = pltpu.make_async_copy(cot_hbm, cot_raw, load_sem.at[0])
    load_tok = pltpu.make_async_copy(tok_hbm, tok, load_sem.at[1])
    load_lengths = pltpu.make_async_copy(lengths_hbm, lengths_ref, load_sem.at[2])
    load_keys = pltpu.make_async_copy(keys_hbm, keys, load_sem.at[3])
    load_values = pltpu.make_async_copy(values_hbm, values, load_sem.at[4])
    load_queries = [
        pltpu.make_async_copy(source, queries.at[i], load_sem.at[5 + i])
        for i, source in enumerate((q1_hbm, q2_hbm))
    ]
    load_inputs = [
        pltpu.make_async_copy(source, inputs.at[i], load_sem.at[7 + i])
        for i, source in enumerate((in1_hbm, in2_hbm))
    ]
    load_state = [
        pltpu.make_async_copy(source, state.at[i], load_sem.at[9 + i])
        for i, source in enumerate((master_hbm, m1_hbm, m2_hbm))
    ]
    load_cot.start()
    barrier = pltpu.get_barrier_semaphore()
    for j in range(1, n_rep):
        pl.semaphore_signal(barrier, inc=1, device_id=((r + j) % n_rep, t), device_id_type=MESH)
    for j in range(1, n_tp):
        pl.semaphore_signal(barrier, inc=1, device_id=(r, (t + j) % n_tp), device_id_type=MESH)
    late_loads = [*load_queries, load_keys, load_values, *load_state, *load_inputs]
    load_cot.wait()
    for load in [load_lengths, *late_loads[:4], load_tok, *late_loads[4:]]:
        load.start()
    cot[t * sub] = cot_raw[:, 0:cw].T
    pl.semaphore_wait(barrier, (n_rep - 1) + (n_tp - 1))

    def neighbour(side):
        return jnp.minimum(t + 1, n_tp - 1) if side == 0 else jnp.maximum(t - 1, 0)

    def z_copy(g, side):
        return send(cot.at[g], cot.at[g], z_ss.at[side], z_rs.at[g], (r, neighbour(side)))

    def z_chunk(g, side, f):
        view = cot.at[g, chunks[f]]
        return send(view, view, z_ss.at[side], z_fs.at[f], (r, neighbour(side)))

    def z_goes(g, side):
        b = g // sub
        if side == 0:
            return jnp.logical_and(b <= t, t < n_tp - 1)
        return jnp.logical_and(b >= t, t > 0)

    def in_chunks(g, side):
        return g == piece_at(orders, neighbour(side), coarse)

    def z_forward(g):
        for side in (0, 1):
            @pl.when(jnp.logical_and(z_goes(g, side), jnp.logical_not(in_chunks(g, side))))
            def _():
                z_copy(g, side).start()

            @pl.when(jnp.logical_and(z_goes(g, side), in_chunks(g, side)))
            def _():
                for f in range(len(chunks)):
                    z_chunk(g, side, f).start()

    def z_forward_chunk(f):
        for side in (0, 1):
            @pl.when(jnp.logical_and(z_goes(last, side), in_chunks(last, side)))
            def _():
                z_chunk(last, side, f).start()

            if f == len(chunks) - 1:
                @pl.when(
                    jnp.logical_and(z_goes(last, side), jnp.logical_not(in_chunks(last, side)))
                )
                def _():
                    z_copy(last, side).start()

    z_forward(t * sub)
    for u in range(1, sub):
        cot[t * sub + u] = cot_raw[:, u * cw : (u + 1) * cw].T
        z_forward(t * sub + u)
    load_lengths.wait()
    row_ids = lax.broadcasted_iota(jnp.int32, (att_rows, HD), 0)
    length = jnp.zeros((att_rows, HD), jnp.int32)
    for row in range(att_rows):
        length = jnp.where(row_ids == row, lengths_ref[row], length)
    table_ref[...] = decode_table(length[:, 0:1])
    mask[...] = table_ref[:, 0:HD]
    for load in load_queries:
        load.wait()
    for i in range(2):
        for h in range(groups):
            for place in range(stacked // 2):
                at = (h * (stacked // 2) + place) * HD
                q_ref[:, h, i * (stacked // 2) + place, :] = queries[i, :, at : at + HD].astype(
                    jnp.float32
                )
    load_tok.wait()
    for load in late_loads[2:]:
        load.wait()

    def a_copy(s, cols, slot):
        return send(
            a_send.at[s, :, cols], a_recv.at[s, :, cols], send_sem.at[0], a_rs.at[slot], sibling
        )

    def b_copy(s, cols, slot, j):
        return send(
            b_send.at[s, j - 1, cols], b_recv.at[s, j - 1, cols], send_sem.at[1], b_rs.at[slot],
            (2 * chip(j) + c, t),
        )

    def w_copy(s, j):
        view = w_buf.at[s, r]
        return send(view, view, send_sem.at[2], w_rs.at[s], (2 * chip(j) + c, t))

    def w_chunk(f, j):
        view = w_fine.at[r, chunks[f]]
        return send(view, view, send_sem.at[3], w_rs.at[coarse + f], (2 * chip(j) + c, t))

    def v_chunk(f, j):
        view = w_fine.at[2 * source_chip(j) + c, chunks[f]]
        return send(view, view, send_sem.at[6], v_rs.at[coarse], sibling)

    def w_direct(j):
        view = w_fine.at[r, chunks[-1]]
        return send(
            view, view, send_sem.at[7], w_rs.at[coarse + len(chunks) - 1], ((r + j) % n_rep, t)
        )

    def v_copy(s, j):
        view = w_buf.at[s, 2 * source_chip(j) + c]
        return send(view, view, send_sem.at[4], v_rs.at[s], sibling)

    def wait_recv(ref, sem):
        send(ref, ref, send_sem.at[0], sem, sibling).wait_recv()

    def wait_send(ref, sem):
        send(ref, ref, sem, a_rs.at[0], sibling).wait_send()

    def terms(g, s, cols, slot):
        def term(owner):
            at = pl.multiple_of(owner * own_rows, own_rows)
            return jnp.dot(
                cot[g, cols], tok[:, pl.ds(at, own_rows)], preferred_element_type=jnp.float32
            )

        for q in range(nc):
            a_send[s, q, cols] = term(2 * q + 1 - c)
        a_copy(s, cols, slot).start()
        for q in range(nc):
            a_keep[s, q, cols] = term(2 * q + c)

    def gradient_stage(s):
        g = piece_at(orders, t, s)

        @pl.when(g // sub != t)
        def _():
            z_copy(g, 0).wait_recv()
            z_forward(g)

        terms(g, s, whole, s)

    def gradient_chunk(f):
        z_chunk(last, 0, f).wait_recv()
        z_forward_chunk(f)
        terms(last, coarse, chunks[f], coarse + f)

    def chip_sum_stage(s, cols, slot):
        a_copy(s, cols, slot).wait_recv()
        for j in range(1, nc):
            q = chip(j)
            b_send[s, j - 1, cols] = (a_keep[s, q, cols] + a_recv[s, q, cols]).astype(
                jnp.bfloat16
            )
            b_copy(s, cols, slot, j).start()

    def summed(s, cols, slot):
        total = a_keep[s, k, cols] + a_recv[s, k, cols]
        wait_recv(b_recv.at[s, :, cols], b_rs.at[slot])
        for j in range(1, nc):
            total = total + b_recv[s, j - 1, cols].astype(jnp.float32)
        return total

    def adam(master, m1, m2, gradient):
        moment_one_new = beta_one * m1 + (1.0 - beta_one) * gradient
        moment_two_new = beta_two * m2 + (1.0 - beta_two) * gradient * gradient
        corrected_one = moment_one_new / (1.0 - beta_one**step_count)
        corrected_two = moment_two_new / (1.0 - beta_two**step_count)
        master_new = master - learning_rate * (
            corrected_one / (jnp.sqrt(corrected_two) + epsilon) + weight_decay * master
        )
        return master_new, moment_one_new, moment_two_new

    outs = (master_out, m1_out, m2_out)

    def update_stage(s):
        cols = pl.ds(pl.multiple_of(piece_at(orders, t, s) * cw, cw), cw)
        updated = adam(*(state[i, :, cols] for i in range(3)), summed(s, whole, s).T)
        w_buf[s, r] = updated[0].astype(jnp.bfloat16)
        for j in range(1, nc):
            w_copy(s, j).start()
        v_copy(s, 0).start()
        for out, value in zip(outs, updated):
            out[:, cols] = value

    def update_chunk(f):
        cols = chunks[f]
        updated = adam(*(state_t[i, cols] for i in range(3)), summed(coarse, cols, coarse + f))
        w_fine[r, cols] = updated[0].astype(jnp.bfloat16)
        if f == len(chunks) - 1:
            for j in range(1, n_rep):
                w_direct(j).start()
        else:
            for j in range(1, nc):
                w_chunk(f, j).start()
            v_chunk(f, 0).start()
        for i, value in enumerate(updated):
            new_t[i, cols] = value

    def share_stage(s):
        wait_recv(w_buf.at[s, 0 : nc - 1], w_rs.at[s])
        for j in range(1, nc):
            v_copy(s, j).start()

    def share_chunk(f):
        wait_recv(w_fine.at[0 : nc - 1, chunks[f]], w_rs.at[coarse + f])
        for j in range(1, nc):
            v_chunk(f, j).start()

    at_end = jnp.logical_or(t == 0, t == n_tp - 1)

    def to_end(j):
        to = (t + j) % n_tp
        return jnp.logical_or(to == 0, to == n_tp - 1)

    def p_copy(g, j):
        to = (t + j) % n_tp
        return send(part.at[g, to], part_recv.at[j - 1, g], send_sem.at[5], p_rs, (r, to))

    def decoded(g, product):
        rows = product.shape[0] // 2
        for i in range(2):
            part[g, :, i] = product[i * rows : (i + 1) * rows].reshape(n_tp, rows // n_tp, cw)

    both = inputs.shape[0] * inputs.shape[1]

    def decode_stage(s):
        wait_recv(w_buf.at[s, 0:nc], v_rs.at[s])
        g = piece_at(orders, t, s)
        block = w_buf[s].reshape(n_rep * own_rows, cw)
        decoded(
            g,
            jnp.dot(
                inputs[...].reshape(both, -1), block, preferred_element_type=jnp.float32
            ),
        )
        for j in range(1, n_tp):
            @pl.when(jnp.logical_not(to_end(j)))
            def _():
                p_copy(g, j).start()

    def decode_last():
        wait_recv(w_fine.at[0 : n_rep - 1, chunks[-1]], w_rs.at[coarse + len(chunks) - 1])
        wait_recv(w_fine.at[0:nc, 0 : chunks[-1].start], v_rs.at[coarse])
        product = 0.0
        for owner in range(n_rep):
            rows = inputs[:, :, owner * own_rows : (owner + 1) * own_rows]
            product = product + lax.dot_general(
                rows.reshape(both, own_rows),
                w_fine[owner],
                (((1,), (1,)), ((), ())),
                preferred_element_type=jnp.float32,
            )
        decoded(last, product)

        @pl.when(at_end)
        def _():
            for j in range(1, n_tp):
                p_copy(last, j).start()

        @pl.when(jnp.logical_not(at_end))
        def _():
            for j in range(1, n_tp):
                @pl.when(jnp.logical_not(to_end(j)))
                def _():
                    p_copy(last, j).start()

    def late_stage(s):
        g = piece_at(orders, t, s)
        for j in range(1, n_tp):
            @pl.when(to_end(j))
            def _():
                p_copy(g, j).start()

    cache_steps = min(4, coarse)

    def cache_stage(s):
        per_step = att_rows // cache_steps

        @pl.loop(0, per_step)
        def _(i):
            row = s * per_step + i
            allowed = mask[pl.ds(row, 1), :] > 0.0
            for h in range(groups):
                head = slice(h * HD, (h + 1) * HD)
                scores = lax.dot_general(
                    q_ref[row, h].astype(jnp.bfloat16),
                    keys[row, :, head],
                    (((1,), (1,)), ((), ())),
                    preferred_element_type=jnp.float32,
                )
                scores = jnp.where(allowed, scores / HD**0.5, -1e30)
                highest = jnp.max(scores, axis=-1, keepdims=True)
                weights = jnp.exp(scores - highest).astype(jnp.bfloat16)
                total = jnp.sum(weights.astype(jnp.float32), axis=-1, keepdims=True)
                mix = jnp.dot(weights, values[row, :, head], preferred_element_type=jnp.float32)
                for ref, value in ((early_max, highest), (early_sum, total), (early_mix, mix)):
                    value = jnp.broadcast_to(value, (stacked, HD))
                    ref[h, :, pl.ds(row, 1), :] = value.reshape(stacked, 1, HD)

    def turn_state():
        for i in range(3):
            state_t[i] = state[i, :, last_cols].T

    def sum_stage(s):
        chip_sum_stage(s, whole, s)

    def ahead(s):
        return jnp.logical_and(at_end, s >= cache_steps)

    def never(s):
        return False

    stages = (
        (sum_stage, 1, ahead),
        (update_stage, 2, lambda s: jnp.logical_and(at_end, s >= cache_steps - 1)),
        (share_stage, 3, never),
        (decode_stage, 4, never),
    )
    cache_now = jnp.where(at_end, cache_steps, 1)

    @pl.loop(0, coarse)
    def _(it):
        for stage, lag, skip in stages:
            @pl.when(jnp.logical_and(it >= lag, jnp.logical_not(skip(it - lag))))
            def _():
                stage(it - lag)

        @pl.when(it < cache_now)
        def _():
            cache_stage(it)

        gradient_stage(it)

        @pl.when(jnp.logical_and(ahead(it), it < coarse - 1))
        def _():
            sum_stage(it)

            @pl.when(it == cache_steps)
            def _():
                update_stage(it - 1)

            update_stage(it)

        @pl.when(it == cache_steps)
        def _():
            turn_state()

    sum_stage(coarse - 1)

    @pl.when(jnp.logical_not(at_end))
    def _():
        update_stage(coarse - 2)

    share_stage(coarse - 3)
    decode_stage(coarse - 4)

    @pl.when(jnp.logical_not(at_end))
    def _():
        cache_stage(1)

    final = len(chunks) - 1
    for f, cols in enumerate(chunks):
        gradient_chunk(f)
        chip_sum_stage(coarse, cols, coarse + f)
        if f == 0:
            share_stage(coarse - 2)
            if final > 1:
                update_stage(coarse - 1)
        if f > 1:
            update_chunk(f - 2)
    if final < 2:
        update_stage(coarse - 1)
    if final > 0:
        update_chunk(final - 1)
    update_chunk(final)
    share_stage(coarse - 1)
    for f in range(final - 1):
        share_chunk(f)
    for s in range(coarse - 3, coarse):
        decode_stage(s)

    @pl.when(at_end)
    def _():
        @pl.loop(0, coarse)
        def _(s):
            late_stage(s)

    if final > 0:
        share_chunk(final - 1)
    for i, out in enumerate(outs):
        out[:, last_cols] = new_t[i].T
    decode_last()

    for place in range(n_tp):
        @pl.when(t == place)
        def _():
            if place < n_tp - 1:
                wait_send(cot.at[0 : (place + 1) * sub], z_ss.at[0])
            if place > 0:
                wait_send(cot.at[0 : (n_tp - place) * sub], z_ss.at[1])

    @pl.when(jnp.logical_not(at_end))
    def _():
        @pl.loop(0, steps)
        def _(s):
            late_stage(s)

        @pl.loop(2, cache_steps)
        def _(s):
            cache_stage(s)

    wait_send(a_send, send_sem.at[0])
    wait_send(b_send, send_sem.at[1])
    wait_send(w_buf.at[:, 0 : nc - 1], send_sem.at[2])
    wait_send(w_fine.at[0 : nc - 1, 0 : chunks[-1].start], send_sem.at[3])
    wait_send(w_fine.at[0:nc, 0 : chunks[-1].start], send_sem.at[6])
    wait_send(w_fine.at[0 : n_rep - 1, chunks[-1]], send_sem.at[7])
    wait_send(w_buf.at[:, 0:nc], send_sem.at[4])
    wait_recv(part_recv, p_rs)
    for g in range(steps):
        for i, out in enumerate((p1_out, p2_out)):
            total = part[g, t, i]
            for j in range(1, n_tp):
                total = total + part_recv[j - 1, g, i]
            out[:, g * cw : (g + 1) * cw] = total
    wait_send(part.at[:, 0 : n_tp - 1], send_sem.at[5])


def finish_kernel(
    master,
    m1,
    m2,
    p1,
    p2,
    early_max,
    early_sum,
    early_mix,
    table,
    queries,
    master_out,
    m1_out,
    m2_out,
    p1_out,
    p2_out,
    att1_out,
    att2_out,
    att,
    sems,
    att_sems,
):
    stores = [
        pltpu.make_async_copy(source, target, sems.at[i])
        for i, (source, target) in enumerate(
            ((master, master_out), (m1, m1_out), (m2, m2_out), (p1, p1_out), (p2, p2_out))
        )
    ]
    for store in stores:
        store.start()
    groups, stacked = early_max.shape[:2]
    half = stacked // 2
    keys, values = [], []
    for i, ref in enumerate((p1, p2)):
        total = ref[...]
        cosine = table[:, (1 + 2 * i) * HD : (2 + 2 * i) * HD]
        sine = table[:, (2 + 2 * i) * HD : (3 + 2 * i) * HD]
        for h in range(groups):
            head = total[:, h * HD : (h + 1) * HD]
            turned = head * cosine + pltpu.roll(head, HD // 2, 1) * sine
            value = total[:, (groups + h) * HD : (groups + h + 1) * HD]
            keys.append(turned.astype(jnp.bfloat16).astype(jnp.float32))
            values.append(value.astype(jnp.bfloat16).astype(jnp.float32))
    for i, out in enumerate((att1_out, att2_out)):
        for h in range(groups):
            for place in range(half):
                at = slice((h * half + place) * HD, (h * half + place + 1) * HD)
                query = queries[i, :, at].astype(jnp.float32)
                scores = [
                    jnp.sum(query * keys[n * groups + h], axis=-1, keepdims=True) / HD**0.5
                    for n in range(i + 1)
                ]
                before = early_max[h, i * half + place]
                highest = before
                for score in scores:
                    highest = jnp.maximum(highest, score)
                scale = jnp.exp(before - highest)
                below = early_sum[h, i * half + place] * scale
                above = early_mix[h, i * half + place] * scale
                for n, score in enumerate(scores):
                    weight = jnp.exp(score - highest).astype(jnp.bfloat16).astype(jnp.float32)
                    below = below + weight
                    above = above + weight * values[n * groups + h]
                att[i, :, at] = above / below
        store = pltpu.make_async_copy(att.at[i], out, att_sems.at[i])
        store.start()
        stores.append(store)
    for store in stores:
        store.wait()


def synchronise(
    n_rep,
    n_tp,
    tokens_in,
    cotangent,
    master,
    m1,
    m2,
    cache_keys,
    cache_values,
    inputs_one,
    inputs_two,
    queries_one,
    queries_two,
    lengths,
):
    tokens, width = tokens_in.shape
    sub = cotangent.shape[1] // SUB
    steps = n_tp * sub
    units = steps - 1 + len(CHUNKS)
    nc = n_rep // 2
    rows, cols = master.shape
    decode = inputs_one.shape[0]
    share = decode // n_tp
    f32, bf16 = jnp.float32, jnp.bfloat16
    count = queries_one.shape[0]
    stacked = (count, KVH, 2 * QH // KVH, HD)
    early = (KVH, 2 * QH // KVH, count, HD)
    vmem = pl.BlockSpec(memory_space=pltpu.VMEM)
    hbm = pl.BlockSpec(memory_space=pl.ANY)
    dma = pltpu.SemaphoreType.DMA
    held = pl.pallas_call(
        functools.partial(sync_kernel, n_rep, n_tp, sub),
        out_shape=[pltpu.VMEM((rows, cols), f32)] * 3
        + [pltpu.VMEM((share, cols), f32)] * 2
        + [pltpu.VMEM(early, f32)] * 3
        + [pltpu.VMEM((count, 5 * HD), f32), pltpu.VMEM((2, *queries_one.shape), bf16)],
        in_specs=[hbm] * 12,
        out_specs=[vmem] * 10,
        scratch_shapes=[
            pltpu.VMEM((3, rows, cols), f32),
            pltpu.VMEM((3, SUB, rows), f32),
            pltpu.VMEM((3, SUB, rows), f32),
            pltpu.VMEM(cache_keys.shape, bf16),
            pltpu.VMEM(cache_values.shape, bf16),
            pltpu.VMEM((2, *inputs_one.shape), bf16),
            pltpu.SMEM(lengths.shape, jnp.int32),
            pltpu.VMEM((count, HD), f32),
            pltpu.VMEM(stacked, f32),
            pltpu.VMEM((tokens, width), bf16),
            pltpu.VMEM((tokens, sub * SUB), bf16),
            pltpu.VMEM((steps, SUB, tokens), bf16),
            pltpu.VMEM((steps, nc, SUB, rows), f32),
            pltpu.VMEM((steps, nc, SUB, rows), f32),
            pltpu.VMEM((steps, nc, SUB, rows), f32),
            pltpu.VMEM((steps, nc - 1, SUB, rows), bf16),
            pltpu.VMEM((steps, nc - 1, SUB, rows), bf16),
            pltpu.VMEM((steps - 1, n_rep, rows, SUB), bf16),
            pltpu.VMEM((n_rep, SUB, rows), bf16),
            pltpu.VMEM((steps, n_tp, 2, share, SUB), f32),
            pltpu.VMEM((n_tp - 1, steps, 2, share, SUB), f32),
            dma((12,)),
            dma((2,)),
            dma((steps,)),
            dma((len(CHUNKS),)),
            dma((8,)),
            dma((units,)),
            dma((units,)),
            dma((units,)),
            dma((steps,)),
            dma(()),
        ],
        compiler_params=pltpu.CompilerParams(
            collective_id=0, has_side_effects=True, vmem_limit_bytes=52 * 2**20
        ),
        name="synchronise",
    )(
        tokens_in,
        cotangent,
        master,
        m1,
        m2,
        cache_keys,
        cache_values,
        inputs_one,
        inputs_two,
        queries_one,
        queries_two,
        lengths,
    )
    wide = queries_one.shape
    return pl.pallas_call(
        finish_kernel,
        out_shape=[jax.ShapeDtypeStruct((rows, cols), f32)] * 3
        + [jax.ShapeDtypeStruct((share, cols), f32)] * 2
        + [jax.ShapeDtypeStruct(wide, f32)] * 2,
        in_specs=[vmem] * 10,
        out_specs=[hbm] * 7,
        scratch_shapes=[pltpu.VMEM((2, *wide), f32), dma((5,)), dma((2,))],
        compiler_params=pltpu.CompilerParams(vmem_limit_bytes=4 * 2**20),
        name="finish",
    )(*held)


def decode_table(lengths):
    shape = (lengths.shape[0], 5 * HD)
    column = lax.broadcasted_iota(jnp.int32, shape, 1)
    kind = column // HD
    lane = column % HD
    half_size = HD // 2
    inverse = rope_base ** (-2.0 * (lane % half_size).astype(jnp.float32) / HD)
    position = lengths + jnp.where(kind >= 3, 1, 0)
    angles = position.astype(jnp.float32) * inverse
    sine = jnp.where(lane < half_size, -jnp.sin(angles), jnp.sin(angles))
    allowed = jnp.where(lane < lengths, 1.0, 0.0)
    return jnp.where(kind == 0, allowed, jnp.where(kind % 2 == 1, jnp.cos(angles), sine))


def fits_kernel(n_rep, n_tp, cotangent, master, inputs_one, cache_keys):
    steps = n_tp * (cotangent.shape[1] // SUB)
    return (
        cache_keys.shape[1] == HD
        and steps > 6
        and cache_keys.shape[0] % 4 == 0
        and n_rep % 2 == 0
        and n_rep >= 4
        and n_tp >= 2
        and cotangent.shape[1] % SUB == 0
        and cotangent.shape[0] % 256 == 0
        and master.shape[1] % 128 == 0
        and inputs_one.shape[0] % (8 * n_tp) == 0
    )


def shards(
    n_rep,
    n_tp,
    tokens_in,
    cotangent,
    master,
    moment_one,
    moment_two,
    inputs_one,
    inputs_two,
    queries_one,
    queries_two,
    cache_keys,
    cache_values,
    lengths,
):
    row_count = cache_keys.shape[0]
    if fits_kernel(n_rep, n_tp, cotangent, master[0], inputs_one, cache_keys):
        *updated, both_one, both_two, attended_one, attended_two = synchronise(
            n_rep,
            n_tp,
            tokens_in,
            cotangent,
            master[0],
            moment_one[0],
            moment_two[0],
            cache_keys,
            cache_values,
            inputs_one,
            inputs_two,
            queries_one,
            queries_two,
            lengths,
        )
        return (
            *(array[None] for array in updated),
            both_one,
            both_two,
            attended_one,
            attended_two,
        )
    places = jnp.arange(cache_keys.shape[1], dtype=jnp.int32)
    cache_allowed = places[None, :] < lengths[:, None]
    fresh = jnp.zeros((row_count, 1), jnp.int32) == 0
    early_one = partial_scores(queries_one, cache_keys, cache_values, cache_allowed)
    early_two = partial_scores(queries_two, cache_keys, cache_values, cache_allowed)
    columns = lax.all_gather(cotangent, "tp", axis=1, tiled=True)
    gradient = lax.psum_scatter(
        lax.dot_general(
            tokens_in, columns, (((0,), (0,)), ((), ())), preferred_element_type=jnp.float32
        ),
        "rep",
        scatter_dimension=0,
        tiled=True,
    ).reshape(master.shape)
    moment_one_new = beta_one * moment_one + (1.0 - beta_one) * gradient
    moment_two_new = beta_two * moment_two + (1.0 - beta_two) * gradient * gradient
    corrected_one = moment_one_new / (1.0 - beta_one**step_count)
    corrected_two = moment_two_new / (1.0 - beta_two**step_count)
    master_new = master - learning_rate * (
        corrected_one / (jnp.sqrt(corrected_two) + epsilon) + weight_decay * master
    )
    weights = master_new[0].astype(jnp.bfloat16)
    shard_rows = lax.all_gather(weights, "rep", axis=0, tiled=True)
    partial_one = jnp.dot(inputs_one, shard_rows, preferred_element_type=jnp.float32)
    partial_two = jnp.dot(inputs_two, shard_rows, preferred_element_type=jnp.float32)
    both_one, both_two = (
        lax.psum_scatter(partial_one, "tp", scatter_dimension=0, tiled=True),
        lax.psum_scatter(partial_two, "tp", scatter_dimension=0, tiled=True),
    )
    key_width = both_one.shape[1] // 2
    keys_one = rotate(both_one[:, :key_width], lengths).astype(jnp.bfloat16)
    values_one = both_one[:, key_width:].astype(jnp.bfloat16)
    keys_two = rotate(both_two[:, :key_width], lengths + 1).astype(jnp.bfloat16)
    values_two = both_two[:, key_width:].astype(jnp.bfloat16)
    late_one = partial_scores(queries_one, keys_one[:, None], values_one[:, None], fresh)
    attended_one = finish(*combine(early_one, late_one))
    fresh_pair = jnp.concatenate([fresh, fresh], axis=1)
    late_two = partial_scores(
        queries_two,
        jnp.stack([keys_one, keys_two], axis=1),
        jnp.stack([values_one, values_two], axis=1),
        fresh_pair,
    )
    attended_two = finish(*combine(early_two, late_two))
    return (
        master_new,
        moment_one_new,
        moment_two_new,
        both_one,
        both_two,
        attended_one,
        attended_two,
    )


def solution(mesh):
    return jax.shard_map(
        functools.partial(shards, mesh.shape["rep"], mesh.shape["tp"]),
        mesh=mesh,
        in_specs=(
            P("rep", "tp"),
            P("rep", "tp"),
            P("tp", "rep", None),
            P("tp", "rep", None),
            P("tp", "rep", None),
            P("rep", "tp"),
            P("rep", "tp"),
            P(("rep", "tp"), None),
            P(("rep", "tp"), None),
            P(("rep", "tp"), None, None),
            P(("rep", "tp"), None, None),
            P(("rep", "tp")),
        ),
        out_specs=(
            P("tp", "rep", None),
            P("tp", "rep", None),
            P("tp", "rep", None),
            P(("rep", "tp"), None),
            P(("rep", "tp"), None),
            P(("rep", "tp"), None),
            P(("rep", "tp"), None),
        ),
        check_vma=False,
    )
```

```python
import functools

import jax
import jax.numpy as jnp
from jax import lax
from jax.experimental import pallas as pl
from jax.experimental.pallas import tpu as pltpu
from jax.sharding import PartitionSpec as P

KVH = 4
QH = 32
HD = 128


learning_rate = 0.001
beta_one = 0.9
beta_two = 0.99
epsilon = 1e-08
weight_decay = 0.1
step_count = 10.0
rope_base = 500000.0


def rotate(vectors, positions):
    row_count = vectors.shape[0]
    half_size = HD // 2
    inverse = rope_base ** (-2.0 * jnp.arange(half_size).astype(jnp.float32) / HD)
    angles = positions.astype(jnp.float32)[:, None, None] * inverse[None, None, :]
    shaped = vectors.reshape(row_count, -1, HD)
    first_half = shaped[..., :half_size]
    second_half = shaped[..., half_size:]
    cosine = jnp.cos(angles)
    sine = jnp.sin(angles)
    turned = jnp.concatenate(
        [first_half * cosine - second_half * sine, second_half * cosine + first_half * sine],
        axis=-1,
    )
    return turned.reshape(row_count, -1)


def partial_scores(queries, all_keys, all_values, allowed):
    row_count = all_keys.shape[0]
    places = all_keys.shape[1]
    group_size = QH // KVH
    shaped_queries = queries.astype(jnp.float32).reshape(row_count, KVH, group_size, HD)
    shaped_keys = all_keys.astype(jnp.float32).reshape(row_count, places, KVH, HD)
    shaped_values = all_values.astype(jnp.float32).reshape(row_count, places, KVH, HD)
    scores = jnp.einsum("rkgd,rpkd->rkgp", shaped_queries, shaped_keys) / HD**0.5
    scores = jnp.where(allowed[:, None, None, :], scores, -1e30)
    highest = jnp.max(scores, axis=-1)
    weights = lax.optimization_barrier(
        jnp.exp(scores - highest[..., None]).astype(jnp.bfloat16)
    ).astype(jnp.float32)
    return (
        highest,
        jnp.sum(weights, axis=-1),
        jnp.einsum("rkgp,rpkd->rkgd", weights, shaped_values),
    )


def finish(highest, denominator, numerator):
    row_count = numerator.shape[0]
    return (numerator / denominator[..., None]).reshape(row_count, -1)


def combine(earlier, later):
    highest = jnp.maximum(earlier[0], later[0])
    scale_early = jnp.exp(earlier[0] - highest)
    scale_late = jnp.exp(later[0] - highest)
    denominator = earlier[1] * scale_early + later[1] * scale_late
    numerator = earlier[2] * scale_early[..., None] + later[2] * scale_late[..., None]
    return (highest, denominator, numerator)


MESH = pl.DeviceIdType.MESH
SUB = 128
CHUNKS = (48, 32, 32, 16)


def arrival_orders(n_tp, sub):
    orders = []
    for t in range(n_tp):
        near = 0 if 2 * t < n_tp else n_tp - 1
        inner = t not in (0, n_tp - 1)
        pieces = []
        for b in range(n_tp):
            away = abs(b - t)
            rank = away
            if inner and away:
                rank = 2 * away + (0 if (b > t) == (near == 0) else 1) - 1
            pieces += [(rank, u, b) for u in range(sub)]
        pieces.sort()
        orders.append([b * sub + u for _, u, b in pieces])
    return orders


def piece_at(orders, t, s):
    found = 0
    for place, order in enumerate(orders):
        for step, piece in enumerate(order):
            if isinstance(s, int):
                if s == step:
                    found = found + jnp.where(t == place, piece, 0)
            else:
                found = found + jnp.where(jnp.logical_and(t == place, s == step), piece, 0)
    return found


def sync_kernel(
    n_rep,
    n_tp,
    sub,
    tok_hbm,
    cot_hbm,
    master_hbm,
    m1_hbm,
    m2_hbm,
    keys_hbm,
    values_hbm,
    in1_hbm,
    in2_hbm,
    q1_hbm,
    q2_hbm,
    lengths_hbm,
    master_out,
    m1_out,
    m2_out,
    p1_out,
    p2_out,
    early_max,
    early_sum,
    early_mix,
    table_ref,
    queries,
    state,
    state_t,
    new_t,
    keys,
    values,
    inputs,
    lengths_ref,
    mask,
    q_ref,
    tok,
    cot_raw,
    cot,
    a_send,
    a_keep,
    a_recv,
    b_send,
    b_recv,
    w_buf,
    w_fine,
    part,
    part_recv,
    load_sem,
    z_ss,
    z_rs,
    z_fs,
    send_sem,
    a_rs,
    b_rs,
    w_rs,
    v_rs,
    p_rs,
):
    nc = n_rep // 2
    steps = n_tp * sub
    coarse = steps - 1
    cw = SUB
    chunks = []
    for width in CHUNKS:
        chunks.append(slice(sum(CHUNKS[: len(chunks)]), sum(CHUNKS[: len(chunks)]) + width))
    whole = slice(0, cw)
    r = lax.axis_index("rep")
    t = lax.axis_index("tp")
    k = r // 2
    c = r % 2
    sibling = (2 * k + 1 - c, t)
    own_rows = master_hbm.shape[0]
    att_rows, groups, stacked, _ = q_ref.shape
    orders = arrival_orders(n_tp, sub)
    last = piece_at(orders, t, coarse)
    last_cols = pl.ds(pl.multiple_of(last * cw, cw), cw)

    def chip(j):
        return (k + j) % nc

    def source_chip(j):
        return (k + nc - j) % nc

    def send(source, target, send_sem_ref, recv_sem_ref, device):
        return pltpu.make_async_remote_copy(
            source, target, send_sem_ref, recv_sem_ref, device_id=device, device_id_type=MESH
        )

    load_cot = pltpu.make_async_copy(cot_hbm, cot_raw, load_sem.at[0])
    load_tok = pltpu.make_async_copy(tok_hbm, tok, load_sem.at[1])
    load_lengths = pltpu.make_async_copy(lengths_hbm, lengths_ref, load_sem.at[2])
    load_keys = pltpu.make_async_copy(keys_hbm, keys, load_sem.at[3])
    load_values = pltpu.make_async_copy(values_hbm, values, load_sem.at[4])
    load_queries = [
        pltpu.make_async_copy(source, queries.at[i], load_sem.at[5 + i])
        for i, source in enumerate((q1_hbm, q2_hbm))
    ]
    load_inputs = [
        pltpu.make_async_copy(source, inputs.at[i], load_sem.at[7 + i])
        for i, source in enumerate((in1_hbm, in2_hbm))
    ]
    load_state = [
        pltpu.make_async_copy(source, state.at[i], load_sem.at[9 + i])
        for i, source in enumerate((master_hbm, m1_hbm, m2_hbm))
    ]
    load_cot.start()
    barrier = pltpu.get_barrier_semaphore()
    for j in range(1, n_rep):
        pl.semaphore_signal(barrier, inc=1, device_id=((r + j) % n_rep, t), device_id_type=MESH)
    for j in range(1, n_tp):
        pl.semaphore_signal(barrier, inc=1, device_id=(r, (t + j) % n_tp), device_id_type=MESH)
    late_loads = [*load_queries, load_keys, load_values, *load_state, *load_inputs]
    load_cot.wait()
    for load in [load_lengths, *late_loads[:4], load_tok, *late_loads[4:]]:
        load.start()
    cot[t * sub] = cot_raw[:, 0:cw].T
    pl.semaphore_wait(barrier, (n_rep - 1) + (n_tp - 1))

    def neighbour(side):
        return jnp.minimum(t + 1, n_tp - 1) if side == 0 else jnp.maximum(t - 1, 0)

    def z_copy(g, side):
        return send(cot.at[g], cot.at[g], z_ss.at[side], z_rs.at[g], (r, neighbour(side)))

    def z_chunk(g, side, f):
        view = cot.at[g, chunks[f]]
        return send(view, view, z_ss.at[side], z_fs.at[f], (r, neighbour(side)))

    def z_goes(g, side):
        b = g // sub
        if side == 0:
            return jnp.logical_and(b <= t, t < n_tp - 1)
        return jnp.logical_and(b >= t, t > 0)

    def in_chunks(g, side):
        return g == piece_at(orders, neighbour(side), coarse)

    def z_forward(g):
        for side in (0, 1):
            @pl.when(jnp.logical_and(z_goes(g, side), jnp.logical_not(in_chunks(g, side))))
            def _():
                z_copy(g, side).start()

            @pl.when(jnp.logical_and(z_goes(g, side), in_chunks(g, side)))
            def _():
                for f in range(len(chunks)):
                    z_chunk(g, side, f).start()

    def z_forward_chunk(f):
        for side in (0, 1):
            @pl.when(jnp.logical_and(z_goes(last, side), in_chunks(last, side)))
            def _():
                z_chunk(last, side, f).start()

            if f == len(chunks) - 1:
                @pl.when(
                    jnp.logical_and(z_goes(last, side), jnp.logical_not(in_chunks(last, side)))
                )
                def _():
                    z_copy(last, side).start()

    z_forward(t * sub)
    for u in range(1, sub):
        cot[t * sub + u] = cot_raw[:, u * cw : (u + 1) * cw].T
        z_forward(t * sub + u)
    load_lengths.wait()
    row_ids = lax.broadcasted_iota(jnp.int32, (att_rows, HD), 0)
    length = jnp.zeros((att_rows, HD), jnp.int32)
    for row in range(att_rows):
        length = jnp.where(row_ids == row, lengths_ref[row], length)
    table_ref[...] = decode_table(length[:, 0:1])
    mask[...] = table_ref[:, 0:HD]
    for load in load_queries:
        load.wait()
    for i in range(2):
        for h in range(groups):
            for place in range(stacked // 2):
                at = (h * (stacked // 2) + place) * HD
                q_ref[:, h, i * (stacked // 2) + place, :] = queries[i, :, at : at + HD].astype(
                    jnp.float32
                )
    load_tok.wait()
    for load in late_loads[2:]:
        load.wait()

    def a_copy(s, cols, slot):
        return send(
            a_send.at[s, :, cols], a_recv.at[s, :, cols], send_sem.at[0], a_rs.at[slot], sibling
        )

    def b_copy(s, cols, slot, j):
        return send(
            b_send.at[s, j - 1, cols], b_recv.at[s, j - 1, cols], send_sem.at[1], b_rs.at[slot],
            (2 * chip(j) + c, t),
        )

    def w_copy(s, j):
        view = w_buf.at[s, r]
        return send(view, view, send_sem.at[2], w_rs.at[s], (2 * chip(j) + c, t))

    def w_chunk(f, j):
        view = w_fine.at[r, chunks[f]]
        return send(view, view, send_sem.at[3], w_rs.at[coarse + f], (2 * chip(j) + c, t))

    def v_chunk(f, j):
        view = w_fine.at[2 * source_chip(j) + c, chunks[f]]
        return send(view, view, send_sem.at[6], v_rs.at[coarse], sibling)

    def w_direct(j):
        view = w_fine.at[r, chunks[-1]]
        return send(
            view, view, send_sem.at[7], w_rs.at[coarse + len(chunks) - 1], ((r + j) % n_rep, t)
        )

    def v_copy(s, j):
        view = w_buf.at[s, 2 * source_chip(j) + c]
        return send(view, view, send_sem.at[4], v_rs.at[s], sibling)

    def wait_recv(ref, sem):
        send(ref, ref, send_sem.at[0], sem, sibling).wait_recv()

    def wait_send(ref, sem):
        send(ref, ref, sem, a_rs.at[0], sibling).wait_send()

    def terms(g, s, cols, slot):
        def term(owner):
            at = pl.multiple_of(owner * own_rows, own_rows)
            return jnp.dot(
                cot[g, cols], tok[:, pl.ds(at, own_rows)], preferred_element_type=jnp.float32
            )

        for q in range(nc):
            a_send[s, q, cols] = term(2 * q + 1 - c)
        a_copy(s, cols, slot).start()
        for q in range(nc):
            a_keep[s, q, cols] = term(2 * q + c)

    def gradient_stage(s):
        g = piece_at(orders, t, s)

        @pl.when(g // sub != t)
        def _():
            z_copy(g, 0).wait_recv()
            z_forward(g)

        terms(g, s, whole, s)

    def gradient_chunk(f):
        z_chunk(last, 0, f).wait_recv()
        z_forward_chunk(f)
        terms(last, coarse, chunks[f], coarse + f)

    def chip_sum_stage(s, cols, slot):
        a_copy(s, cols, slot).wait_recv()
        for j in range(1, nc):
            q = chip(j)
            b_send[s, j - 1, cols] = (a_keep[s, q, cols] + a_recv[s, q, cols]).astype(
                jnp.bfloat16
            )
            b_copy(s, cols, slot, j).start()

    def summed(s, cols, slot):
        total = a_keep[s, k, cols] + a_recv[s, k, cols]
        wait_recv(b_recv.at[s, :, cols], b_rs.at[slot])
        for j in range(1, nc):
            total = total + b_recv[s, j - 1, cols].astype(jnp.float32)
        return total

    def adam(master, m1, m2, gradient):
        moment_one_new = beta_one * m1 + (1.0 - beta_one) * gradient
        moment_two_new = beta_two * m2 + (1.0 - beta_two) * gradient * gradient
        corrected_one = moment_one_new / (1.0 - beta_one**step_count)
        corrected_two = moment_two_new / (1.0 - beta_two**step_count)
        master_new = master - learning_rate * (
            corrected_one / (jnp.sqrt(corrected_two) + epsilon) + weight_decay * master
        )
        return master_new, moment_one_new, moment_two_new

    outs = (master_out, m1_out, m2_out)

    def update_stage(s):
        cols = pl.ds(pl.multiple_of(piece_at(orders, t, s) * cw, cw), cw)
        updated = adam(*(state[i, :, cols] for i in range(3)), summed(s, whole, s).T)
        w_buf[s, r] = updated[0].astype(jnp.bfloat16)
        for j in range(1, nc):
            w_copy(s, j).start()
        v_copy(s, 0).start()
        for out, value in zip(outs, updated):
            out[:, cols] = value

    def update_chunk(f):
        cols = chunks[f]
        updated = adam(*(state_t[i, cols] for i in range(3)), summed(coarse, cols, coarse + f))
        w_fine[r, cols] = updated[0].astype(jnp.bfloat16)
        if f == len(chunks) - 1:
            for j in range(1, n_rep):
                w_direct(j).start()
        else:
            for j in range(1, nc):
                w_chunk(f, j).start()
            v_chunk(f, 0).start()
        for i, value in enumerate(updated):
            new_t[i, cols] = value

    def share_stage(s):
        wait_recv(w_buf.at[s, 0 : nc - 1], w_rs.at[s])
        for j in range(1, nc):
            v_copy(s, j).start()

    def share_chunk(f):
        wait_recv(w_fine.at[0 : nc - 1, chunks[f]], w_rs.at[coarse + f])
        for j in range(1, nc):
            v_chunk(f, j).start()

    at_end = jnp.logical_or(t == 0, t == n_tp - 1)

    def to_end(j):
        to = (t + j) % n_tp
        return jnp.logical_or(to == 0, to == n_tp - 1)

    def p_copy(g, j):
        to = (t + j) % n_tp
        return send(part.at[g, to], part_recv.at[j - 1, g], send_sem.at[5], p_rs, (r, to))

    def decoded(g, product):
        rows = product.shape[0] // 2
        for i in range(2):
            part[g, :, i] = product[i * rows : (i + 1) * rows].reshape(n_tp, rows // n_tp, cw)

    both = inputs.shape[0] * inputs.shape[1]

    def decode_stage(s):
        wait_recv(w_buf.at[s, 0:nc], v_rs.at[s])
        g = piece_at(orders, t, s)
        block = w_buf[s].reshape(n_rep * own_rows, cw)
        decoded(
            g,
            jnp.dot(
                inputs[...].reshape(both, -1), block, preferred_element_type=jnp.float32
            ),
        )
        for j in range(1, n_tp):
            @pl.when(jnp.logical_not(to_end(j)))
            def _():
                p_copy(g, j).start()

    def decode_last():
        wait_recv(w_fine.at[0 : n_rep - 1, chunks[-1]], w_rs.at[coarse + len(chunks) - 1])
        wait_recv(w_fine.at[0:nc, 0 : chunks[-1].start], v_rs.at[coarse])
        product = 0.0
        for owner in range(n_rep):
            rows = inputs[:, :, owner * own_rows : (owner + 1) * own_rows]
            product = product + lax.dot_general(
                rows.reshape(both, own_rows),
                w_fine[owner],
                (((1,), (1,)), ((), ())),
                preferred_element_type=jnp.float32,
            )
        decoded(last, product)

        @pl.when(at_end)
        def _():
            for far in (True, False):
                for j in range(1, n_tp):
                    @pl.when(to_end(j) == far)
                    def _():
                        p_copy(last, j).start()

        @pl.when(jnp.logical_not(at_end))
        def _():
            for j in range(1, n_tp):
                @pl.when(jnp.logical_not(to_end(j)))
                def _():
                    p_copy(last, j).start()

    def late_stage(s):
        g = piece_at(orders, t, s)
        for j in range(1, n_tp):
            @pl.when(to_end(j))
            def _():
                p_copy(g, j).start()

    cache_steps = min(4, coarse)

    def cache_stage(s):
        per_step = att_rows // cache_steps

        @pl.loop(0, per_step)
        def _(i):
            row = s * per_step + i
            allowed = mask[pl.ds(row, 1), :] > 0.0
            for h in range(groups):
                head = slice(h * HD, (h + 1) * HD)
                scores = lax.dot_general(
                    q_ref[row, h].astype(jnp.bfloat16),
                    keys[row, :, head],
                    (((1,), (1,)), ((), ())),
                    preferred_element_type=jnp.float32,
                )
                scores = jnp.where(allowed, scores / HD**0.5, -1e30)
                highest = jnp.max(scores, axis=-1, keepdims=True)
                weights = jnp.exp(scores - highest).astype(jnp.bfloat16)
                total = jnp.sum(weights.astype(jnp.float32), axis=-1, keepdims=True)
                mix = jnp.dot(weights, values[row, :, head], preferred_element_type=jnp.float32)
                for ref, value in ((early_max, highest), (early_sum, total), (early_mix, mix)):
                    value = jnp.broadcast_to(value, (stacked, HD))
                    ref[h, :, pl.ds(row, 1), :] = value.reshape(stacked, 1, HD)

    def turn_state():
        for i in range(3):
            state_t[i] = state[i, :, last_cols].T

    def sum_stage(s):
        chip_sum_stage(s, whole, s)

    def ahead(s):
        return jnp.logical_and(at_end, s >= cache_steps)

    def never(s):
        return False

    stages = (
        (sum_stage, 1, ahead),
        (update_stage, 2, lambda s: jnp.logical_and(at_end, s >= cache_steps - 1)),
        (share_stage, 3, never),
        (decode_stage, 4, never),
    )
    cache_now = jnp.where(at_end, cache_steps, 1)

    @pl.loop(0, coarse)
    def _(it):
        for stage, lag, skip in stages:
            @pl.when(jnp.logical_and(it >= lag, jnp.logical_not(skip(it - lag))))
            def _():
                stage(it - lag)

        @pl.when(it < cache_now)
        def _():
            cache_stage(it)

        gradient_stage(it)

        @pl.when(jnp.logical_and(ahead(it), it < coarse - 1))
        def _():
            sum_stage(it)

            @pl.when(it == cache_steps)
            def _():
                update_stage(it - 1)

            update_stage(it)

        @pl.when(it == cache_steps)
        def _():
            turn_state()

    sum_stage(coarse - 1)

    @pl.when(jnp.logical_not(at_end))
    def _():
        update_stage(coarse - 2)

    share_stage(coarse - 3)
    decode_stage(coarse - 4)

    @pl.when(jnp.logical_not(at_end))
    def _():
        cache_stage(1)

    final = len(chunks) - 1
    for f, cols in enumerate(chunks):
        gradient_chunk(f)
        chip_sum_stage(coarse, cols, coarse + f)
        if f == 0:
            share_stage(coarse - 2)
            if final > 1:
                update_stage(coarse - 1)
        if f > 1:
            update_chunk(f - 2)
    if final < 2:
        update_stage(coarse - 1)
    if final > 0:
        update_chunk(final - 1)
    for s in range(coarse - 3, coarse - 1):
        decode_stage(s)
    share_stage(coarse - 1)

    @pl.when(at_end)
    def _():
        @pl.loop(0, coarse - 1)
        def _(s):
            late_stage(s)

    for f in range(final - 2):
        share_chunk(f)
    decode_stage(coarse - 1)

    @pl.when(at_end)
    def _():
        late_stage(coarse - 1)

    update_chunk(final)
    for f in range(max(final - 2, 0), final - 1):
        share_chunk(f)
    if final > 0:
        share_chunk(final - 1)
    for i, out in enumerate(outs):
        out[:, last_cols] = new_t[i].T
    decode_last()

    for place in range(n_tp):
        @pl.when(t == place)
        def _():
            if place < n_tp - 1:
                wait_send(cot.at[0 : (place + 1) * sub], z_ss.at[0])
            if place > 0:
                wait_send(cot.at[0 : (n_tp - place) * sub], z_ss.at[1])

    @pl.when(jnp.logical_not(at_end))
    def _():
        cache_stage(2)

        @pl.loop(0, steps)
        def _(s):
            late_stage(s)

        @pl.loop(3, cache_steps)
        def _(s):
            cache_stage(s)

    wait_send(a_send, send_sem.at[0])
    wait_send(b_send, send_sem.at[1])
    wait_send(w_buf.at[:, 0 : nc - 1], send_sem.at[2])
    wait_send(w_fine.at[0 : nc - 1, 0 : chunks[-1].start], send_sem.at[3])
    wait_send(w_fine.at[0:nc, 0 : chunks[-1].start], send_sem.at[6])
    wait_send(w_fine.at[0 : n_rep - 1, chunks[-1]], send_sem.at[7])
    wait_send(w_buf.at[:, 0:nc], send_sem.at[4])
    wait_recv(part_recv, p_rs)
    for g in range(steps):
        for i, out in enumerate((p1_out, p2_out)):
            total = part[g, t, i]
            for j in range(1, n_tp):
                total = total + part_recv[j - 1, g, i]
            out[:, g * cw : (g + 1) * cw] = total
    wait_send(part.at[:, 0 : n_tp - 1], send_sem.at[5])


def finish_kernel(
    master,
    m1,
    m2,
    p1,
    p2,
    early_max,
    early_sum,
    early_mix,
    table,
    queries,
    master_out,
    m1_out,
    m2_out,
    p1_out,
    p2_out,
    att1_out,
    att2_out,
    att,
    sems,
    att_sems,
):
    stores = [
        pltpu.make_async_copy(source, target, sems.at[i])
        for i, (source, target) in enumerate(
            ((master, master_out), (m1, m1_out), (m2, m2_out), (p1, p1_out), (p2, p2_out))
        )
    ]
    for store in stores:
        store.start()
    groups, stacked = early_max.shape[:2]
    half = stacked // 2
    keys, values = [], []
    for i, ref in enumerate((p1, p2)):
        total = ref[...]
        cosine = table[:, (1 + 2 * i) * HD : (2 + 2 * i) * HD]
        sine = table[:, (2 + 2 * i) * HD : (3 + 2 * i) * HD]
        for h in range(groups):
            head = total[:, h * HD : (h + 1) * HD]
            turned = head * cosine + pltpu.roll(head, HD // 2, 1) * sine
            value = total[:, (groups + h) * HD : (groups + h + 1) * HD]
            keys.append(turned.astype(jnp.bfloat16).astype(jnp.float32))
            values.append(value.astype(jnp.bfloat16).astype(jnp.float32))
    for i, out in enumerate((att1_out, att2_out)):
        for h in range(groups):
            for place in range(half):
                at = slice((h * half + place) * HD, (h * half + place + 1) * HD)
                query = queries[i, :, at].astype(jnp.float32)
                scores = [
                    jnp.sum(query * keys[n * groups + h], axis=-1, keepdims=True) / HD**0.5
                    for n in range(i + 1)
                ]
                before = early_max[h, i * half + place]
                highest = before
                for score in scores:
                    highest = jnp.maximum(highest, score)
                scale = jnp.exp(before - highest)
                below = early_sum[h, i * half + place] * scale
                above = early_mix[h, i * half + place] * scale
                for n, score in enumerate(scores):
                    weight = jnp.exp(score - highest).astype(jnp.bfloat16).astype(jnp.float32)
                    below = below + weight
                    above = above + weight * values[n * groups + h]
                att[i, :, at] = above / below
        store = pltpu.make_async_copy(att.at[i], out, att_sems.at[i])
        store.start()
        stores.append(store)
    for store in stores:
        store.wait()


def synchronise(
    n_rep,
    n_tp,
    tokens_in,
    cotangent,
    master,
    m1,
    m2,
    cache_keys,
    cache_values,
    inputs_one,
    inputs_two,
    queries_one,
    queries_two,
    lengths,
):
    tokens, width = tokens_in.shape
    sub = cotangent.shape[1] // SUB
    steps = n_tp * sub
    units = steps - 1 + len(CHUNKS)
    nc = n_rep // 2
    rows, cols = master.shape
    decode = inputs_one.shape[0]
    share = decode // n_tp
    f32, bf16 = jnp.float32, jnp.bfloat16
    count = queries_one.shape[0]
    stacked = (count, KVH, 2 * QH // KVH, HD)
    early = (KVH, 2 * QH // KVH, count, HD)
    vmem = pl.BlockSpec(memory_space=pltpu.VMEM)
    hbm = pl.BlockSpec(memory_space=pl.ANY)
    dma = pltpu.SemaphoreType.DMA
    held = pl.pallas_call(
        functools.partial(sync_kernel, n_rep, n_tp, sub),
        out_shape=[pltpu.VMEM((rows, cols), f32)] * 3
        + [pltpu.VMEM((share, cols), f32)] * 2
        + [pltpu.VMEM(early, f32)] * 3
        + [pltpu.VMEM((count, 5 * HD), f32), pltpu.VMEM((2, *queries_one.shape), bf16)],
        in_specs=[hbm] * 12,
        out_specs=[vmem] * 10,
        scratch_shapes=[
            pltpu.VMEM((3, rows, cols), f32),
            pltpu.VMEM((3, SUB, rows), f32),
            pltpu.VMEM((3, SUB, rows), f32),
            pltpu.VMEM(cache_keys.shape, bf16),
            pltpu.VMEM(cache_values.shape, bf16),
            pltpu.VMEM((2, *inputs_one.shape), bf16),
            pltpu.SMEM(lengths.shape, jnp.int32),
            pltpu.VMEM((count, HD), f32),
            pltpu.VMEM(stacked, f32),
            pltpu.VMEM((tokens, width), bf16),
            pltpu.VMEM((tokens, sub * SUB), bf16),
            pltpu.VMEM((steps, SUB, tokens), bf16),
            pltpu.VMEM((steps, nc, SUB, rows), f32),
            pltpu.VMEM((steps, nc, SUB, rows), f32),
            pltpu.VMEM((steps, nc, SUB, rows), f32),
            pltpu.VMEM((steps, nc - 1, SUB, rows), bf16),
            pltpu.VMEM((steps, nc - 1, SUB, rows), bf16),
            pltpu.VMEM((steps - 1, n_rep, rows, SUB), bf16),
            pltpu.VMEM((n_rep, SUB, rows), bf16),
            pltpu.VMEM((steps, n_tp, 2, share, SUB), f32),
            pltpu.VMEM((n_tp - 1, steps, 2, share, SUB), f32),
            dma((12,)),
            dma((2,)),
            dma((steps,)),
            dma((len(CHUNKS),)),
            dma((8,)),
            dma((units,)),
            dma((units,)),
            dma((units,)),
            dma((steps,)),
            dma(()),
        ],
        compiler_params=pltpu.CompilerParams(
            collective_id=0, has_side_effects=True, vmem_limit_bytes=52 * 2**20
        ),
        name="synchronise",
    )(
        tokens_in,
        cotangent,
        master,
        m1,
        m2,
        cache_keys,
        cache_values,
        inputs_one,
        inputs_two,
        queries_one,
        queries_two,
        lengths,
    )
    wide = queries_one.shape
    return pl.pallas_call(
        finish_kernel,
        out_shape=[jax.ShapeDtypeStruct((rows, cols), f32)] * 3
        + [jax.ShapeDtypeStruct((share, cols), f32)] * 2
        + [jax.ShapeDtypeStruct(wide, f32)] * 2,
        in_specs=[vmem] * 10,
        out_specs=[hbm] * 7,
        scratch_shapes=[pltpu.VMEM((2, *wide), f32), dma((5,)), dma((2,))],
        compiler_params=pltpu.CompilerParams(vmem_limit_bytes=4 * 2**20),
        name="finish",
    )(*held)


def decode_table(lengths):
    shape = (lengths.shape[0], 5 * HD)
    column = lax.broadcasted_iota(jnp.int32, shape, 1)
    kind = column // HD
    lane = column % HD
    half_size = HD // 2
    inverse = rope_base ** (-2.0 * (lane % half_size).astype(jnp.float32) / HD)
    position = lengths + jnp.where(kind >= 3, 1, 0)
    angles = position.astype(jnp.float32) * inverse
    sine = jnp.where(lane < half_size, -jnp.sin(angles), jnp.sin(angles))
    allowed = jnp.where(lane < lengths, 1.0, 0.0)
    return jnp.where(kind == 0, allowed, jnp.where(kind % 2 == 1, jnp.cos(angles), sine))


def fits_kernel(n_rep, n_tp, cotangent, master, inputs_one, cache_keys):
    steps = n_tp * (cotangent.shape[1] // SUB)
    return (
        cache_keys.shape[1] == HD
        and steps > 6
        and cache_keys.shape[0] % 4 == 0
        and n_rep % 2 == 0
        and n_rep >= 4
        and n_tp >= 2
        and cotangent.shape[1] % SUB == 0
        and cotangent.shape[0] % 256 == 0
        and master.shape[1] % 128 == 0
        and inputs_one.shape[0] % (8 * n_tp) == 0
    )


def shards(
    n_rep,
    n_tp,
    tokens_in,
    cotangent,
    master,
    moment_one,
    moment_two,
    inputs_one,
    inputs_two,
    queries_one,
    queries_two,
    cache_keys,
    cache_values,
    lengths,
):
    row_count = cache_keys.shape[0]
    if fits_kernel(n_rep, n_tp, cotangent, master[0], inputs_one, cache_keys):
        *updated, both_one, both_two, attended_one, attended_two = synchronise(
            n_rep,
            n_tp,
            tokens_in,
            cotangent,
            master[0],
            moment_one[0],
            moment_two[0],
            cache_keys,
            cache_values,
            inputs_one,
            inputs_two,
            queries_one,
            queries_two,
            lengths,
        )
        return (
            *(array[None] for array in updated),
            both_one,
            both_two,
            attended_one,
            attended_two,
        )
    places = jnp.arange(cache_keys.shape[1], dtype=jnp.int32)
    cache_allowed = places[None, :] < lengths[:, None]
    fresh = jnp.zeros((row_count, 1), jnp.int32) == 0
    early_one = partial_scores(queries_one, cache_keys, cache_values, cache_allowed)
    early_two = partial_scores(queries_two, cache_keys, cache_values, cache_allowed)
    columns = lax.all_gather(cotangent, "tp", axis=1, tiled=True)
    gradient = lax.psum_scatter(
        lax.dot_general(
            tokens_in, columns, (((0,), (0,)), ((), ())), preferred_element_type=jnp.float32
        ),
        "rep",
        scatter_dimension=0,
        tiled=True,
    ).reshape(master.shape)
    moment_one_new = beta_one * moment_one + (1.0 - beta_one) * gradient
    moment_two_new = beta_two * moment_two + (1.0 - beta_two) * gradient * gradient
    corrected_one = moment_one_new / (1.0 - beta_one**step_count)
    corrected_two = moment_two_new / (1.0 - beta_two**step_count)
    master_new = master - learning_rate * (
        corrected_one / (jnp.sqrt(corrected_two) + epsilon) + weight_decay * master
    )
    weights = master_new[0].astype(jnp.bfloat16)
    shard_rows = lax.all_gather(weights, "rep", axis=0, tiled=True)
    partial_one = jnp.dot(inputs_one, shard_rows, preferred_element_type=jnp.float32)
    partial_two = jnp.dot(inputs_two, shard_rows, preferred_element_type=jnp.float32)
    both_one, both_two = (
        lax.psum_scatter(partial_one, "tp", scatter_dimension=0, tiled=True),
        lax.psum_scatter(partial_two, "tp", scatter_dimension=0, tiled=True),
    )
    key_width = both_one.shape[1] // 2
    keys_one = rotate(both_one[:, :key_width], lengths).astype(jnp.bfloat16)
    values_one = both_one[:, key_width:].astype(jnp.bfloat16)
    keys_two = rotate(both_two[:, :key_width], lengths + 1).astype(jnp.bfloat16)
    values_two = both_two[:, key_width:].astype(jnp.bfloat16)
    late_one = partial_scores(queries_one, keys_one[:, None], values_one[:, None], fresh)
    attended_one = finish(*combine(early_one, late_one))
    fresh_pair = jnp.concatenate([fresh, fresh], axis=1)
    late_two = partial_scores(
        queries_two,
        jnp.stack([keys_one, keys_two], axis=1),
        jnp.stack([values_one, values_two], axis=1),
        fresh_pair,
    )
    attended_two = finish(*combine(early_two, late_two))
    return (
        master_new,
        moment_one_new,
        moment_two_new,
        both_one,
        both_two,
        attended_one,
        attended_two,
    )


def solution(mesh):
    return jax.shard_map(
        functools.partial(shards, mesh.shape["rep"], mesh.shape["tp"]),
        mesh=mesh,
        in_specs=(
            P("rep", "tp"),
            P("rep", "tp"),
            P("tp", "rep", None),
            P("tp", "rep", None),
            P("tp", "rep", None),
            P("rep", "tp"),
            P("rep", "tp"),
            P(("rep", "tp"), None),
            P(("rep", "tp"), None),
            P(("rep", "tp"), None, None),
            P(("rep", "tp"), None, None),
            P(("rep", "tp")),
        ),
        out_specs=(
            P("tp", "rep", None),
            P("tp", "rep", None),
            P("tp", "rep", None),
            P(("rep", "tp"), None),
            P(("rep", "tp"), None),
            P(("rep", "tp"), None),
            P(("rep", "tp"), None),
        ),
        check_vma=False,
    )
```

```python
import functools

import jax
import jax.numpy as jnp
from jax import lax
from jax.experimental import pallas as pl
from jax.experimental.pallas import tpu as pltpu
from jax.sharding import PartitionSpec as P

KVH = 4
QH = 32
HD = 128


learning_rate = 0.001
beta_one = 0.9
beta_two = 0.99
epsilon = 1e-08
weight_decay = 0.1
step_count = 10.0
rope_base = 500000.0


def rotate(vectors, positions):
    row_count = vectors.shape[0]
    half_size = HD // 2
    inverse = rope_base ** (-2.0 * jnp.arange(half_size).astype(jnp.float32) / HD)
    angles = positions.astype(jnp.float32)[:, None, None] * inverse[None, None, :]
    shaped = vectors.reshape(row_count, -1, HD)
    first_half = shaped[..., :half_size]
    second_half = shaped[..., half_size:]
    cosine = jnp.cos(angles)
    sine = jnp.sin(angles)
    turned = jnp.concatenate(
        [first_half * cosine - second_half * sine, second_half * cosine + first_half * sine],
        axis=-1,
    )
    return turned.reshape(row_count, -1)


def partial_scores(queries, all_keys, all_values, allowed):
    row_count = all_keys.shape[0]
    places = all_keys.shape[1]
    group_size = QH // KVH
    shaped_queries = queries.astype(jnp.float32).reshape(row_count, KVH, group_size, HD)
    shaped_keys = all_keys.astype(jnp.float32).reshape(row_count, places, KVH, HD)
    shaped_values = all_values.astype(jnp.float32).reshape(row_count, places, KVH, HD)
    scores = jnp.einsum("rkgd,rpkd->rkgp", shaped_queries, shaped_keys) / HD**0.5
    scores = jnp.where(allowed[:, None, None, :], scores, -1e30)
    highest = jnp.max(scores, axis=-1)
    weights = lax.optimization_barrier(
        jnp.exp(scores - highest[..., None]).astype(jnp.bfloat16)
    ).astype(jnp.float32)
    return (
        highest,
        jnp.sum(weights, axis=-1),
        jnp.einsum("rkgp,rpkd->rkgd", weights, shaped_values),
    )


def finish(highest, denominator, numerator):
    row_count = numerator.shape[0]
    return (numerator / denominator[..., None]).reshape(row_count, -1)


def combine(earlier, later):
    highest = jnp.maximum(earlier[0], later[0])
    scale_early = jnp.exp(earlier[0] - highest)
    scale_late = jnp.exp(later[0] - highest)
    denominator = earlier[1] * scale_early + later[1] * scale_late
    numerator = earlier[2] * scale_early[..., None] + later[2] * scale_late[..., None]
    return (highest, denominator, numerator)


MESH = pl.DeviceIdType.MESH
SUB = 128
CHUNKS = (48, 32, 32, 16)
DIRECT = 2


def arrival_orders(n_tp, sub):
    orders = []
    for t in range(n_tp):
        near = 0 if 2 * t < n_tp else n_tp - 1
        inner = t not in (0, n_tp - 1)
        pieces = []
        for b in range(n_tp):
            away = abs(b - t)
            rank = away
            if inner and away:
                rank = 2 * away + (0 if (b > t) == (near == 0) else 1) - 1
            pieces += [(rank, u, b) for u in range(sub)]
        pieces.sort()
        orders.append([b * sub + u for _, u, b in pieces])
    return orders


def piece_at(orders, t, s):
    found = 0
    for place, order in enumerate(orders):
        for step, piece in enumerate(order):
            if isinstance(s, int):
                if s == step:
                    found = found + jnp.where(t == place, piece, 0)
            else:
                found = found + jnp.where(jnp.logical_and(t == place, s == step), piece, 0)
    return found


def sync_kernel(
    n_rep,
    n_tp,
    sub,
    tok_hbm,
    cot_hbm,
    master_hbm,
    m1_hbm,
    m2_hbm,
    keys_hbm,
    values_hbm,
    in1_hbm,
    in2_hbm,
    q1_hbm,
    q2_hbm,
    lengths_hbm,
    master_out,
    m1_out,
    m2_out,
    p1_out,
    p2_out,
    early_max,
    early_sum,
    early_mix,
    table_ref,
    queries,
    state,
    state_t,
    new_t,
    keys,
    values,
    inputs,
    lengths_ref,
    mask,
    q_ref,
    tok,
    cot_raw,
    cot,
    a_send,
    a_keep,
    a_recv,
    b_send,
    b_recv,
    w_buf,
    w_fine,
    d_send,
    d_recv,
    d_own,
    part,
    part_recv,
    load_sem,
    z_ss,
    z_rs,
    z_fs,
    send_sem,
    d_rs,
    a_rs,
    b_rs,
    w_rs,
    v_rs,
    p_rs,
):
    nc = n_rep // 2
    steps = n_tp * sub
    coarse = steps - 1
    cw = SUB
    chunks = []
    for width in CHUNKS:
        chunks.append(slice(sum(CHUNKS[: len(chunks)]), sum(CHUNKS[: len(chunks)]) + width))
    whole = slice(0, cw)
    final = len(chunks) - 1
    direct = len(chunks) - DIRECT
    shared_cols = slice(0, chunks[direct].start)
    direct_cols = slice(chunks[direct].start, cw)
    summed_cols = slice(0, chunks[final].start)
    r = lax.axis_index("rep")
    t = lax.axis_index("tp")
    k = r // 2
    c = r % 2
    sibling = (2 * k + 1 - c, t)
    own_rows = master_hbm.shape[0]
    att_rows, groups, stacked, _ = q_ref.shape
    orders = arrival_orders(n_tp, sub)
    last = piece_at(orders, t, coarse)
    last_cols = pl.ds(pl.multiple_of(last * cw, cw), cw)

    def chip(j):
        return (k + j) % nc

    def source_chip(j):
        return (k + nc - j) % nc

    def send(source, target, send_sem_ref, recv_sem_ref, device):
        return pltpu.make_async_remote_copy(
            source, target, send_sem_ref, recv_sem_ref, device_id=device, device_id_type=MESH
        )

    load_cot = pltpu.make_async_copy(cot_hbm, cot_raw, load_sem.at[0])
    load_tok = pltpu.make_async_copy(tok_hbm, tok, load_sem.at[1])
    load_lengths = pltpu.make_async_copy(lengths_hbm, lengths_ref, load_sem.at[2])
    load_keys = pltpu.make_async_copy(keys_hbm, keys, load_sem.at[3])
    load_values = pltpu.make_async_copy(values_hbm, values, load_sem.at[4])
    load_queries = [
        pltpu.make_async_copy(source, queries.at[i], load_sem.at[5 + i])
        for i, source in enumerate((q1_hbm, q2_hbm))
    ]
    load_inputs = [
        pltpu.make_async_copy(source, inputs.at[i], load_sem.at[7 + i])
        for i, source in enumerate((in1_hbm, in2_hbm))
    ]
    load_state = [
        pltpu.make_async_copy(source, state.at[i], load_sem.at[9 + i])
        for i, source in enumerate((master_hbm, m1_hbm, m2_hbm))
    ]
    load_cot.start()
    barrier = pltpu.get_barrier_semaphore()
    for j in range(1, n_rep):
        pl.semaphore_signal(barrier, inc=1, device_id=((r + j) % n_rep, t), device_id_type=MESH)
    for j in range(1, n_tp):
        pl.semaphore_signal(barrier, inc=1, device_id=(r, (t + j) % n_tp), device_id_type=MESH)
    late_loads = [*load_queries, load_keys, load_values, *load_state, *load_inputs]
    load_cot.wait()
    for load in [load_lengths, *late_loads[:4], load_tok, *late_loads[4:]]:
        load.start()
    cot[t * sub] = cot_raw[:, 0:cw].T
    pl.semaphore_wait(barrier, (n_rep - 1) + (n_tp - 1))

    def neighbour(side):
        return jnp.minimum(t + 1, n_tp - 1) if side == 0 else jnp.maximum(t - 1, 0)

    def z_copy(g, side):
        return send(cot.at[g], cot.at[g], z_ss.at[side], z_rs.at[g], (r, neighbour(side)))

    def z_chunk(g, side, f):
        view = cot.at[g, chunks[f]]
        return send(view, view, z_ss.at[side], z_fs.at[f], (r, neighbour(side)))

    def z_goes(g, side):
        b = g // sub
        if side == 0:
            return jnp.logical_and(b <= t, t < n_tp - 1)
        return jnp.logical_and(b >= t, t > 0)

    def in_chunks(g, side):
        return g == piece_at(orders, neighbour(side), coarse)

    def z_forward(g):
        for side in (0, 1):
            @pl.when(jnp.logical_and(z_goes(g, side), jnp.logical_not(in_chunks(g, side))))
            def _():
                z_copy(g, side).start()

            @pl.when(jnp.logical_and(z_goes(g, side), in_chunks(g, side)))
            def _():
                for f in range(len(chunks)):
                    z_chunk(g, side, f).start()

    def z_forward_chunk(f):
        for side in (0, 1):
            @pl.when(jnp.logical_and(z_goes(last, side), in_chunks(last, side)))
            def _():
                z_chunk(last, side, f).start()

            if f == len(chunks) - 1:
                @pl.when(
                    jnp.logical_and(z_goes(last, side), jnp.logical_not(in_chunks(last, side)))
                )
                def _():
                    z_copy(last, side).start()

    z_forward(t * sub)
    for u in range(1, sub):
        cot[t * sub + u] = cot_raw[:, u * cw : (u + 1) * cw].T
        z_forward(t * sub + u)
    load_lengths.wait()
    row_ids = lax.broadcasted_iota(jnp.int32, (att_rows, HD), 0)
    length = jnp.zeros((att_rows, HD), jnp.int32)
    for row in range(att_rows):
        length = jnp.where(row_ids == row, lengths_ref[row], length)
    table_ref[...] = decode_table(length[:, 0:1])
    mask[...] = table_ref[:, 0:HD]
    for load in load_queries:
        load.wait()
    for i in range(2):
        for h in range(groups):
            for place in range(stacked // 2):
                at = (h * (stacked // 2) + place) * HD
                q_ref[:, h, i * (stacked // 2) + place, :] = queries[i, :, at : at + HD].astype(
                    jnp.float32
                )
    load_tok.wait()
    for load in late_loads[2:]:
        load.wait()

    def kind(slot, sem):
        return send_sem.at[sem + (8 if isinstance(slot, int) and slot >= coarse else 0)]

    def d_copy(at, owner, slot):
        return send(d_send.at[at], d_recv.at[slot], send_sem.at[10], d_rs, (owner, t))

    def a_copy(s, cols, slot):
        return send(
            a_send.at[s, :, cols], a_recv.at[s, :, cols], kind(slot, 0), a_rs.at[slot], sibling
        )

    def b_copy(s, cols, slot, j):
        return send(
            b_send.at[s, j - 1, cols], b_recv.at[s, j - 1, cols], kind(slot, 1), b_rs.at[slot],
            (2 * chip(j) + c, t),
        )

    def w_copy(s, j):
        view = w_buf.at[s, r]
        return send(view, view, send_sem.at[2], w_rs.at[s], (2 * chip(j) + c, t))

    def w_chunk(f, j):
        view = w_fine.at[r, chunks[f]]
        return send(view, view, send_sem.at[3], w_rs.at[coarse + f], (2 * chip(j) + c, t))

    def v_chunk(f, j):
        view = w_fine.at[2 * source_chip(j) + c, chunks[f]]
        return send(view, view, send_sem.at[6], v_rs.at[coarse], sibling)

    def w_direct(f, j):
        view = w_fine.at[r, chunks[f]]
        return send(view, view, send_sem.at[7], w_rs.at[coarse + f], ((r + j) % n_rep, t))

    def v_copy(s, j):
        view = w_buf.at[s, 2 * source_chip(j) + c]
        return send(view, view, send_sem.at[4], v_rs.at[s], sibling)

    def wait_recv(ref, sem):
        send(ref, ref, send_sem.at[0], sem, sibling).wait_recv()

    def wait_send(ref, sem):
        send(ref, ref, sem, a_rs.at[0], sibling).wait_send()

    def terms(g, s, cols, slot):
        def term(owner):
            at = pl.multiple_of(owner * own_rows, own_rows)
            return jnp.dot(
                cot[g, cols], tok[:, pl.ds(at, own_rows)], preferred_element_type=jnp.float32
            )

        for q in range(nc):
            a_send[s, q, cols] = term(2 * q + 1 - c)
        a_copy(s, cols, slot).start()
        for q in range(nc):
            a_keep[s, q, cols] = term(2 * q + c)

    def gradient_stage(s):
        g = piece_at(orders, t, s)

        @pl.when(g // sub != t)
        def _():
            z_copy(g, 0).wait_recv()
            z_forward(g)

        terms(g, s, whole, s)

    def gradient_chunk(f):
        z_chunk(last, 0, f).wait_recv()
        z_forward_chunk(f)
        terms(last, coarse, chunks[f], coarse + f)

    def gradient_final():
        z_chunk(last, 0, final).wait_recv()
        z_forward_chunk(final)

        def term(owner):
            at = pl.multiple_of(owner * own_rows, own_rows)
            return jnp.dot(
                cot[last, chunks[final]], tok[:, pl.ds(at, own_rows)],
                preferred_element_type=jnp.float32,
            )

        goals = []
        for i in range(nc - 1):
            away = i + 1
            if nc == 4:
                away = (3 - 2 * (k % 2), 1 + k % 2, 2 + k % 2)[i]
            for parity in range(2):
                goals.append((2 * ((k + away) % nc) + parity, 2 * (away - 1) + c))
        goals.append((2 * k + 1 - c, n_rep - 2))
        group = 8
        for start in range(0, n_rep, group):
            now = range(start, min(start + group, n_rep - 1))
            products = [term(goals[at][0]) for at in now]
            if start + group >= n_rep:
                d_own[...] = term(r)
            for at, product in zip(now, products):
                d_send[at] = product.astype(jnp.bfloat16)
            for at in now:
                d_copy(at, *goals[at]).start()

    def summed_final():
        total = d_own[...]
        wait_recv(d_recv, d_rs)
        for i in range(n_rep - 1):
            total = total + d_recv[i].astype(jnp.float32)
        return total

    def chip_sum_stage(s, cols, slot):
        a_copy(s, cols, slot).wait_recv()
        for j in range(1, nc):
            q = chip(j)
            b_send[s, j - 1, cols] = (a_keep[s, q, cols] + a_recv[s, q, cols]).astype(
                jnp.bfloat16
            )
            b_copy(s, cols, slot, j).start()

    def summed(s, cols, slot):
        total = a_keep[s, k, cols] + a_recv[s, k, cols]
        wait_recv(b_recv.at[s, :, cols], b_rs.at[slot])
        for j in range(1, nc):
            total = total + b_recv[s, j - 1, cols].astype(jnp.float32)
        return total

    def adam(master, m1, m2, gradient):
        moment_one_new = beta_one * m1 + (1.0 - beta_one) * gradient
        moment_two_new = beta_two * m2 + (1.0 - beta_two) * gradient * gradient
        corrected_one = moment_one_new / (1.0 - beta_one**step_count)
        corrected_two = moment_two_new / (1.0 - beta_two**step_count)
        master_new = master - learning_rate * (
            corrected_one / (jnp.sqrt(corrected_two) + epsilon) + weight_decay * master
        )
        return master_new, moment_one_new, moment_two_new

    outs = (master_out, m1_out, m2_out)

    def update_stage(s):
        cols = pl.ds(pl.multiple_of(piece_at(orders, t, s) * cw, cw), cw)
        updated = adam(*(state[i, :, cols] for i in range(3)), summed(s, whole, s).T)
        w_buf[s, r] = updated[0].astype(jnp.bfloat16)
        for j in range(1, nc):
            w_copy(s, j).start()
        v_copy(s, 0).start()
        for out, value in zip(outs, updated):
            out[:, cols] = value

    def update_chunk(f):
        cols = chunks[f]
        total = summed_final() if f == final else summed(coarse, cols, coarse + f)
        updated = adam(*(state_t[i, cols] for i in range(3)), total)
        w_fine[r, cols] = updated[0].astype(jnp.bfloat16)
        if f >= direct:
            for j in range(1, n_rep):
                w_direct(f, j).start()
        else:
            for j in range(1, nc):
                w_chunk(f, j).start()
            v_chunk(f, 0).start()
        for i, value in enumerate(updated):
            new_t[i, cols] = value

    def share_stage(s):
        wait_recv(w_buf.at[s, 0 : nc - 1], w_rs.at[s])
        for j in range(1, nc):
            v_copy(s, j).start()

    def share_chunk(f):
        wait_recv(w_fine.at[0 : nc - 1, chunks[f]], w_rs.at[coarse + f])
        for j in range(1, nc):
            v_chunk(f, j).start()

    at_end = jnp.logical_or(t == 0, t == n_tp - 1)

    def to_end(j):
        to = (t + j) % n_tp
        return jnp.logical_or(to == 0, to == n_tp - 1)

    def p_copy(g, j):
        to = (t + j) % n_tp
        return send(part.at[g, to], part_recv.at[j - 1, g], send_sem.at[5], p_rs, (r, to))

    def decoded(g, product):
        rows = product.shape[0] // 2
        for i in range(2):
            part[g, :, i] = product[i * rows : (i + 1) * rows].reshape(n_tp, rows // n_tp, cw)

    both = inputs.shape[0] * inputs.shape[1]

    def decode_stage(s):
        wait_recv(w_buf.at[s, 0:nc], v_rs.at[s])
        g = piece_at(orders, t, s)
        block = w_buf[s].reshape(n_rep * own_rows, cw)
        decoded(
            g,
            jnp.dot(
                inputs[...].reshape(both, -1), block, preferred_element_type=jnp.float32
            ),
        )
        for j in range(1, n_tp):
            @pl.when(jnp.logical_not(to_end(j)))
            def _():
                p_copy(g, j).start()

    def decode_last():
        for f in range(direct, final + 1):
            wait_recv(w_fine.at[0 : n_rep - 1, chunks[f]], w_rs.at[coarse + f])
        wait_recv(w_fine.at[0:nc, shared_cols], v_rs.at[coarse])
        product = 0.0
        for owner in range(n_rep):
            rows = inputs[:, :, owner * own_rows : (owner + 1) * own_rows]
            product = product + lax.dot_general(
                rows.reshape(both, own_rows),
                w_fine[owner],
                (((1,), (1,)), ((), ())),
                preferred_element_type=jnp.float32,
            )
        decoded(last, product)

        @pl.when(at_end)
        def _():
            for far in (True, False):
                for j in range(1, n_tp):
                    @pl.when(to_end(j) == far)
                    def _():
                        p_copy(last, j).start()

        @pl.when(jnp.logical_not(at_end))
        def _():
            for j in range(1, n_tp):
                @pl.when(jnp.logical_not(to_end(j)))
                def _():
                    p_copy(last, j).start()

    def late_stage(s):
        g = piece_at(orders, t, s)
        for j in range(1, n_tp):
            @pl.when(to_end(j))
            def _():
                p_copy(g, j).start()

    cache_steps = min(4, coarse)

    def cache_stage(s):
        per_step = att_rows // cache_steps

        @pl.loop(0, per_step)
        def _(i):
            row = s * per_step + i
            allowed = mask[pl.ds(row, 1), :] > 0.0
            for h in range(groups):
                head = slice(h * HD, (h + 1) * HD)
                scores = lax.dot_general(
                    q_ref[row, h].astype(jnp.bfloat16),
                    keys[row, :, head],
                    (((1,), (1,)), ((), ())),
                    preferred_element_type=jnp.float32,
                )
                scores = jnp.where(allowed, scores / HD**0.5, -1e30)
                highest = jnp.max(scores, axis=-1, keepdims=True)
                weights = jnp.exp(scores - highest).astype(jnp.bfloat16)
                total = jnp.sum(weights.astype(jnp.float32), axis=-1, keepdims=True)
                mix = jnp.dot(weights, values[row, :, head], preferred_element_type=jnp.float32)
                for ref, value in ((early_max, highest), (early_sum, total), (early_mix, mix)):
                    value = jnp.broadcast_to(value, (stacked, HD))
                    ref[h, :, pl.ds(row, 1), :] = value.reshape(stacked, 1, HD)

    def turn_state():
        for i in range(3):
            state_t[i] = state[i, :, last_cols].T

    def sum_stage(s):
        chip_sum_stage(s, whole, s)

    def ahead(s):
        return jnp.logical_and(at_end, s >= cache_steps)

    def never(s):
        return False

    stages = (
        (sum_stage, 1, ahead),
        (update_stage, 2, lambda s: jnp.logical_and(at_end, s >= cache_steps - 1)),
        (share_stage, 3, never),
        (decode_stage, 4, never),
    )
    cache_now = jnp.where(at_end, cache_steps, 1)

    @pl.loop(0, coarse)
    def _(it):
        for stage, lag, skip in stages:
            @pl.when(jnp.logical_and(it >= lag, jnp.logical_not(skip(it - lag))))
            def _():
                stage(it - lag)

        @pl.when(it < cache_now)
        def _():
            cache_stage(it)

        gradient_stage(it)

        @pl.when(jnp.logical_and(ahead(it), it < coarse - 1))
        def _():
            sum_stage(it)

            @pl.when(it == cache_steps)
            def _():
                update_stage(it - 1)

            update_stage(it)

        @pl.when(it == cache_steps)
        def _():
            turn_state()

    sum_stage(coarse - 1)

    @pl.when(jnp.logical_not(at_end))
    def _():
        update_stage(coarse - 2)

    share_stage(coarse - 3)
    decode_stage(coarse - 4)

    @pl.when(jnp.logical_not(at_end))
    def _():
        cache_stage(1)

    for f, cols in enumerate(chunks[:-1]):
        gradient_chunk(f)
        chip_sum_stage(coarse, cols, coarse + f)
        if f == 0:
            share_stage(coarse - 2)
            update_stage(coarse - 1)
        if f > 1:
            update_chunk(f - 2)
    gradient_final()
    if final > 1:
        update_chunk(final - 2)
    for s in range(coarse - 3, coarse - 1):
        decode_stage(s)
    share_stage(coarse - 1)

    @pl.when(at_end)
    def _():
        @pl.loop(0, coarse - 1)
        def _(s):
            late_stage(s)

    update_chunk(final - 1)
    update_chunk(final)
    if direct > 0:
        share_chunk(0)
    decode_stage(coarse - 1)

    @pl.when(at_end)
    def _():
        late_stage(coarse - 1)

    for f in range(1, direct):
        share_chunk(f)
    for i, out in enumerate(outs):
        out[:, last_cols] = new_t[i].T
    decode_last()

    for place in range(n_tp):
        @pl.when(t == place)
        def _():
            if place < n_tp - 1:
                wait_send(cot.at[0 : (place + 1) * sub], z_ss.at[0])
            if place > 0:
                wait_send(cot.at[0 : (n_tp - place) * sub], z_ss.at[1])

    @pl.when(jnp.logical_not(at_end))
    def _():
        cache_stage(2)

        @pl.loop(0, steps)
        def _(s):
            late_stage(s)

        @pl.loop(3, cache_steps)
        def _(s):
            cache_stage(s)

    wait_send(a_send.at[0:coarse], send_sem.at[0])
    wait_send(b_send.at[0:coarse], send_sem.at[1])
    wait_send(a_send.at[coarse, :, summed_cols], send_sem.at[8])
    wait_send(b_send.at[coarse, :, summed_cols], send_sem.at[9])
    wait_send(d_send, send_sem.at[10])
    wait_send(w_buf.at[:, 0 : nc - 1], send_sem.at[2])
    wait_send(w_fine.at[0 : nc - 1, shared_cols], send_sem.at[3])
    wait_send(w_fine.at[0:nc, shared_cols], send_sem.at[6])
    wait_send(w_fine.at[0 : n_rep - 1, direct_cols], send_sem.at[7])
    wait_send(w_buf.at[:, 0:nc], send_sem.at[4])
    wait_recv(part_recv, p_rs)
    for g in range(steps):
        for i, out in enumerate((p1_out, p2_out)):
            total = part[g, t, i]
            for j in range(1, n_tp):
                total = total + part_recv[j - 1, g, i]
            out[:, g * cw : (g + 1) * cw] = total
    wait_send(part.at[:, 0 : n_tp - 1], send_sem.at[5])


def finish_kernel(
    master,
    m1,
    m2,
    p1,
    p2,
    early_max,
    early_sum,
    early_mix,
    table,
    queries,
    master_out,
    m1_out,
    m2_out,
    p1_out,
    p2_out,
    att1_out,
    att2_out,
    att,
    sems,
    att_sems,
):
    stores = [
        pltpu.make_async_copy(source, target, sems.at[i])
        for i, (source, target) in enumerate(
            ((master, master_out), (m1, m1_out), (m2, m2_out), (p1, p1_out), (p2, p2_out))
        )
    ]
    for store in stores:
        store.start()
    groups, stacked = early_max.shape[:2]
    half = stacked // 2
    keys, values = [], []
    for i, ref in enumerate((p1, p2)):
        total = ref[...]
        cosine = table[:, (1 + 2 * i) * HD : (2 + 2 * i) * HD]
        sine = table[:, (2 + 2 * i) * HD : (3 + 2 * i) * HD]
        for h in range(groups):
            head = total[:, h * HD : (h + 1) * HD]
            turned = head * cosine + pltpu.roll(head, HD // 2, 1) * sine
            value = total[:, (groups + h) * HD : (groups + h + 1) * HD]
            keys.append(turned.astype(jnp.bfloat16).astype(jnp.float32))
            values.append(value.astype(jnp.bfloat16).astype(jnp.float32))
    for i, out in enumerate((att1_out, att2_out)):
        for h in range(groups):
            for place in range(half):
                at = slice((h * half + place) * HD, (h * half + place + 1) * HD)
                query = queries[i, :, at].astype(jnp.float32)
                scores = [
                    jnp.sum(query * keys[n * groups + h], axis=-1, keepdims=True) / HD**0.5
                    for n in range(i + 1)
                ]
                before = early_max[h, i * half + place]
                highest = before
                for score in scores:
                    highest = jnp.maximum(highest, score)
                scale = jnp.exp(before - highest)
                below = early_sum[h, i * half + place] * scale
                above = early_mix[h, i * half + place] * scale
                for n, score in enumerate(scores):
                    weight = jnp.exp(score - highest).astype(jnp.bfloat16).astype(jnp.float32)
                    below = below + weight
                    above = above + weight * values[n * groups + h]
                att[i, :, at] = above / below
        store = pltpu.make_async_copy(att.at[i], out, att_sems.at[i])
        store.start()
        stores.append(store)
    for store in stores:
        store.wait()


def synchronise(
    n_rep,
    n_tp,
    tokens_in,
    cotangent,
    master,
    m1,
    m2,
    cache_keys,
    cache_values,
    inputs_one,
    inputs_two,
    queries_one,
    queries_two,
    lengths,
):
    tokens, width = tokens_in.shape
    sub = cotangent.shape[1] // SUB
    steps = n_tp * sub
    units = steps - 1 + len(CHUNKS)
    nc = n_rep // 2
    rows, cols = master.shape
    decode = inputs_one.shape[0]
    share = decode // n_tp
    f32, bf16 = jnp.float32, jnp.bfloat16
    count = queries_one.shape[0]
    stacked = (count, KVH, 2 * QH // KVH, HD)
    early = (KVH, 2 * QH // KVH, count, HD)
    vmem = pl.BlockSpec(memory_space=pltpu.VMEM)
    hbm = pl.BlockSpec(memory_space=pl.ANY)
    dma = pltpu.SemaphoreType.DMA
    held = pl.pallas_call(
        functools.partial(sync_kernel, n_rep, n_tp, sub),
        out_shape=[pltpu.VMEM((rows, cols), f32)] * 3
        + [pltpu.VMEM((share, cols), f32)] * 2
        + [pltpu.VMEM(early, f32)] * 3
        + [pltpu.VMEM((count, 5 * HD), f32), pltpu.VMEM((2, *queries_one.shape), bf16)],
        in_specs=[hbm] * 12,
        out_specs=[vmem] * 10,
        scratch_shapes=[
            pltpu.VMEM((3, rows, cols), f32),
            pltpu.VMEM((3, SUB, rows), f32),
            pltpu.VMEM((3, SUB, rows), f32),
            pltpu.VMEM(cache_keys.shape, bf16),
            pltpu.VMEM(cache_values.shape, bf16),
            pltpu.VMEM((2, *inputs_one.shape), bf16),
            pltpu.SMEM(lengths.shape, jnp.int32),
            pltpu.VMEM((count, HD), f32),
            pltpu.VMEM(stacked, f32),
            pltpu.VMEM((tokens, width), bf16),
            pltpu.VMEM((tokens, sub * SUB), bf16),
            pltpu.VMEM((steps, SUB, tokens), bf16),
            pltpu.VMEM((steps, nc, SUB, rows), f32),
            pltpu.VMEM((steps, nc, SUB, rows), f32),
            pltpu.VMEM((steps, nc, SUB, rows), f32),
            pltpu.VMEM((steps, nc - 1, SUB, rows), bf16),
            pltpu.VMEM((steps, nc - 1, SUB, rows), bf16),
            pltpu.VMEM((steps - 1, n_rep, rows, SUB), bf16),
            pltpu.VMEM((n_rep, SUB, rows), bf16),
            pltpu.VMEM((n_rep - 1, CHUNKS[-1], rows), bf16),
            pltpu.VMEM((n_rep - 1, CHUNKS[-1], rows), bf16),
            pltpu.VMEM((CHUNKS[-1], rows), f32),
            pltpu.VMEM((steps, n_tp, 2, share, SUB), f32),
            pltpu.VMEM((n_tp - 1, steps, 2, share, SUB), f32),
            dma((12,)),
            dma((2,)),
            dma((steps,)),
            dma((len(CHUNKS),)),
            dma((11,)),
            dma(()),
            dma((units,)),
            dma((units,)),
            dma((units,)),
            dma((steps,)),
            dma(()),
        ],
        compiler_params=pltpu.CompilerParams(
            collective_id=0, has_side_effects=True, vmem_limit_bytes=52 * 2**20
        ),
        name="synchronise",
    )(
        tokens_in,
        cotangent,
        master,
        m1,
        m2,
        cache_keys,
        cache_values,
        inputs_one,
        inputs_two,
        queries_one,
        queries_two,
        lengths,
    )
    wide = queries_one.shape
    return pl.pallas_call(
        finish_kernel,
        out_shape=[jax.ShapeDtypeStruct((rows, cols), f32)] * 3
        + [jax.ShapeDtypeStruct((share, cols), f32)] * 2
        + [jax.ShapeDtypeStruct(wide, f32)] * 2,
        in_specs=[vmem] * 10,
        out_specs=[hbm] * 7,
        scratch_shapes=[pltpu.VMEM((2, *wide), f32), dma((5,)), dma((2,))],
        compiler_params=pltpu.CompilerParams(vmem_limit_bytes=4 * 2**20),
        name="finish",
    )(*held)


def decode_table(lengths):
    shape = (lengths.shape[0], 5 * HD)
    column = lax.broadcasted_iota(jnp.int32, shape, 1)
    kind = column // HD
    lane = column % HD
    half_size = HD // 2
    inverse = rope_base ** (-2.0 * (lane % half_size).astype(jnp.float32) / HD)
    position = lengths + jnp.where(kind >= 3, 1, 0)
    angles = position.astype(jnp.float32) * inverse
    sine = jnp.where(lane < half_size, -jnp.sin(angles), jnp.sin(angles))
    allowed = jnp.where(lane < lengths, 1.0, 0.0)
    return jnp.where(kind == 0, allowed, jnp.where(kind % 2 == 1, jnp.cos(angles), sine))


def fits_kernel(n_rep, n_tp, cotangent, master, inputs_one, cache_keys):
    steps = n_tp * (cotangent.shape[1] // SUB)
    return (
        cache_keys.shape[1] == HD
        and steps > 6
        and len(CHUNKS) > 2
        and cache_keys.shape[0] % 4 == 0
        and n_rep % 2 == 0
        and n_rep >= 4
        and n_tp >= 2
        and cotangent.shape[1] % SUB == 0
        and cotangent.shape[0] % 256 == 0
        and master.shape[1] % 128 == 0
        and inputs_one.shape[0] % (8 * n_tp) == 0
    )


def shards(
    n_rep,
    n_tp,
    tokens_in,
    cotangent,
    master,
    moment_one,
    moment_two,
    inputs_one,
    inputs_two,
    queries_one,
    queries_two,
    cache_keys,
    cache_values,
    lengths,
):
    row_count = cache_keys.shape[0]
    if fits_kernel(n_rep, n_tp, cotangent, master[0], inputs_one, cache_keys):
        *updated, both_one, both_two, attended_one, attended_two = synchronise(
            n_rep,
            n_tp,
            tokens_in,
            cotangent,
            master[0],
            moment_one[0],
            moment_two[0],
            cache_keys,
            cache_values,
            inputs_one,
            inputs_two,
            queries_one,
            queries_two,
            lengths,
        )
        return (
            *(array[None] for array in updated),
            both_one,
            both_two,
            attended_one,
            attended_two,
        )
    places = jnp.arange(cache_keys.shape[1], dtype=jnp.int32)
    cache_allowed = places[None, :] < lengths[:, None]
    fresh = jnp.zeros((row_count, 1), jnp.int32) == 0
    early_one = partial_scores(queries_one, cache_keys, cache_values, cache_allowed)
    early_two = partial_scores(queries_two, cache_keys, cache_values, cache_allowed)
    columns = lax.all_gather(cotangent, "tp", axis=1, tiled=True)
    gradient = lax.psum_scatter(
        lax.dot_general(
            tokens_in, columns, (((0,), (0,)), ((), ())), preferred_element_type=jnp.float32
        ),
        "rep",
        scatter_dimension=0,
        tiled=True,
    ).reshape(master.shape)
    moment_one_new = beta_one * moment_one + (1.0 - beta_one) * gradient
    moment_two_new = beta_two * moment_two + (1.0 - beta_two) * gradient * gradient
    corrected_one = moment_one_new / (1.0 - beta_one**step_count)
    corrected_two = moment_two_new / (1.0 - beta_two**step_count)
    master_new = master - learning_rate * (
        corrected_one / (jnp.sqrt(corrected_two) + epsilon) + weight_decay * master
    )
    weights = master_new[0].astype(jnp.bfloat16)
    shard_rows = lax.all_gather(weights, "rep", axis=0, tiled=True)
    partial_one = jnp.dot(inputs_one, shard_rows, preferred_element_type=jnp.float32)
    partial_two = jnp.dot(inputs_two, shard_rows, preferred_element_type=jnp.float32)
    both_one, both_two = (
        lax.psum_scatter(partial_one, "tp", scatter_dimension=0, tiled=True),
        lax.psum_scatter(partial_two, "tp", scatter_dimension=0, tiled=True),
    )
    key_width = both_one.shape[1] // 2
    keys_one = rotate(both_one[:, :key_width], lengths).astype(jnp.bfloat16)
    values_one = both_one[:, key_width:].astype(jnp.bfloat16)
    keys_two = rotate(both_two[:, :key_width], lengths + 1).astype(jnp.bfloat16)
    values_two = both_two[:, key_width:].astype(jnp.bfloat16)
    late_one = partial_scores(queries_one, keys_one[:, None], values_one[:, None], fresh)
    attended_one = finish(*combine(early_one, late_one))
    fresh_pair = jnp.concatenate([fresh, fresh], axis=1)
    late_two = partial_scores(
        queries_two,
        jnp.stack([keys_one, keys_two], axis=1),
        jnp.stack([values_one, values_two], axis=1),
        fresh_pair,
    )
    attended_two = finish(*combine(early_two, late_two))
    return (
        master_new,
        moment_one_new,
        moment_two_new,
        both_one,
        both_two,
        attended_one,
        attended_two,
    )


def solution(mesh):
    return jax.shard_map(
        functools.partial(shards, mesh.shape["rep"], mesh.shape["tp"]),
        mesh=mesh,
        in_specs=(
            P("rep", "tp"),
            P("rep", "tp"),
            P("tp", "rep", None),
            P("tp", "rep", None),
            P("tp", "rep", None),
            P("rep", "tp"),
            P("rep", "tp"),
            P(("rep", "tp"), None),
            P(("rep", "tp"), None),
            P(("rep", "tp"), None, None),
            P(("rep", "tp"), None, None),
            P(("rep", "tp")),
        ),
        out_specs=(
            P("tp", "rep", None),
            P("tp", "rep", None),
            P("tp", "rep", None),
            P(("rep", "tp"), None),
            P(("rep", "tp"), None),
            P(("rep", "tp"), None),
            P(("rep", "tp"), None),
        ),
        check_vma=False,
    )
```

```python
import functools

import jax
import jax.numpy as jnp
from jax import lax
from jax.experimental import pallas as pl
from jax.experimental.pallas import tpu as pltpu
from jax.sharding import PartitionSpec as P

KVH = 4
QH = 32
HD = 128


learning_rate = 0.001
beta_one = 0.9
beta_two = 0.99
epsilon = 1e-08
weight_decay = 0.1
step_count = 10.0
rope_base = 500000.0


def rotate(vectors, positions):
    row_count = vectors.shape[0]
    half_size = HD // 2
    inverse = rope_base ** (-2.0 * jnp.arange(half_size).astype(jnp.float32) / HD)
    angles = positions.astype(jnp.float32)[:, None, None] * inverse[None, None, :]
    shaped = vectors.reshape(row_count, -1, HD)
    first_half = shaped[..., :half_size]
    second_half = shaped[..., half_size:]
    cosine = jnp.cos(angles)
    sine = jnp.sin(angles)
    turned = jnp.concatenate(
        [first_half * cosine - second_half * sine, second_half * cosine + first_half * sine],
        axis=-1,
    )
    return turned.reshape(row_count, -1)


def partial_scores(queries, all_keys, all_values, allowed):
    row_count = all_keys.shape[0]
    places = all_keys.shape[1]
    group_size = QH // KVH
    shaped_queries = queries.astype(jnp.float32).reshape(row_count, KVH, group_size, HD)
    shaped_keys = all_keys.astype(jnp.float32).reshape(row_count, places, KVH, HD)
    shaped_values = all_values.astype(jnp.float32).reshape(row_count, places, KVH, HD)
    scores = jnp.einsum("rkgd,rpkd->rkgp", shaped_queries, shaped_keys) / HD**0.5
    scores = jnp.where(allowed[:, None, None, :], scores, -1e30)
    highest = jnp.max(scores, axis=-1)
    weights = lax.optimization_barrier(
        jnp.exp(scores - highest[..., None]).astype(jnp.bfloat16)
    ).astype(jnp.float32)
    return (
        highest,
        jnp.sum(weights, axis=-1),
        jnp.einsum("rkgp,rpkd->rkgd", weights, shaped_values),
    )


def finish(highest, denominator, numerator):
    row_count = numerator.shape[0]
    return (numerator / denominator[..., None]).reshape(row_count, -1)


def combine(earlier, later):
    highest = jnp.maximum(earlier[0], later[0])
    scale_early = jnp.exp(earlier[0] - highest)
    scale_late = jnp.exp(later[0] - highest)
    denominator = earlier[1] * scale_early + later[1] * scale_late
    numerator = earlier[2] * scale_early[..., None] + later[2] * scale_late[..., None]
    return (highest, denominator, numerator)


MESH = pl.DeviceIdType.MESH
SUB = 128
CHUNKS = (48, 32, 32, 16)
DIRECT = 2


def arrival_orders(n_tp, sub):
    orders = []
    for t in range(n_tp):
        near = 0 if 2 * t < n_tp else n_tp - 1
        inner = t not in (0, n_tp - 1)
        pieces = []
        for b in range(n_tp):
            away = abs(b - t)
            rank = away
            if inner and away:
                rank = 2 * away + (0 if (b > t) == (near == 0) else 1) - 1
            pieces += [(rank, u, b) for u in range(sub)]
        pieces.sort()
        orders.append([b * sub + u for _, u, b in pieces])
    return orders


def piece_at(orders, t, s):
    found = 0
    for place, order in enumerate(orders):
        for step, piece in enumerate(order):
            if isinstance(s, int):
                if s == step:
                    found = found + jnp.where(t == place, piece, 0)
            else:
                found = found + jnp.where(jnp.logical_and(t == place, s == step), piece, 0)
    return found


def sync_kernel(
    n_rep,
    n_tp,
    sub,
    tok_hbm,
    cot_hbm,
    master_hbm,
    m1_hbm,
    m2_hbm,
    keys_hbm,
    values_hbm,
    in1_hbm,
    in2_hbm,
    q1_hbm,
    q2_hbm,
    lengths_hbm,
    master_out,
    m1_out,
    m2_out,
    p1_out,
    p2_out,
    early_max,
    early_sum,
    early_mix,
    table_ref,
    queries,
    state,
    state_t,
    new_t,
    keys,
    values,
    inputs,
    lengths_ref,
    mask,
    q_ref,
    tok,
    cot_raw,
    cot,
    a_send,
    a_keep,
    a_recv,
    b_send,
    b_recv,
    w_buf,
    w_fine,
    d_send,
    d_recv,
    d_own,
    part,
    part_recv,
    load_sem,
    z_ss,
    z_rs,
    z_fs,
    send_sem,
    d_rs,
    a_rs,
    b_rs,
    w_rs,
    v_rs,
    p_rs,
):
    nc = n_rep // 2
    steps = n_tp * sub
    coarse = steps - 1
    cw = SUB
    chunks = []
    for width in CHUNKS:
        chunks.append(slice(sum(CHUNKS[: len(chunks)]), sum(CHUNKS[: len(chunks)]) + width))
    whole = slice(0, cw)
    final = len(chunks) - 1
    direct = len(chunks) - DIRECT
    shared_cols = slice(0, chunks[direct].start)
    direct_cols = slice(chunks[direct].start, cw)
    summed_cols = slice(0, chunks[final].start)
    r = lax.axis_index("rep")
    t = lax.axis_index("tp")
    k = r // 2
    c = r % 2
    sibling = (2 * k + 1 - c, t)
    own_rows = master_hbm.shape[0]
    att_rows, groups, stacked, _ = q_ref.shape
    orders = arrival_orders(n_tp, sub)
    last = piece_at(orders, t, coarse)
    last_cols = pl.ds(pl.multiple_of(last * cw, cw), cw)

    def chip(j):
        return (k + j) % nc

    def source_chip(j):
        return (k + nc - j) % nc

    def send(source, target, send_sem_ref, recv_sem_ref, device):
        return pltpu.make_async_remote_copy(
            source, target, send_sem_ref, recv_sem_ref, device_id=device, device_id_type=MESH
        )

    load_cot = pltpu.make_async_copy(cot_hbm, cot_raw, load_sem.at[0])
    load_tok = pltpu.make_async_copy(tok_hbm, tok, load_sem.at[1])
    load_lengths = pltpu.make_async_copy(lengths_hbm, lengths_ref, load_sem.at[2])
    load_keys = pltpu.make_async_copy(keys_hbm, keys, load_sem.at[3])
    load_values = pltpu.make_async_copy(values_hbm, values, load_sem.at[4])
    load_queries = [
        pltpu.make_async_copy(source, queries.at[i], load_sem.at[5 + i])
        for i, source in enumerate((q1_hbm, q2_hbm))
    ]
    load_inputs = [
        pltpu.make_async_copy(source, inputs.at[i], load_sem.at[7 + i])
        for i, source in enumerate((in1_hbm, in2_hbm))
    ]
    load_state = [
        pltpu.make_async_copy(source, state.at[i], load_sem.at[9 + i])
        for i, source in enumerate((master_hbm, m1_hbm, m2_hbm))
    ]
    load_cot.start()
    barrier = pltpu.get_barrier_semaphore()
    pl.semaphore_signal(barrier, inc=1, device_id=sibling, device_id_type=MESH)
    for j in range(1, nc):
        pl.semaphore_signal(barrier, inc=1, device_id=(2 * chip(j) + c, t), device_id_type=MESH)

    @pl.when(t < n_tp - 1)
    def _():
        pl.semaphore_signal(barrier, inc=1, device_id=(r, t + 1), device_id_type=MESH)

    @pl.when(t > 0)
    def _():
        pl.semaphore_signal(barrier, inc=1, device_id=(r, t - 1), device_id_type=MESH)

    late_loads = [*load_queries, load_keys, load_values, *load_state, *load_inputs]
    load_cot.wait()
    for load in [load_lengths, *late_loads[:4], load_tok, *late_loads[4:]]:
        load.start()
    cot[t * sub] = cot_raw[:, 0:cw].T
    near = jnp.where(t > 0, 1, 0) + jnp.where(t < n_tp - 1, 1, 0)
    pl.semaphore_wait(barrier, nc + near)

    def neighbour(side):
        return jnp.minimum(t + 1, n_tp - 1) if side == 0 else jnp.maximum(t - 1, 0)

    def z_copy(g, side):
        return send(cot.at[g], cot.at[g], z_ss.at[side], z_rs.at[g], (r, neighbour(side)))

    def z_chunk(g, side, f):
        view = cot.at[g, chunks[f]]
        return send(view, view, z_ss.at[side], z_fs.at[f], (r, neighbour(side)))

    def z_goes(g, side):
        b = g // sub
        if side == 0:
            return jnp.logical_and(b <= t, t < n_tp - 1)
        return jnp.logical_and(b >= t, t > 0)

    def in_chunks(g, side):
        return g == piece_at(orders, neighbour(side), coarse)

    def z_forward(g):
        for side in (0, 1):
            @pl.when(jnp.logical_and(z_goes(g, side), jnp.logical_not(in_chunks(g, side))))
            def _():
                z_copy(g, side).start()

            @pl.when(jnp.logical_and(z_goes(g, side), in_chunks(g, side)))
            def _():
                for f in range(len(chunks)):
                    z_chunk(g, side, f).start()

    def z_forward_chunk(f):
        for side in (0, 1):
            @pl.when(jnp.logical_and(z_goes(last, side), in_chunks(last, side)))
            def _():
                z_chunk(last, side, f).start()

            if f == len(chunks) - 1:
                @pl.when(
                    jnp.logical_and(z_goes(last, side), jnp.logical_not(in_chunks(last, side)))
                )
                def _():
                    z_copy(last, side).start()

    z_forward(t * sub)
    for u in range(1, sub):
        cot[t * sub + u] = cot_raw[:, u * cw : (u + 1) * cw].T
        z_forward(t * sub + u)
    load_lengths.wait()
    row_ids = lax.broadcasted_iota(jnp.int32, (att_rows, HD), 0)
    length = jnp.zeros((att_rows, HD), jnp.int32)
    for row in range(att_rows):
        length = jnp.where(row_ids == row, lengths_ref[row], length)
    table_ref[...] = decode_table(length[:, 0:1])
    mask[...] = table_ref[:, 0:HD]
    for load in load_queries:
        load.wait()
    for i in range(2):
        for h in range(groups):
            for place in range(stacked // 2):
                at = (h * (stacked // 2) + place) * HD
                q_ref[:, h, i * (stacked // 2) + place, :] = queries[i, :, at : at + HD].astype(
                    jnp.float32
                )
    load_tok.wait()
    for load in late_loads[2:]:
        load.wait()

    def kind(slot, sem):
        return send_sem.at[sem + (8 if isinstance(slot, int) and slot >= coarse else 0)]

    def d_copy(at, owner, slot):
        return send(d_send.at[at], d_recv.at[slot], send_sem.at[10], d_rs, (owner, t))

    def a_copy(s, cols, slot):
        return send(
            a_send.at[s, :, cols], a_recv.at[s, :, cols], kind(slot, 0), a_rs.at[slot], sibling
        )

    def b_copy(s, cols, slot, j):
        return send(
            b_send.at[s, j - 1, cols], b_recv.at[s, j - 1, cols], kind(slot, 1), b_rs.at[slot],
            (2 * chip(j) + c, t),
        )

    def w_copy(s, j):
        view = w_buf.at[s, r]
        return send(view, view, send_sem.at[2], w_rs.at[s], (2 * chip(j) + c, t))

    def w_chunk(f, j):
        view = w_fine.at[r, chunks[f]]
        return send(view, view, send_sem.at[3], w_rs.at[coarse + f], (2 * chip(j) + c, t))

    def v_chunk(f, j):
        view = w_fine.at[2 * source_chip(j) + c, chunks[f]]
        return send(view, view, send_sem.at[6], v_rs.at[coarse], sibling)

    def w_direct(f, j):
        view = w_fine.at[r, chunks[f]]
        return send(view, view, send_sem.at[7], w_rs.at[coarse + f], ((r + j) % n_rep, t))

    def v_copy(s, j):
        view = w_buf.at[s, 2 * source_chip(j) + c]
        return send(view, view, send_sem.at[4], v_rs.at[s], sibling)

    def wait_recv(ref, sem):
        send(ref, ref, send_sem.at[0], sem, sibling).wait_recv()

    def wait_send(ref, sem):
        send(ref, ref, sem, a_rs.at[0], sibling).wait_send()

    def terms(g, s, cols, slot):
        def term(owner):
            at = pl.multiple_of(owner * own_rows, own_rows)
            return jnp.dot(
                cot[g, cols], tok[:, pl.ds(at, own_rows)], preferred_element_type=jnp.float32
            )

        for q in range(nc):
            a_send[s, q, cols] = term(2 * q + 1 - c)
        a_copy(s, cols, slot).start()
        for q in range(nc):
            a_keep[s, q, cols] = term(2 * q + c)

    def gradient_stage(s):
        g = piece_at(orders, t, s)

        @pl.when(g // sub != t)
        def _():
            z_copy(g, 0).wait_recv()
            z_forward(g)

        terms(g, s, whole, s)

    def gradient_chunk(f):
        z_chunk(last, 0, f).wait_recv()
        z_forward_chunk(f)
        terms(last, coarse, chunks[f], coarse + f)

    def gradient_final():
        z_chunk(last, 0, final).wait_recv()
        z_forward_chunk(final)

        def term(owner):
            at = pl.multiple_of(owner * own_rows, own_rows)
            return jnp.dot(
                cot[last, chunks[final]], tok[:, pl.ds(at, own_rows)],
                preferred_element_type=jnp.float32,
            )

        goals = []
        for i in range(nc - 1):
            away = i + 1
            if nc == 4:
                away = (3 - 2 * (k % 2), 1 + k % 2, 2 + k % 2)[i]
            for parity in range(2):
                goals.append((2 * ((k + away) % nc) + parity, 2 * (away - 1) + c))
        goals.append((2 * k + 1 - c, n_rep - 2))
        group = 8
        for start in range(0, n_rep, group):
            now = range(start, min(start + group, n_rep - 1))
            products = [term(goals[at][0]) for at in now]
            if start + group >= n_rep:
                d_own[...] = term(r)
            for at, product in zip(now, products):
                d_send[at] = product.astype(jnp.bfloat16)
            for at in now:
                d_copy(at, *goals[at]).start()

    def summed_final():
        total = d_own[...]
        wait_recv(d_recv, d_rs)
        for i in range(n_rep - 1):
            total = total + d_recv[i].astype(jnp.float32)
        return total

    def chip_sum_stage(s, cols, slot):
        a_copy(s, cols, slot).wait_recv()
        for j in range(1, nc):
            q = chip(j)
            b_send[s, j - 1, cols] = (a_keep[s, q, cols] + a_recv[s, q, cols]).astype(
                jnp.bfloat16
            )
            b_copy(s, cols, slot, j).start()

    def summed(s, cols, slot):
        total = a_keep[s, k, cols] + a_recv[s, k, cols]
        wait_recv(b_recv.at[s, :, cols], b_rs.at[slot])
        for j in range(1, nc):
            total = total + b_recv[s, j - 1, cols].astype(jnp.float32)
        return total

    def adam(master, m1, m2, gradient):
        moment_one_new = beta_one * m1 + (1.0 - beta_one) * gradient
        moment_two_new = beta_two * m2 + (1.0 - beta_two) * gradient * gradient
        corrected_one = moment_one_new / (1.0 - beta_one**step_count)
        corrected_two = moment_two_new / (1.0 - beta_two**step_count)
        master_new = master - learning_rate * (
            corrected_one / (jnp.sqrt(corrected_two) + epsilon) + weight_decay * master
        )
        return master_new, moment_one_new, moment_two_new

    outs = (master_out, m1_out, m2_out)

    def update_stage(s):
        cols = pl.ds(pl.multiple_of(piece_at(orders, t, s) * cw, cw), cw)
        updated = adam(*(state[i, :, cols] for i in range(3)), summed(s, whole, s).T)
        w_buf[s, r] = updated[0].astype(jnp.bfloat16)
        for j in range(1, nc):
            w_copy(s, j).start()
        v_copy(s, 0).start()
        for out, value in zip(outs, updated):
            out[:, cols] = value

    def update_chunk(f):
        cols = chunks[f]
        total = summed_final() if f == final else summed(coarse, cols, coarse + f)
        updated = adam(*(state_t[i, cols] for i in range(3)), total)
        w_fine[r, cols] = updated[0].astype(jnp.bfloat16)
        if f >= direct:
            for j in range(1, n_rep):
                w_direct(f, j).start()
        else:
            for j in range(1, nc):
                w_chunk(f, j).start()
            v_chunk(f, 0).start()
        for i, value in enumerate(updated):
            new_t[i, cols] = value

    def share_stage(s):
        wait_recv(w_buf.at[s, 0 : nc - 1], w_rs.at[s])
        for j in range(1, nc):
            v_copy(s, j).start()

    def share_chunk(f):
        wait_recv(w_fine.at[0 : nc - 1, chunks[f]], w_rs.at[coarse + f])
        for j in range(1, nc):
            v_chunk(f, j).start()

    at_end = jnp.logical_or(t == 0, t == n_tp - 1)

    def to_end(j):
        to = (t + j) % n_tp
        return jnp.logical_or(to == 0, to == n_tp - 1)

    def p_copy(g, j):
        to = (t + j) % n_tp
        return send(part.at[g, to], part_recv.at[j - 1, g], send_sem.at[5], p_rs, (r, to))

    def decoded(g, product):
        rows = product.shape[0] // 2
        for i in range(2):
            part[g, :, i] = product[i * rows : (i + 1) * rows].reshape(n_tp, rows // n_tp, cw)

    both = inputs.shape[0] * inputs.shape[1]

    def decode_stage(s):
        wait_recv(w_buf.at[s, 0:nc], v_rs.at[s])
        g = piece_at(orders, t, s)
        block = w_buf[s].reshape(n_rep * own_rows, cw)
        decoded(
            g,
            jnp.dot(
                inputs[...].reshape(both, -1), block, preferred_element_type=jnp.float32
            ),
        )
        for j in range(1, n_tp):
            @pl.when(jnp.logical_not(to_end(j)))
            def _():
                p_copy(g, j).start()

    def decode_last():
        for f in range(direct, final + 1):
            wait_recv(w_fine.at[0 : n_rep - 1, chunks[f]], w_rs.at[coarse + f])
        wait_recv(w_fine.at[0:nc, shared_cols], v_rs.at[coarse])
        product = 0.0
        for owner in range(n_rep):
            rows = inputs[:, :, owner * own_rows : (owner + 1) * own_rows]
            product = product + lax.dot_general(
                rows.reshape(both, own_rows),
                w_fine[owner],
                (((1,), (1,)), ((), ())),
                preferred_element_type=jnp.float32,
            )
        decoded(last, product)

        @pl.when(at_end)
        def _():
            for far in (True, False):
                for j in range(1, n_tp):
                    @pl.when(to_end(j) == far)
                    def _():
                        p_copy(last, j).start()

        @pl.when(jnp.logical_not(at_end))
        def _():
            for j in range(1, n_tp):
                @pl.when(jnp.logical_not(to_end(j)))
                def _():
                    p_copy(last, j).start()

    def late_stage(s):
        g = piece_at(orders, t, s)
        for j in range(1, n_tp):
            @pl.when(to_end(j))
            def _():
                p_copy(g, j).start()

    cache_steps = min(4, coarse)

    def cache_stage(s):
        per_step = att_rows // cache_steps

        @pl.loop(0, per_step)
        def _(i):
            row = s * per_step + i
            allowed = mask[pl.ds(row, 1), :] > 0.0
            for h in range(groups):
                head = slice(h * HD, (h + 1) * HD)
                scores = lax.dot_general(
                    q_ref[row, h].astype(jnp.bfloat16),
                    keys[row, :, head],
                    (((1,), (1,)), ((), ())),
                    preferred_element_type=jnp.float32,
                )
                scores = jnp.where(allowed, scores / HD**0.5, -1e30)
                highest = jnp.max(scores, axis=-1, keepdims=True)
                weights = jnp.exp(scores - highest).astype(jnp.bfloat16)
                total = jnp.sum(weights.astype(jnp.float32), axis=-1, keepdims=True)
                mix = jnp.dot(weights, values[row, :, head], preferred_element_type=jnp.float32)
                for ref, value in ((early_max, highest), (early_sum, total), (early_mix, mix)):
                    value = jnp.broadcast_to(value, (stacked, HD))
                    ref[h, :, pl.ds(row, 1), :] = value.reshape(stacked, 1, HD)

    def turn_state():
        for i in range(3):
            state_t[i] = state[i, :, last_cols].T

    def sum_stage(s):
        chip_sum_stage(s, whole, s)

    def ahead(s):
        return jnp.logical_and(at_end, s >= cache_steps)

    def never(s):
        return False

    stages = (
        (sum_stage, 1, ahead),
        (update_stage, 2, lambda s: jnp.logical_and(at_end, s >= cache_steps - 1)),
        (share_stage, 3, never),
        (decode_stage, 4, never),
    )
    cache_now = jnp.where(at_end, cache_steps, 1)

    @pl.loop(0, coarse)
    def _(it):
        for stage, lag, skip in stages:
            @pl.when(jnp.logical_and(it >= lag, jnp.logical_not(skip(it - lag))))
            def _():
                stage(it - lag)

        @pl.when(it < cache_now)
        def _():
            cache_stage(it)

        gradient_stage(it)

        @pl.when(jnp.logical_and(ahead(it), it < coarse - 1))
        def _():
            sum_stage(it)

            @pl.when(it == cache_steps)
            def _():
                update_stage(it - 1)

            update_stage(it)

        @pl.when(it == cache_steps)
        def _():
            turn_state()

    sum_stage(coarse - 1)

    @pl.when(jnp.logical_not(at_end))
    def _():
        update_stage(coarse - 2)

    share_stage(coarse - 3)
    decode_stage(coarse - 4)

    @pl.when(jnp.logical_not(at_end))
    def _():
        cache_stage(1)

    for f, cols in enumerate(chunks[:-1]):
        gradient_chunk(f)
        chip_sum_stage(coarse, cols, coarse + f)
        if f == 0:
            share_stage(coarse - 2)
            update_stage(coarse - 1)
        if f > 1:
            update_chunk(f - 2)
    gradient_final()
    if final > 1:
        update_chunk(final - 2)
    for s in range(coarse - 3, coarse - 1):
        decode_stage(s)
    share_stage(coarse - 1)

    @pl.when(at_end)
    def _():
        @pl.loop(0, coarse - 1)
        def _(s):
            late_stage(s)

    update_chunk(final - 1)
    update_chunk(final)
    if direct > 0:
        share_chunk(0)
    decode_stage(coarse - 1)

    @pl.when(at_end)
    def _():
        late_stage(coarse - 1)

    for f in range(1, direct):
        share_chunk(f)
    for i, out in enumerate(outs):
        out[:, last_cols] = new_t[i].T
    decode_last()

    for place in range(n_tp):
        @pl.when(t == place)
        def _():
            if place < n_tp - 1:
                wait_send(cot.at[0 : (place + 1) * sub], z_ss.at[0])
            if place > 0:
                wait_send(cot.at[0 : (n_tp - place) * sub], z_ss.at[1])

    @pl.when(jnp.logical_not(at_end))
    def _():
        cache_stage(2)

        @pl.loop(0, steps)
        def _(s):
            late_stage(s)

        @pl.loop(3, cache_steps)
        def _(s):
            cache_stage(s)

    wait_send(a_send.at[0:coarse], send_sem.at[0])
    wait_send(b_send.at[0:coarse], send_sem.at[1])
    wait_send(a_send.at[coarse, :, summed_cols], send_sem.at[8])
    wait_send(b_send.at[coarse, :, summed_cols], send_sem.at[9])
    wait_send(d_send, send_sem.at[10])
    wait_send(w_buf.at[:, 0 : nc - 1], send_sem.at[2])
    wait_send(w_fine.at[0 : nc - 1, shared_cols], send_sem.at[3])
    wait_send(w_fine.at[0:nc, shared_cols], send_sem.at[6])
    wait_send(w_fine.at[0 : n_rep - 1, direct_cols], send_sem.at[7])
    wait_send(w_buf.at[:, 0:nc], send_sem.at[4])
    wait_recv(part_recv, p_rs)
    for g in range(steps):
        for i, out in enumerate((p1_out, p2_out)):
            total = part[g, t, i]
            for j in range(1, n_tp):
                total = total + part_recv[j - 1, g, i]
            out[:, g * cw : (g + 1) * cw] = total
    wait_send(part.at[:, 0 : n_tp - 1], send_sem.at[5])


def finish_kernel(
    master,
    m1,
    m2,
    p1,
    p2,
    early_max,
    early_sum,
    early_mix,
    table,
    queries,
    master_out,
    m1_out,
    m2_out,
    p1_out,
    p2_out,
    att1_out,
    att2_out,
    att,
    sems,
    att_sems,
):
    stores = [
        pltpu.make_async_copy(source, target, sems.at[i])
        for i, (source, target) in enumerate(
            ((master, master_out), (m1, m1_out), (m2, m2_out), (p1, p1_out), (p2, p2_out))
        )
    ]
    for store in stores:
        store.start()
    groups, stacked = early_max.shape[:2]
    half = stacked // 2
    keys, values = [], []
    for i, ref in enumerate((p1, p2)):
        total = ref[...]
        cosine = table[:, (1 + 2 * i) * HD : (2 + 2 * i) * HD]
        sine = table[:, (2 + 2 * i) * HD : (3 + 2 * i) * HD]
        for h in range(groups):
            head = total[:, h * HD : (h + 1) * HD]
            turned = head * cosine + pltpu.roll(head, HD // 2, 1) * sine
            value = total[:, (groups + h) * HD : (groups + h + 1) * HD]
            keys.append(turned.astype(jnp.bfloat16).astype(jnp.float32))
            values.append(value.astype(jnp.bfloat16).astype(jnp.float32))
    for i, out in enumerate((att1_out, att2_out)):
        for h in range(groups):
            for place in range(half):
                at = slice((h * half + place) * HD, (h * half + place + 1) * HD)
                query = queries[i, :, at].astype(jnp.float32)
                scores = [
                    jnp.sum(query * keys[n * groups + h], axis=-1, keepdims=True) / HD**0.5
                    for n in range(i + 1)
                ]
                before = early_max[h, i * half + place]
                highest = before
                for score in scores:
                    highest = jnp.maximum(highest, score)
                scale = jnp.exp(before - highest)
                below = early_sum[h, i * half + place] * scale
                above = early_mix[h, i * half + place] * scale
                for n, score in enumerate(scores):
                    weight = jnp.exp(score - highest).astype(jnp.bfloat16).astype(jnp.float32)
                    below = below + weight
                    above = above + weight * values[n * groups + h]
                att[i, :, at] = above / below
        store = pltpu.make_async_copy(att.at[i], out, att_sems.at[i])
        store.start()
        stores.append(store)
    for store in stores:
        store.wait()


def synchronise(
    n_rep,
    n_tp,
    tokens_in,
    cotangent,
    master,
    m1,
    m2,
    cache_keys,
    cache_values,
    inputs_one,
    inputs_two,
    queries_one,
    queries_two,
    lengths,
):
    tokens, width = tokens_in.shape
    sub = cotangent.shape[1] // SUB
    steps = n_tp * sub
    units = steps - 1 + len(CHUNKS)
    nc = n_rep // 2
    rows, cols = master.shape
    decode = inputs_one.shape[0]
    share = decode // n_tp
    f32, bf16 = jnp.float32, jnp.bfloat16
    count = queries_one.shape[0]
    stacked = (count, KVH, 2 * QH // KVH, HD)
    early = (KVH, 2 * QH // KVH, count, HD)
    vmem = pl.BlockSpec(memory_space=pltpu.VMEM)
    hbm = pl.BlockSpec(memory_space=pl.ANY)
    dma = pltpu.SemaphoreType.DMA
    held = pl.pallas_call(
        functools.partial(sync_kernel, n_rep, n_tp, sub),
        out_shape=[pltpu.VMEM((rows, cols), f32)] * 3
        + [pltpu.VMEM((share, cols), f32)] * 2
        + [pltpu.VMEM(early, f32)] * 3
        + [pltpu.VMEM((count, 5 * HD), f32), pltpu.VMEM((2, *queries_one.shape), bf16)],
        in_specs=[hbm] * 12,
        out_specs=[vmem] * 10,
        scratch_shapes=[
            pltpu.VMEM((3, rows, cols), f32),
            pltpu.VMEM((3, SUB, rows), f32),
            pltpu.VMEM((3, SUB, rows), f32),
            pltpu.VMEM(cache_keys.shape, bf16),
            pltpu.VMEM(cache_values.shape, bf16),
            pltpu.VMEM((2, *inputs_one.shape), bf16),
            pltpu.SMEM(lengths.shape, jnp.int32),
            pltpu.VMEM((count, HD), f32),
            pltpu.VMEM(stacked, f32),
            pltpu.VMEM((tokens, width), bf16),
            pltpu.VMEM((tokens, sub * SUB), bf16),
            pltpu.VMEM((steps, SUB, tokens), bf16),
            pltpu.VMEM((steps, nc, SUB, rows), f32),
            pltpu.VMEM((steps, nc, SUB, rows), f32),
            pltpu.VMEM((steps, nc, SUB, rows), f32),
            pltpu.VMEM((steps, nc - 1, SUB, rows), bf16),
            pltpu.VMEM((steps, nc - 1, SUB, rows), bf16),
            pltpu.VMEM((steps - 1, n_rep, rows, SUB), bf16),
            pltpu.VMEM((n_rep, SUB, rows), bf16),
            pltpu.VMEM((n_rep - 1, CHUNKS[-1], rows), bf16),
            pltpu.VMEM((n_rep - 1, CHUNKS[-1], rows), bf16),
            pltpu.VMEM((CHUNKS[-1], rows), f32),
            pltpu.VMEM((steps, n_tp, 2, share, SUB), f32),
            pltpu.VMEM((n_tp - 1, steps, 2, share, SUB), f32),
            dma((12,)),
            dma((2,)),
            dma((steps,)),
            dma((len(CHUNKS),)),
            dma((11,)),
            dma(()),
            dma((units,)),
            dma((units,)),
            dma((units,)),
            dma((steps,)),
            dma(()),
        ],
        compiler_params=pltpu.CompilerParams(
            collective_id=0, has_side_effects=True, vmem_limit_bytes=52 * 2**20
        ),
        name="synchronise",
    )(
        tokens_in,
        cotangent,
        master,
        m1,
        m2,
        cache_keys,
        cache_values,
        inputs_one,
        inputs_two,
        queries_one,
        queries_two,
        lengths,
    )
    wide = queries_one.shape
    return pl.pallas_call(
        finish_kernel,
        out_shape=[jax.ShapeDtypeStruct((rows, cols), f32)] * 3
        + [jax.ShapeDtypeStruct((share, cols), f32)] * 2
        + [jax.ShapeDtypeStruct(wide, f32)] * 2,
        in_specs=[vmem] * 10,
        out_specs=[hbm] * 7,
        scratch_shapes=[pltpu.VMEM((2, *wide), f32), dma((5,)), dma((2,))],
        compiler_params=pltpu.CompilerParams(vmem_limit_bytes=4 * 2**20),
        name="finish",
    )(*held)


def decode_table(lengths):
    shape = (lengths.shape[0], 5 * HD)
    column = lax.broadcasted_iota(jnp.int32, shape, 1)
    kind = column // HD
    lane = column % HD
    half_size = HD // 2
    inverse = rope_base ** (-2.0 * (lane % half_size).astype(jnp.float32) / HD)
    position = lengths + jnp.where(kind >= 3, 1, 0)
    angles = position.astype(jnp.float32) * inverse
    sine = jnp.where(lane < half_size, -jnp.sin(angles), jnp.sin(angles))
    allowed = jnp.where(lane < lengths, 1.0, 0.0)
    return jnp.where(kind == 0, allowed, jnp.where(kind % 2 == 1, jnp.cos(angles), sine))


def fits_kernel(n_rep, n_tp, cotangent, master, inputs_one, cache_keys):
    steps = n_tp * (cotangent.shape[1] // SUB)
    return (
        cache_keys.shape[1] == HD
        and steps > 6
        and len(CHUNKS) > 2
        and cache_keys.shape[0] % 4 == 0
        and n_rep % 2 == 0
        and n_rep >= 4
        and n_tp >= 2
        and cotangent.shape[1] % SUB == 0
        and cotangent.shape[0] % 256 == 0
        and master.shape[1] % 128 == 0
        and inputs_one.shape[0] % (8 * n_tp) == 0
    )


def shards(
    n_rep,
    n_tp,
    tokens_in,
    cotangent,
    master,
    moment_one,
    moment_two,
    inputs_one,
    inputs_two,
    queries_one,
    queries_two,
    cache_keys,
    cache_values,
    lengths,
):
    row_count = cache_keys.shape[0]
    if fits_kernel(n_rep, n_tp, cotangent, master[0], inputs_one, cache_keys):
        *updated, both_one, both_two, attended_one, attended_two = synchronise(
            n_rep,
            n_tp,
            tokens_in,
            cotangent,
            master[0],
            moment_one[0],
            moment_two[0],
            cache_keys,
            cache_values,
            inputs_one,
            inputs_two,
            queries_one,
            queries_two,
            lengths,
        )
        return (
            *(array[None] for array in updated),
            both_one,
            both_two,
            attended_one,
            attended_two,
        )
    places = jnp.arange(cache_keys.shape[1], dtype=jnp.int32)
    cache_allowed = places[None, :] < lengths[:, None]
    fresh = jnp.zeros((row_count, 1), jnp.int32) == 0
    early_one = partial_scores(queries_one, cache_keys, cache_values, cache_allowed)
    early_two = partial_scores(queries_two, cache_keys, cache_values, cache_allowed)
    columns = lax.all_gather(cotangent, "tp", axis=1, tiled=True)
    gradient = lax.psum_scatter(
        lax.dot_general(
            tokens_in, columns, (((0,), (0,)), ((), ())), preferred_element_type=jnp.float32
        ),
        "rep",
        scatter_dimension=0,
        tiled=True,
    ).reshape(master.shape)
    moment_one_new = beta_one * moment_one + (1.0 - beta_one) * gradient
    moment_two_new = beta_two * moment_two + (1.0 - beta_two) * gradient * gradient
    corrected_one = moment_one_new / (1.0 - beta_one**step_count)
    corrected_two = moment_two_new / (1.0 - beta_two**step_count)
    master_new = master - learning_rate * (
        corrected_one / (jnp.sqrt(corrected_two) + epsilon) + weight_decay * master
    )
    weights = master_new[0].astype(jnp.bfloat16)
    shard_rows = lax.all_gather(weights, "rep", axis=0, tiled=True)
    partial_one = jnp.dot(inputs_one, shard_rows, preferred_element_type=jnp.float32)
    partial_two = jnp.dot(inputs_two, shard_rows, preferred_element_type=jnp.float32)
    both_one, both_two = (
        lax.psum_scatter(partial_one, "tp", scatter_dimension=0, tiled=True),
        lax.psum_scatter(partial_two, "tp", scatter_dimension=0, tiled=True),
    )
    key_width = both_one.shape[1] // 2
    keys_one = rotate(both_one[:, :key_width], lengths).astype(jnp.bfloat16)
    values_one = both_one[:, key_width:].astype(jnp.bfloat16)
    keys_two = rotate(both_two[:, :key_width], lengths + 1).astype(jnp.bfloat16)
    values_two = both_two[:, key_width:].astype(jnp.bfloat16)
    late_one = partial_scores(queries_one, keys_one[:, None], values_one[:, None], fresh)
    attended_one = finish(*combine(early_one, late_one))
    fresh_pair = jnp.concatenate([fresh, fresh], axis=1)
    late_two = partial_scores(
        queries_two,
        jnp.stack([keys_one, keys_two], axis=1),
        jnp.stack([values_one, values_two], axis=1),
        fresh_pair,
    )
    attended_two = finish(*combine(early_two, late_two))
    return (
        master_new,
        moment_one_new,
        moment_two_new,
        both_one,
        both_two,
        attended_one,
        attended_two,
    )


def solution(mesh):
    return jax.shard_map(
        functools.partial(shards, mesh.shape["rep"], mesh.shape["tp"]),
        mesh=mesh,
        in_specs=(
            P("rep", "tp"),
            P("rep", "tp"),
            P("tp", "rep", None),
            P("tp", "rep", None),
            P("tp", "rep", None),
            P("rep", "tp"),
            P("rep", "tp"),
            P(("rep", "tp"), None),
            P(("rep", "tp"), None),
            P(("rep", "tp"), None, None),
            P(("rep", "tp"), None, None),
            P(("rep", "tp")),
        ),
        out_specs=(
            P("tp", "rep", None),
            P("tp", "rep", None),
            P("tp", "rep", None),
            P(("rep", "tp"), None),
            P(("rep", "tp"), None),
            P(("rep", "tp"), None),
            P(("rep", "tp"), None),
        ),
        check_vma=False,
    )
```

```python
import functools

import jax
import jax.numpy as jnp
from jax import lax
from jax.experimental import pallas as pl
from jax.experimental.pallas import tpu as pltpu
from jax.sharding import PartitionSpec as P

KVH = 4
QH = 32
HD = 128


learning_rate = 0.001
beta_one = 0.9
beta_two = 0.99
epsilon = 1e-08
weight_decay = 0.1
step_count = 10.0
rope_base = 500000.0


def rotate(vectors, positions):
    row_count = vectors.shape[0]
    half_size = HD // 2
    inverse = rope_base ** (-2.0 * jnp.arange(half_size).astype(jnp.float32) / HD)
    angles = positions.astype(jnp.float32)[:, None, None] * inverse[None, None, :]
    shaped = vectors.reshape(row_count, -1, HD)
    first_half = shaped[..., :half_size]
    second_half = shaped[..., half_size:]
    cosine = jnp.cos(angles)
    sine = jnp.sin(angles)
    turned = jnp.concatenate(
        [first_half * cosine - second_half * sine, second_half * cosine + first_half * sine],
        axis=-1,
    )
    return turned.reshape(row_count, -1)


def partial_scores(queries, all_keys, all_values, allowed):
    row_count = all_keys.shape[0]
    places = all_keys.shape[1]
    group_size = QH // KVH
    shaped_queries = queries.astype(jnp.float32).reshape(row_count, KVH, group_size, HD)
    shaped_keys = all_keys.astype(jnp.float32).reshape(row_count, places, KVH, HD)
    shaped_values = all_values.astype(jnp.float32).reshape(row_count, places, KVH, HD)
    scores = jnp.einsum("rkgd,rpkd->rkgp", shaped_queries, shaped_keys) / HD**0.5
    scores = jnp.where(allowed[:, None, None, :], scores, -1e30)
    highest = jnp.max(scores, axis=-1)
    weights = lax.optimization_barrier(
        jnp.exp(scores - highest[..., None]).astype(jnp.bfloat16)
    ).astype(jnp.float32)
    return (
        highest,
        jnp.sum(weights, axis=-1),
        jnp.einsum("rkgp,rpkd->rkgd", weights, shaped_values),
    )


def finish(highest, denominator, numerator):
    row_count = numerator.shape[0]
    return (numerator / denominator[..., None]).reshape(row_count, -1)


def combine(earlier, later):
    highest = jnp.maximum(earlier[0], later[0])
    scale_early = jnp.exp(earlier[0] - highest)
    scale_late = jnp.exp(later[0] - highest)
    denominator = earlier[1] * scale_early + later[1] * scale_late
    numerator = earlier[2] * scale_early[..., None] + later[2] * scale_late[..., None]
    return (highest, denominator, numerator)


MESH = pl.DeviceIdType.MESH
SUB = 128
CHUNKS = (48, 32, 32, 16)
DIRECT = 2
RING = 4


def arrival_orders(n_tp, sub):
    orders = []
    for t in range(n_tp):
        near = 0 if 2 * t < n_tp else n_tp - 1
        inner = t not in (0, n_tp - 1)
        pieces = []
        for b in range(n_tp):
            away = abs(b - t)
            rank = away
            if inner and away:
                rank = 2 * away + (0 if (b > t) == (near == 0) else 1) - 1
            pieces += [(rank, u, b) for u in range(sub)]
        pieces.sort()
        orders.append([b * sub + u for _, u, b in pieces])
    return orders


def piece_at(orders, t, s):
    found = 0
    for place, order in enumerate(orders):
        for step, piece in enumerate(order):
            if isinstance(s, int):
                if s == step:
                    found = found + jnp.where(t == place, piece, 0)
            else:
                found = found + jnp.where(jnp.logical_and(t == place, s == step), piece, 0)
    return found


def sync_kernel(
    n_rep,
    n_tp,
    sub,
    tok_hbm,
    cot_hbm,
    master_hbm,
    m1_hbm,
    m2_hbm,
    keys_hbm,
    values_hbm,
    in1_hbm,
    in2_hbm,
    q1_hbm,
    q2_hbm,
    lengths_hbm,
    master_out,
    m1_out,
    m2_out,
    p1_out,
    p2_out,
    early_max,
    early_sum,
    early_mix,
    table_ref,
    queries,
    state,
    state_t,
    new_t,
    keys,
    values,
    inputs,
    lengths_ref,
    mask,
    q_ref,
    tok,
    cot_raw,
    cot,
    a_send,
    a_keep,
    a_recv,
    b_send,
    b_recv,
    w_buf,
    w_fine,
    d_send,
    d_recv,
    d_own,
    part,
    part_recv,
    load_sem,
    z_ss,
    z_rs,
    z_fs,
    send_sem,
    d_rs,
    a_rs,
    b_rs,
    w_rs,
    v_rs,
    p_rs,
):
    nc = n_rep // 2
    steps = n_tp * sub
    coarse = steps - 1
    cw = SUB
    chunks = []
    for width in CHUNKS:
        chunks.append(slice(sum(CHUNKS[: len(chunks)]), sum(CHUNKS[: len(chunks)]) + width))
    whole = slice(0, cw)
    final = len(chunks) - 1
    direct = len(chunks) - DIRECT
    shared_cols = slice(0, chunks[direct].start)
    direct_cols = slice(chunks[direct].start, cw)
    summed_cols = slice(0, chunks[final].start)
    r = lax.axis_index("rep")
    t = lax.axis_index("tp")
    k = r // 2
    c = r % 2
    sibling = (2 * k + 1 - c, t)
    own_rows = master_hbm.shape[0]
    att_rows, groups, stacked, _ = q_ref.shape
    orders = arrival_orders(n_tp, sub)
    last = piece_at(orders, t, coarse)
    last_cols = pl.ds(pl.multiple_of(last * cw, cw), cw)

    def chip(j):
        return (k + j) % nc

    def source_chip(j):
        return (k + nc - j) % nc

    def send(source, target, send_sem_ref, recv_sem_ref, device):
        return pltpu.make_async_remote_copy(
            source, target, send_sem_ref, recv_sem_ref, device_id=device, device_id_type=MESH
        )

    load_cot = pltpu.make_async_copy(cot_hbm, cot_raw, load_sem.at[0])
    load_tok = pltpu.make_async_copy(tok_hbm, tok, load_sem.at[1])
    load_lengths = pltpu.make_async_copy(lengths_hbm, lengths_ref, load_sem.at[2])
    load_keys = pltpu.make_async_copy(keys_hbm, keys, load_sem.at[3])
    load_values = pltpu.make_async_copy(values_hbm, values, load_sem.at[4])
    load_queries = [
        pltpu.make_async_copy(source, queries.at[i], load_sem.at[5 + i])
        for i, source in enumerate((q1_hbm, q2_hbm))
    ]
    load_inputs = [
        pltpu.make_async_copy(source, inputs.at[i], load_sem.at[7 + i])
        for i, source in enumerate((in1_hbm, in2_hbm))
    ]
    load_state = [
        pltpu.make_async_copy(source, state.at[i], load_sem.at[9 + i])
        for i, source in enumerate((master_hbm, m1_hbm, m2_hbm))
    ]
    load_cot.start()
    barrier = pltpu.get_barrier_semaphore()
    pl.semaphore_signal(barrier, inc=1, device_id=sibling, device_id_type=MESH)
    for j in range(1, nc):
        pl.semaphore_signal(barrier, inc=1, device_id=(2 * chip(j) + c, t), device_id_type=MESH)

    @pl.when(t < n_tp - 1)
    def _():
        pl.semaphore_signal(barrier, inc=1, device_id=(r, t + 1), device_id_type=MESH)

    @pl.when(t > 0)
    def _():
        pl.semaphore_signal(barrier, inc=1, device_id=(r, t - 1), device_id_type=MESH)

    late_loads = [*load_queries, load_keys, load_values, *load_state, *load_inputs]
    load_cot.wait()
    for load in [load_lengths, *late_loads[:4], load_tok, *late_loads[4:]]:
        load.start()
    cot[t * sub] = cot_raw[:, 0:cw].T
    near = jnp.where(t > 0, 1, 0) + jnp.where(t < n_tp - 1, 1, 0)
    pl.semaphore_wait(barrier, nc + near)

    def neighbour(side):
        return jnp.minimum(t + 1, n_tp - 1) if side == 0 else jnp.maximum(t - 1, 0)

    def z_copy(g, side):
        return send(cot.at[g], cot.at[g], z_ss.at[side], z_rs.at[g], (r, neighbour(side)))

    def z_chunk(g, side, f):
        view = cot.at[g, chunks[f]]
        return send(view, view, z_ss.at[side], z_fs.at[f], (r, neighbour(side)))

    def z_goes(g, side):
        b = g // sub
        if side == 0:
            return jnp.logical_and(b <= t, t < n_tp - 1)
        return jnp.logical_and(b >= t, t > 0)

    def in_chunks(g, side):
        return g == piece_at(orders, neighbour(side), coarse)

    def z_forward(g):
        for side in (0, 1):
            @pl.when(jnp.logical_and(z_goes(g, side), jnp.logical_not(in_chunks(g, side))))
            def _():
                z_copy(g, side).start()

            @pl.when(jnp.logical_and(z_goes(g, side), in_chunks(g, side)))
            def _():
                for f in range(len(chunks)):
                    z_chunk(g, side, f).start()

    def z_forward_chunk(f):
        for side in (0, 1):
            @pl.when(jnp.logical_and(z_goes(last, side), in_chunks(last, side)))
            def _():
                z_chunk(last, side, f).start()

            if f == len(chunks) - 1:
                @pl.when(
                    jnp.logical_and(z_goes(last, side), jnp.logical_not(in_chunks(last, side)))
                )
                def _():
                    z_copy(last, side).start()

    z_forward(t * sub)
    for u in range(1, sub):
        cot[t * sub + u] = cot_raw[:, u * cw : (u + 1) * cw].T
        z_forward(t * sub + u)
    load_lengths.wait()
    row_ids = lax.broadcasted_iota(jnp.int32, (att_rows, HD), 0)
    length = jnp.zeros((att_rows, HD), jnp.int32)
    for row in range(att_rows):
        length = jnp.where(row_ids == row, lengths_ref[row], length)
    table_ref[...] = decode_table(length[:, 0:1])
    mask[...] = table_ref[:, 0:HD]
    for load in load_queries:
        load.wait()
    for i in range(2):
        for h in range(groups):
            for place in range(stacked // 2):
                at = (h * (stacked // 2) + place) * HD
                q_ref[:, h, i * (stacked // 2) + place, :] = queries[i, :, at : at + HD].astype(
                    jnp.float32
                )
    load_tok.wait()
    for load in late_loads[2:]:
        load.wait()

    def ring(slot):
        if isinstance(slot, int) and slot >= coarse:
            return RING + slot - coarse
        return slot % RING

    def kind(slot, sem):
        return send_sem.at[sem + (8 if isinstance(slot, int) and slot >= coarse else 0)]

    def d_copy(at, owner, slot):
        return send(d_send.at[at], d_recv.at[slot], send_sem.at[10], d_rs, (owner, t))

    def a_copy(s, cols, slot):
        return send(
            a_send.at[s, :, cols], a_recv.at[s, :, cols], kind(slot, 0), a_rs.at[ring(slot)], sibling
        )

    def b_copy(s, cols, slot, j):
        return send(
            b_send.at[s, j - 1, cols], b_recv.at[s, j - 1, cols], kind(slot, 1), b_rs.at[ring(slot)],
            (2 * chip(j) + c, t),
        )

    def w_copy(s, j):
        view = w_buf.at[s, r]
        return send(view, view, send_sem.at[2], w_rs.at[ring(s)], (2 * chip(j) + c, t))

    def w_chunk(f, j):
        view = w_fine.at[r, chunks[f]]
        return send(view, view, send_sem.at[3], w_rs.at[ring(coarse + f)], (2 * chip(j) + c, t))

    def v_chunk(f, j):
        view = w_fine.at[2 * source_chip(j) + c, chunks[f]]
        return send(view, view, send_sem.at[6], v_rs.at[coarse], sibling)

    def w_direct(f, j):
        view = w_fine.at[r, chunks[f]]
        return send(view, view, send_sem.at[7], w_rs.at[ring(coarse + f)], ((r + j) % n_rep, t))

    def v_copy(s, j):
        view = w_buf.at[s, 2 * source_chip(j) + c]
        return send(view, view, send_sem.at[4], v_rs.at[s], sibling)

    def wait_recv(ref, sem):
        send(ref, ref, send_sem.at[0], sem, sibling).wait_recv()

    def wait_send(ref, sem):
        send(ref, ref, sem, a_rs.at[0], sibling).wait_send()

    def terms(g, s, cols, slot):
        def term(owner):
            at = pl.multiple_of(owner * own_rows, own_rows)
            return jnp.dot(
                cot[g, cols], tok[:, pl.ds(at, own_rows)], preferred_element_type=jnp.float32
            )

        for q in range(nc):
            a_send[s, q, cols] = term(2 * q + 1 - c)
        a_copy(s, cols, slot).start()
        for q in range(nc):
            a_keep[s, q, cols] = term(2 * q + c)

    def gradient_stage(s):
        g = piece_at(orders, t, s)

        @pl.when(g // sub != t)
        def _():
            z_copy(g, 0).wait_recv()
            z_forward(g)

        terms(g, s, whole, s)

    def gradient_chunk(f):
        z_chunk(last, 0, f).wait_recv()
        z_forward_chunk(f)
        terms(last, coarse, chunks[f], coarse + f)

    def gradient_final():
        z_chunk(last, 0, final).wait_recv()
        z_forward_chunk(final)

        def term(owner):
            at = pl.multiple_of(owner * own_rows, own_rows)
            return jnp.dot(
                cot[last, chunks[final]], tok[:, pl.ds(at, own_rows)],
                preferred_element_type=jnp.float32,
            )

        goals = []
        for i in range(nc - 1):
            away = i + 1
            if nc == 4:
                away = (3 - 2 * (k % 2), 1 + k % 2, 2 + k % 2)[i]
            for parity in range(2):
                goals.append((2 * ((k + away) % nc) + parity, 2 * (away - 1) + c))
        goals.append((2 * k + 1 - c, n_rep - 2))
        group = 8
        for start in range(0, n_rep, group):
            now = range(start, min(start + group, n_rep - 1))
            products = [term(goals[at][0]) for at in now]
            if start + group >= n_rep:
                d_own[...] = term(r)
            for at, product in zip(now, products):
                d_send[at] = product.astype(jnp.bfloat16)
            for at in now:
                d_copy(at, *goals[at]).start()

    def summed_final():
        total = d_own[...]
        wait_recv(d_recv, d_rs)
        for i in range(n_rep - 1):
            total = total + d_recv[i].astype(jnp.float32)
        return total

    def chip_sum_stage(s, cols, slot):
        a_copy(s, cols, slot).wait_recv()
        for j in range(1, nc):
            q = chip(j)
            b_send[s, j - 1, cols] = (a_keep[s, q, cols] + a_recv[s, q, cols]).astype(
                jnp.bfloat16
            )
            b_copy(s, cols, slot, j).start()

    def summed(s, cols, slot):
        total = a_keep[s, k, cols] + a_recv[s, k, cols]
        wait_recv(b_recv.at[s, :, cols], b_rs.at[ring(slot)])
        for j in range(1, nc):
            total = total + b_recv[s, j - 1, cols].astype(jnp.float32)
        return total

    def adam(master, m1, m2, gradient):
        moment_one_new = beta_one * m1 + (1.0 - beta_one) * gradient
        moment_two_new = beta_two * m2 + (1.0 - beta_two) * gradient * gradient
        corrected_one = moment_one_new / (1.0 - beta_one**step_count)
        corrected_two = moment_two_new / (1.0 - beta_two**step_count)
        master_new = master - learning_rate * (
            corrected_one / (jnp.sqrt(corrected_two) + epsilon) + weight_decay * master
        )
        return master_new, moment_one_new, moment_two_new

    outs = (master_out, m1_out, m2_out)

    def update_stage(s):
        cols = pl.ds(pl.multiple_of(piece_at(orders, t, s) * cw, cw), cw)
        updated = adam(*(state[i, :, cols] for i in range(3)), summed(s, whole, s).T)
        w_buf[s, r] = updated[0].astype(jnp.bfloat16)
        for j in range(1, nc):
            w_copy(s, j).start()
        v_copy(s, 0).start()
        for out, value in zip(outs, updated):
            out[:, cols] = value

    def update_chunk(f):
        cols = chunks[f]
        total = summed_final() if f == final else summed(coarse, cols, coarse + f)
        updated = adam(*(state_t[i, cols] for i in range(3)), total)
        w_fine[r, cols] = updated[0].astype(jnp.bfloat16)
        if f >= direct:
            for j in range(1, n_rep):
                w_direct(f, j).start()
        else:
            for j in range(1, nc):
                w_chunk(f, j).start()
            v_chunk(f, 0).start()
        for i, value in enumerate(updated):
            new_t[i, cols] = value

    def share_stage(s):
        wait_recv(w_buf.at[s, 0 : nc - 1], w_rs.at[ring(s)])
        for j in range(1, nc):
            v_copy(s, j).start()

    def share_chunk(f):
        wait_recv(w_fine.at[0 : nc - 1, chunks[f]], w_rs.at[ring(coarse + f)])
        for j in range(1, nc):
            v_chunk(f, j).start()

    at_end = jnp.logical_or(t == 0, t == n_tp - 1)

    def to_end(j):
        to = (t + j) % n_tp
        return jnp.logical_or(to == 0, to == n_tp - 1)

    def p_copy(g, j):
        to = (t + j) % n_tp
        return send(part.at[g, to], part_recv.at[j - 1, g], send_sem.at[5], p_rs, (r, to))

    def decoded(g, product):
        rows = product.shape[0] // 2
        for i in range(2):
            part[g, :, i] = product[i * rows : (i + 1) * rows].reshape(n_tp, rows // n_tp, cw)

    both = inputs.shape[0] * inputs.shape[1]

    def decode_stage(s):
        wait_recv(w_buf.at[s, 0:nc], v_rs.at[s])
        g = piece_at(orders, t, s)
        block = w_buf[s].reshape(n_rep * own_rows, cw)
        decoded(
            g,
            jnp.dot(
                inputs[...].reshape(both, -1), block, preferred_element_type=jnp.float32
            ),
        )
        for j in range(1, n_tp):
            @pl.when(jnp.logical_not(to_end(j)))
            def _():
                p_copy(g, j).start()

    def decode_last():
        for f in range(direct, final + 1):
            wait_recv(w_fine.at[0 : n_rep - 1, chunks[f]], w_rs.at[ring(coarse + f)])
        wait_recv(w_fine.at[0:nc, shared_cols], v_rs.at[coarse])
        product = 0.0
        for owner in range(n_rep):
            rows = inputs[:, :, owner * own_rows : (owner + 1) * own_rows]
            product = product + lax.dot_general(
                rows.reshape(both, own_rows),
                w_fine[owner],
                (((1,), (1,)), ((), ())),
                preferred_element_type=jnp.float32,
            )
        decoded(last, product)

        @pl.when(at_end)
        def _():
            for far in (True, False):
                for j in range(1, n_tp):
                    @pl.when(to_end(j) == far)
                    def _():
                        p_copy(last, j).start()

        @pl.when(jnp.logical_not(at_end))
        def _():
            for j in range(1, n_tp):
                @pl.when(jnp.logical_not(to_end(j)))
                def _():
                    p_copy(last, j).start()

    def late_stage(s):
        g = piece_at(orders, t, s)
        for j in range(1, n_tp):
            @pl.when(to_end(j))
            def _():
                p_copy(g, j).start()

    cache_steps = min(4, coarse)

    def cache_stage(s):
        per_step = att_rows // cache_steps

        @pl.loop(0, per_step)
        def _(i):
            row = s * per_step + i
            allowed = mask[pl.ds(row, 1), :] > 0.0
            for h in range(groups):
                head = slice(h * HD, (h + 1) * HD)
                scores = lax.dot_general(
                    q_ref[row, h].astype(jnp.bfloat16),
                    keys[row, :, head],
                    (((1,), (1,)), ((), ())),
                    preferred_element_type=jnp.float32,
                )
                scores = jnp.where(allowed, scores / HD**0.5, -1e30)
                highest = jnp.max(scores, axis=-1, keepdims=True)
                weights = jnp.exp(scores - highest).astype(jnp.bfloat16)
                total = jnp.sum(weights.astype(jnp.float32), axis=-1, keepdims=True)
                mix = jnp.dot(weights, values[row, :, head], preferred_element_type=jnp.float32)
                for ref, value in ((early_max, highest), (early_sum, total), (early_mix, mix)):
                    value = jnp.broadcast_to(value, (stacked, HD))
                    ref[h, :, pl.ds(row, 1), :] = value.reshape(stacked, 1, HD)

    def turn_state():
        for i in range(3):
            state_t[i] = state[i, :, last_cols].T

    def sum_stage(s):
        chip_sum_stage(s, whole, s)

    def ahead(s):
        return jnp.logical_and(at_end, s >= cache_steps)

    def never(s):
        return False

    stages = (
        (sum_stage, 1, ahead),
        (update_stage, 2, lambda s: jnp.logical_and(at_end, s >= cache_steps - 1)),
        (share_stage, 3, never),
        (decode_stage, 4, never),
    )
    cache_now = jnp.where(at_end, cache_steps, 1)

    @pl.loop(0, coarse)
    def _(it):
        for stage, lag, skip in stages:
            @pl.when(jnp.logical_and(it >= lag, jnp.logical_not(skip(it - lag))))
            def _():
                stage(it - lag)

        @pl.when(it < cache_now)
        def _():
            cache_stage(it)

        gradient_stage(it)

        @pl.when(jnp.logical_and(ahead(it), it < coarse - 1))
        def _():
            sum_stage(it)

            @pl.when(it == cache_steps)
            def _():
                update_stage(it - 1)

            update_stage(it)

        @pl.when(it == cache_steps)
        def _():
            turn_state()

    sum_stage(coarse - 1)

    @pl.when(jnp.logical_not(at_end))
    def _():
        update_stage(coarse - 2)

    share_stage(coarse - 3)
    decode_stage(coarse - 4)

    @pl.when(jnp.logical_not(at_end))
    def _():
        cache_stage(1)

    for f, cols in enumerate(chunks[:-1]):
        gradient_chunk(f)
        chip_sum_stage(coarse, cols, coarse + f)
        if f == 0:
            share_stage(coarse - 2)
            update_stage(coarse - 1)
        if f > 1:
            update_chunk(f - 2)
    gradient_final()
    if final > 1:
        update_chunk(final - 2)
    for s in range(coarse - 3, coarse - 1):
        decode_stage(s)
    share_stage(coarse - 1)

    @pl.when(at_end)
    def _():
        @pl.loop(0, coarse - 1)
        def _(s):
            late_stage(s)

    update_chunk(final - 1)
    update_chunk(final)
    if direct > 0:
        share_chunk(0)
    decode_stage(coarse - 1)

    @pl.when(at_end)
    def _():
        late_stage(coarse - 1)

    for f in range(1, direct):
        share_chunk(f)
    for i, out in enumerate(outs):
        out[:, last_cols] = new_t[i].T
    decode_last()

    for place in range(n_tp):
        @pl.when(t == place)
        def _():
            if place < n_tp - 1:
                wait_send(cot.at[0 : (place + 1) * sub], z_ss.at[0])
            if place > 0:
                wait_send(cot.at[0 : (n_tp - place) * sub], z_ss.at[1])

    @pl.when(jnp.logical_not(at_end))
    def _():
        cache_stage(2)

        @pl.loop(0, steps)
        def _(s):
            late_stage(s)

        @pl.loop(3, cache_steps)
        def _(s):
            cache_stage(s)

    wait_send(a_send.at[0:coarse], send_sem.at[0])
    wait_send(b_send.at[0:coarse], send_sem.at[1])
    wait_send(a_send.at[coarse, :, summed_cols], send_sem.at[8])
    wait_send(b_send.at[coarse, :, summed_cols], send_sem.at[9])
    wait_send(d_send, send_sem.at[10])
    wait_send(w_buf.at[:, 0 : nc - 1], send_sem.at[2])
    wait_send(w_fine.at[0 : nc - 1, shared_cols], send_sem.at[3])
    wait_send(w_fine.at[0:nc, shared_cols], send_sem.at[6])
    wait_send(w_fine.at[0 : n_rep - 1, direct_cols], send_sem.at[7])
    wait_send(w_buf.at[:, 0:nc], send_sem.at[4])
    wait_recv(part_recv, p_rs)
    for g in range(steps):
        for i, out in enumerate((p1_out, p2_out)):
            total = part[g, t, i]
            for j in range(1, n_tp):
                total = total + part_recv[j - 1, g, i]
            out[:, g * cw : (g + 1) * cw] = total
    wait_send(part.at[:, 0 : n_tp - 1], send_sem.at[5])


def finish_kernel(
    master,
    m1,
    m2,
    p1,
    p2,
    early_max,
    early_sum,
    early_mix,
    table,
    queries,
    master_out,
    m1_out,
    m2_out,
    p1_out,
    p2_out,
    att1_out,
    att2_out,
    att,
    sems,
    att_sems,
):
    stores = [
        pltpu.make_async_copy(source, target, sems.at[i])
        for i, (source, target) in enumerate(
            ((master, master_out), (m1, m1_out), (m2, m2_out), (p1, p1_out), (p2, p2_out))
        )
    ]
    for store in stores:
        store.start()
    groups, stacked = early_max.shape[:2]
    half = stacked // 2
    keys, values = [], []
    for i, ref in enumerate((p1, p2)):
        total = ref[...]
        cosine = table[:, (1 + 2 * i) * HD : (2 + 2 * i) * HD]
        sine = table[:, (2 + 2 * i) * HD : (3 + 2 * i) * HD]
        for h in range(groups):
            head = total[:, h * HD : (h + 1) * HD]
            turned = head * cosine + pltpu.roll(head, HD // 2, 1) * sine
            value = total[:, (groups + h) * HD : (groups + h + 1) * HD]
            keys.append(turned.astype(jnp.bfloat16).astype(jnp.float32))
            values.append(value.astype(jnp.bfloat16).astype(jnp.float32))
    for i, out in enumerate((att1_out, att2_out)):
        for h in range(groups):
            for place in range(half):
                at = slice((h * half + place) * HD, (h * half + place + 1) * HD)
                query = queries[i, :, at].astype(jnp.float32)
                scores = [
                    jnp.sum(query * keys[n * groups + h], axis=-1, keepdims=True) / HD**0.5
                    for n in range(i + 1)
                ]
                before = early_max[h, i * half + place]
                highest = before
                for score in scores:
                    highest = jnp.maximum(highest, score)
                scale = jnp.exp(before - highest)
                below = early_sum[h, i * half + place] * scale
                above = early_mix[h, i * half + place] * scale
                for n, score in enumerate(scores):
                    weight = jnp.exp(score - highest).astype(jnp.bfloat16).astype(jnp.float32)
                    below = below + weight
                    above = above + weight * values[n * groups + h]
                att[i, :, at] = above / below
        store = pltpu.make_async_copy(att.at[i], out, att_sems.at[i])
        store.start()
        stores.append(store)
    for store in stores:
        store.wait()


def synchronise(
    n_rep,
    n_tp,
    tokens_in,
    cotangent,
    master,
    m1,
    m2,
    cache_keys,
    cache_values,
    inputs_one,
    inputs_two,
    queries_one,
    queries_two,
    lengths,
):
    tokens, width = tokens_in.shape
    sub = cotangent.shape[1] // SUB
    steps = n_tp * sub
    units = steps - 1 + len(CHUNKS)
    nc = n_rep // 2
    rows, cols = master.shape
    decode = inputs_one.shape[0]
    share = decode // n_tp
    f32, bf16 = jnp.float32, jnp.bfloat16
    count = queries_one.shape[0]
    stacked = (count, KVH, 2 * QH // KVH, HD)
    early = (KVH, 2 * QH // KVH, count, HD)
    vmem = pl.BlockSpec(memory_space=pltpu.VMEM)
    hbm = pl.BlockSpec(memory_space=pl.ANY)
    dma = pltpu.SemaphoreType.DMA
    held = pl.pallas_call(
        functools.partial(sync_kernel, n_rep, n_tp, sub),
        out_shape=[pltpu.VMEM((rows, cols), f32)] * 3
        + [pltpu.VMEM((share, cols), f32)] * 2
        + [pltpu.VMEM(early, f32)] * 3
        + [pltpu.VMEM((count, 5 * HD), f32), pltpu.VMEM((2, *queries_one.shape), bf16)],
        in_specs=[hbm] * 12,
        out_specs=[vmem] * 10,
        scratch_shapes=[
            pltpu.VMEM((3, rows, cols), f32),
            pltpu.VMEM((3, SUB, rows), f32),
            pltpu.VMEM((3, SUB, rows), f32),
            pltpu.VMEM(cache_keys.shape, bf16),
            pltpu.VMEM(cache_values.shape, bf16),
            pltpu.VMEM((2, *inputs_one.shape), bf16),
            pltpu.SMEM(lengths.shape, jnp.int32),
            pltpu.VMEM((count, HD), f32),
            pltpu.VMEM(stacked, f32),
            pltpu.VMEM((tokens, width), bf16),
            pltpu.VMEM((tokens, sub * SUB), bf16),
            pltpu.VMEM((steps, SUB, tokens), bf16),
            pltpu.VMEM((steps, nc, SUB, rows), f32),
            pltpu.VMEM((steps, nc, SUB, rows), f32),
            pltpu.VMEM((steps, nc, SUB, rows), f32),
            pltpu.VMEM((steps, nc - 1, SUB, rows), bf16),
            pltpu.VMEM((steps, nc - 1, SUB, rows), bf16),
            pltpu.VMEM((steps - 1, n_rep, rows, SUB), bf16),
            pltpu.VMEM((n_rep, SUB, rows), bf16),
            pltpu.VMEM((n_rep - 1, CHUNKS[-1], rows), bf16),
            pltpu.VMEM((n_rep - 1, CHUNKS[-1], rows), bf16),
            pltpu.VMEM((CHUNKS[-1], rows), f32),
            pltpu.VMEM((steps, n_tp, 2, share, SUB), f32),
            pltpu.VMEM((n_tp - 1, steps, 2, share, SUB), f32),
            dma((12,)),
            dma((2,)),
            dma((steps,)),
            dma((len(CHUNKS),)),
            dma((11,)),
            dma(()),
            dma((RING + len(CHUNKS),)),
            dma((RING + len(CHUNKS),)),
            dma((RING + len(CHUNKS),)),
            dma((steps,)),
            dma(()),
        ],
        compiler_params=pltpu.CompilerParams(
            collective_id=0, has_side_effects=True, vmem_limit_bytes=52 * 2**20
        ),
        name="synchronise",
    )(
        tokens_in,
        cotangent,
        master,
        m1,
        m2,
        cache_keys,
        cache_values,
        inputs_one,
        inputs_two,
        queries_one,
        queries_two,
        lengths,
    )
    wide = queries_one.shape
    return pl.pallas_call(
        finish_kernel,
        out_shape=[jax.ShapeDtypeStruct((rows, cols), f32)] * 3
        + [jax.ShapeDtypeStruct((share, cols), f32)] * 2
        + [jax.ShapeDtypeStruct(wide, f32)] * 2,
        in_specs=[vmem] * 10,
        out_specs=[hbm] * 7,
        scratch_shapes=[pltpu.VMEM((2, *wide), f32), dma((5,)), dma((2,))],
        compiler_params=pltpu.CompilerParams(vmem_limit_bytes=4 * 2**20),
        name="finish",
    )(*held)


def decode_table(lengths):
    shape = (lengths.shape[0], 5 * HD)
    column = lax.broadcasted_iota(jnp.int32, shape, 1)
    kind = column // HD
    lane = column % HD
    half_size = HD // 2
    inverse = rope_base ** (-2.0 * (lane % half_size).astype(jnp.float32) / HD)
    position = lengths + jnp.where(kind >= 3, 1, 0)
    angles = position.astype(jnp.float32) * inverse
    sine = jnp.where(lane < half_size, -jnp.sin(angles), jnp.sin(angles))
    allowed = jnp.where(lane < lengths, 1.0, 0.0)
    return jnp.where(kind == 0, allowed, jnp.where(kind % 2 == 1, jnp.cos(angles), sine))


def fits_kernel(n_rep, n_tp, cotangent, master, inputs_one, cache_keys):
    steps = n_tp * (cotangent.shape[1] // SUB)
    return (
        cache_keys.shape[1] == HD
        and steps > 6
        and len(CHUNKS) > 2
        and cache_keys.shape[0] % 4 == 0
        and n_rep % 2 == 0
        and n_rep >= 4
        and n_tp >= 2
        and cotangent.shape[1] % SUB == 0
        and cotangent.shape[0] % 256 == 0
        and master.shape[1] % 128 == 0
        and inputs_one.shape[0] % (8 * n_tp) == 0
    )


def shards(
    n_rep,
    n_tp,
    tokens_in,
    cotangent,
    master,
    moment_one,
    moment_two,
    inputs_one,
    inputs_two,
    queries_one,
    queries_two,
    cache_keys,
    cache_values,
    lengths,
):
    row_count = cache_keys.shape[0]
    if fits_kernel(n_rep, n_tp, cotangent, master[0], inputs_one, cache_keys):
        *updated, both_one, both_two, attended_one, attended_two = synchronise(
            n_rep,
            n_tp,
            tokens_in,
            cotangent,
            master[0],
            moment_one[0],
            moment_two[0],
            cache_keys,
            cache_values,
            inputs_one,
            inputs_two,
            queries_one,
            queries_two,
            lengths,
        )
        return (
            *(array[None] for array in updated),
            both_one,
            both_two,
            attended_one,
            attended_two,
        )
    places = jnp.arange(cache_keys.shape[1], dtype=jnp.int32)
    cache_allowed = places[None, :] < lengths[:, None]
    fresh = jnp.zeros((row_count, 1), jnp.int32) == 0
    early_one = partial_scores(queries_one, cache_keys, cache_values, cache_allowed)
    early_two = partial_scores(queries_two, cache_keys, cache_values, cache_allowed)
    columns = lax.all_gather(cotangent, "tp", axis=1, tiled=True)
    gradient = lax.psum_scatter(
        lax.dot_general(
            tokens_in, columns, (((0,), (0,)), ((), ())), preferred_element_type=jnp.float32
        ),
        "rep",
        scatter_dimension=0,
        tiled=True,
    ).reshape(master.shape)
    moment_one_new = beta_one * moment_one + (1.0 - beta_one) * gradient
    moment_two_new = beta_two * moment_two + (1.0 - beta_two) * gradient * gradient
    corrected_one = moment_one_new / (1.0 - beta_one**step_count)
    corrected_two = moment_two_new / (1.0 - beta_two**step_count)
    master_new = master - learning_rate * (
        corrected_one / (jnp.sqrt(corrected_two) + epsilon) + weight_decay * master
    )
    weights = master_new[0].astype(jnp.bfloat16)
    shard_rows = lax.all_gather(weights, "rep", axis=0, tiled=True)
    partial_one = jnp.dot(inputs_one, shard_rows, preferred_element_type=jnp.float32)
    partial_two = jnp.dot(inputs_two, shard_rows, preferred_element_type=jnp.float32)
    both_one, both_two = (
        lax.psum_scatter(partial_one, "tp", scatter_dimension=0, tiled=True),
        lax.psum_scatter(partial_two, "tp", scatter_dimension=0, tiled=True),
    )
    key_width = both_one.shape[1] // 2
    keys_one = rotate(both_one[:, :key_width], lengths).astype(jnp.bfloat16)
    values_one = both_one[:, key_width:].astype(jnp.bfloat16)
    keys_two = rotate(both_two[:, :key_width], lengths + 1).astype(jnp.bfloat16)
    values_two = both_two[:, key_width:].astype(jnp.bfloat16)
    late_one = partial_scores(queries_one, keys_one[:, None], values_one[:, None], fresh)
    attended_one = finish(*combine(early_one, late_one))
    fresh_pair = jnp.concatenate([fresh, fresh], axis=1)
    late_two = partial_scores(
        queries_two,
        jnp.stack([keys_one, keys_two], axis=1),
        jnp.stack([values_one, values_two], axis=1),
        fresh_pair,
    )
    attended_two = finish(*combine(early_two, late_two))
    return (
        master_new,
        moment_one_new,
        moment_two_new,
        both_one,
        both_two,
        attended_one,
        attended_two,
    )


def solution(mesh):
    return jax.shard_map(
        functools.partial(shards, mesh.shape["rep"], mesh.shape["tp"]),
        mesh=mesh,
        in_specs=(
            P("rep", "tp"),
            P("rep", "tp"),
            P("tp", "rep", None),
            P("tp", "rep", None),
            P("tp", "rep", None),
            P("rep", "tp"),
            P("rep", "tp"),
            P(("rep", "tp"), None),
            P(("rep", "tp"), None),
            P(("rep", "tp"), None, None),
            P(("rep", "tp"), None, None),
            P(("rep", "tp")),
        ),
        out_specs=(
            P("tp", "rep", None),
            P("tp", "rep", None),
            P("tp", "rep", None),
            P(("rep", "tp"), None),
            P(("rep", "tp"), None),
            P(("rep", "tp"), None),
            P(("rep", "tp"), None),
        ),
        check_vma=False,
    )
```
